256 devices in a mesh: row: 16 (over x_hi, y, core), col: 16 (over x_lo, z).
Axes of the slice: x: 4 (x_hi: 2, x_lo: 2; x = x_hi * 2 + x_lo), y: 4, z: 8, core: 2. Of those that a mesh axis runs over, the one named last changes fastest.
Arguments:
- left_factors: float32 [128, 512, 32], P(None, ('row', 'col')), may hold values from -12 to 12
- right_factors: float32 [128, 512, 32], P(None, ('col', 'row')), may hold values from -12 to 12
- weight: float32 [1024, 128], replicated, may hold values from -0.1875 to 0.1875
- bias: float32 [128], replicated, may hold values from -2 to 2
- cotangent: float32 [512, 512, 128], P('row', 'col'), may hold values from -6 to 6
Outputs:
- pair_out: float32 [512, 512, 128], P('row', 'col')
- left_grad: float32 [128, 512, 32], P(None, ('row', 'col'))
- right_grad: float32 [128, 512, 32], P(None, ('col', 'row'))
- weight_grad: float32 [1024, 128], replicated
- bias_grad: float32 [128], replicated
The draws below stay inside these ranges and needn't reach their ends.
All inputs are finite; a program needn't handle non-finite values.
Results may differ from the reference program's by a relative error of at most 0.0001.
Values sent between devices are 32-bit elements; how exact they have to be, the bound alone decides.
No kernel may reach another device: no remote copies, remote signals or barrier semaphores. Data moves between devices by JAX's collectives and lax.ppermute only.
A program may use at most 64 MiB of HBM per device.

```python
import jax
import jax.numpy as jnp
from jax import lax

S = 128
C = 32
CZ = 128
NI = 512
NJ = 512


def block_scale(rng, extent, cuts, low, high):
    def one(dim, blocks):
        steps = jax.random.uniform(jax.random.fold_in(jax.random.fold_in(rng, 6), dim), (blocks,), jnp.float32, low / len(cuts), high / len(cuts))
        return jnp.repeat(jnp.exp(steps), extent[dim] // blocks).reshape((-1,) + (1,) * (len(extent) - dim - 1))

    level = one(*cuts[0])
    for cut in cuts[1:]:
        level = level * one(*cut)
    return level


def noise(rng, shape, deviation, limit, shards=(), dtype=jnp.bfloat16):
    loudness = block_scale(rng, shape, shards, -0.22, 0.18) if shards else 1.0
    drawn = jax.random.normal(rng, shape, jnp.float32) * deviation * loudness
    return jnp.minimum(jnp.maximum(drawn, -limit), limit).astype(dtype)


def setup_inputs(seed: int = 0) -> dict:
    arg_keys = jax.random.split(jax.random.key(seed), 6)
    return {
        "left_factors": noise(arg_keys[0], (S, NI, C), 2.0, 12.0, ((1, 256),), jnp.float32),
        "right_factors": noise(arg_keys[1], (S, NJ, C), 2.0, 12.0, ((1, 256),), jnp.float32),
        "weight": noise(arg_keys[2], (C * C, CZ), (C * C) ** -0.5, 0.1875, (), jnp.float32),
        "bias": noise(arg_keys[3], (CZ,), 0.3, 2.0, (), jnp.float32),
        "cotangent": noise(arg_keys[4], (NI, NJ, CZ), 1.0, 6.0, ((0, 16), (1, 16)), jnp.float32),
    }


def reference(left_factors, right_factors, weight, bias, cotangent):
    high = lax.Precision.HIGHEST
    step_rows = 16
    blocks = NI // step_rows
    left_blocks = left_factors.reshape(S, blocks, step_rows, C).transpose(1, 0, 2, 3)
    cot_blocks = cotangent.reshape(blocks, step_rows, NJ, CZ)

    def visit(carry, item):
        weight_sum, right_sum = carry
        left_block, cot_block = item
        outer = jnp.einsum("sic,sjd->ijcd", left_block, right_factors, precision=high) / S
        flat = outer.reshape(step_rows, NJ, C * C)
        pair_block = jnp.einsum("ijk,ke->ije", flat, weight, precision=high) + bias
        grad_flat = jnp.einsum("ije,ke->ijk", cot_block, weight, precision=high)
        weight_sum = weight_sum + jnp.einsum("ijk,ije->ke", flat, cot_block, precision=high)
        grad_outer = grad_flat.reshape(step_rows, NJ, C, C)
        left_block_grad = jnp.einsum("ijcd,sjd->sic", grad_outer, right_factors, precision=high) / S
        right_sum = right_sum + jnp.einsum("ijcd,sic->sjd", grad_outer, left_block, precision=high) / S
        return (weight_sum, right_sum), (pair_block, left_block_grad)

    start = (jnp.zeros((C * C, CZ), jnp.float32), jnp.zeros((S, NJ, C), jnp.float32))
    (weight_sum, right_grad), (pair_blocks, left_parts) = lax.scan(visit, start, (left_blocks, cot_blocks))
    pair_out = pair_blocks.reshape(NI, NJ, CZ)
    left_grad = left_parts.transpose(1, 0, 2, 3).reshape(S, NI, C)
    weight_grad = weight_sum / NI
    bias_grad = jnp.sum(cotangent, axis=(0, 1)) / NI
    return pair_out, left_grad, right_grad, weight_grad, bias_grad
```

```python
import jax
import jax.numpy as jnp
from jax import lax
from jax.experimental import pallas as pl
from jax.experimental.pallas import tpu as pltpu
from jax.sharding import Mesh
from jax.sharding import PartitionSpec as P

S = 128
C = 32
CZ = 128
T = 32
PEERS = 16
F32 = jnp.float32
BF16 = jnp.bfloat16
ROW = ("xh", "y", "core")
COL = ("xl", "z")
PLANE = ("xh", "y", "xl")


def params(mib):
    return pltpu.CompilerParams(vmem_limit_bytes=mib << 20)


def split(x):
    hi = x.astype(BF16)
    return hi, (x - hi.astype(F32)).astype(BF16)


def mm(a, b):
    return lax.dot_general(a, b, (((1,), (0,)), ((), ())), preferred_element_type=F32)


def mm_t(a, b):
    return lax.dot_general(a, b, (((1,), (1,)), ((), ())), preferred_element_type=F32)


def lanes(shape):
    return lax.broadcasted_iota(jnp.int32, shape, 1)


def swap_groups(a):
    lane = lanes(a[0].shape)
    low = lane < 64
    even = (lane & 32) == 0
    b = [None] * 4
    for g in (0, 1):
        b[g] = jnp.where(low, a[g], pltpu.roll(a[g + 2], 64, 1))
        b[g + 2] = jnp.where(low, pltpu.roll(a[g], 64, 1), a[g + 2])
    out = [None] * 4
    for g in (0, 2):
        out[g] = jnp.where(even, b[g], pltpu.roll(b[g + 1], 32, 1))
        out[g + 1] = jnp.where(even, pltpu.roll(b[g], 96, 1), b[g + 1])
    return out


def relayout(x, hi_ref, lo_ref, outer):
    for q in range(8):
        pieces = [x[32 * g : 32 * g + 32, 128 * q : 128 * q + 128] for g in range(4)]
        for r, piece in enumerate(swap_groups(pieces)):
            hi, lo = split(piece)
            rows = pl.ds((4 * q + r) * 32, 32)
            hi_ref[rows, pl.ds(outer, 128)] = hi
            lo_ref[rows, pl.ds(outer, 128)] = lo


def by_second(w_ref, hi_ref, lo_ref):
    for d in range(C):
        hi, lo = split(w_ref[pl.ds(d, C, stride=C), :])
        hi_ref[32 * d : 32 * d + 32, :] = hi
        lo_ref[32 * d : 32 * d + 32, :] = lo


def grad_kernel(cot_ref, w_ref, ghi_ref, glo_ref, bias_ref, whi, wlo):
    by_second(w_ref, whi, wlo)
    bias_ref[...] = jnp.zeros_like(bias_ref)

    def step(q, carry):
        at = pl.multiple_of(q * 128, 128)
        cot = cot_ref[pl.ds(at, 128), :]
        bias_ref[...] += cot.reshape(16, 8, CZ).sum(axis=0)
        hi, lo = split(cot)
        g = mm_t(hi, whi[...]) + mm_t(hi, wlo[...]) + mm_t(lo, whi[...])
        relayout(g, ghi_ref, glo_ref, at)
        return carry

    lax.fori_loop(0, 8, step, 0)


def read_left(gl_ref, m):
    a, b = gl_ref[2 * m], gl_ref[2 * m + 1]
    low = lanes(a.shape) < 64
    top = jnp.where(low, a, pltpu.roll(b, 64, 1))
    bottom = jnp.where(low, pltpu.roll(a, 64, 1), b)
    return jnp.concatenate([top, bottom], axis=0) * (1.0 / S)


def outer_kernel(gl_ref, gr_ref, cot_ref, fhi_ref, flo_ref, wg_ref, lhi_ref, llo_ref, rt_ref, ct):
    for m in range(8):
        hi, lo = split(read_left(gl_ref, m))
        lhi_ref[:, 128 * m : 128 * m + 128] = hi
        llo_ref[:, 128 * m : 128 * m + 128] = lo
    for p in range(PEERS):
        for t in range(2):
            rt_ref[pl.ds(2 * p + t, 32, stride=32), :] = gr_ref[p, 32 * t : 32 * t + 32, :]

    def step(q, carry):
        at = pl.multiple_of(q * 128, 128)
        hi, lo = split(rt_ref[pl.ds(at, 128), :])
        x = mm(hi, lhi_ref[...]) + mm(hi, llo_ref[...]) + mm(lo, lhi_ref[...])
        relayout(x, fhi_ref, flo_ref, at)
        chi, clo = split(cot_ref[pl.ds(at, 128), :].T)
        ct[0:128, pl.ds(at, 128)] = chi
        ct[128:256, pl.ds(at, 128)] = clo
        return carry

    lax.fori_loop(0, 8, step, 0)

    def wgrad(n, carry):
        at = pl.multiple_of(n * 256, 256)
        both = mm(ct[...], fhi_ref[:, pl.ds(at, 256)])
        out = both[:CZ] + both[CZ:] + mm(ct[0:128, :], flo_ref[:, pl.ds(at, 256)])
        out = out.T
        for k in range(8):
            wg_ref[pl.ds(n * 8 + k, C, stride=C), :] = out[32 * k : 32 * k + 32]
        return carry

    lax.fori_loop(0, 4, wgrad, 0)


def pair_kernel(fhi_ref, flo_ref, w_ref, bias_ref, out_ref, w2):
    for d in range(C):
        hi, lo = split(w_ref[pl.ds(d, C, stride=C), :])
        w2[32 * d : 32 * d + 32, 0:128] = hi
        w2[32 * d : 32 * d + 32, 128:256] = lo

    def step(n, carry):
        rows = pl.ds(pl.multiple_of(n * 256, 256), 256)
        both = mm(fhi_ref[rows, :], w2[...])
        out = both[:, :CZ] + both[:, CZ:] + mm(flo_ref[rows, :], w2[:, 0:128])
        out_ref[rows, :] = out + bias_ref[...]
        return carry

    lax.fori_loop(0, 4, step, 0)


def factor_kernel(ghi_ref, glo_ref, lhi_ref, llo_ref, rt_ref, lp_ref, rp_ref, r2, l2, rp):
    l2[0:128, :] = lhi_ref[...]
    l2[128:256, :] = llo_ref[...]
    for q in range(8):
        hi, lo = split(rt_ref[128 * q : 128 * q + 128, :].T)
        r2[0:128, 128 * q : 128 * q + 128] = hi
        r2[128:256, 128 * q : 128 * q + 128] = lo

    def left(n, carry):
        at = pl.multiple_of(n * 256, 256)
        both = mm(r2[...], ghi_ref[:, pl.ds(at, 256)])
        out = both[:S] + both[S:] + mm(r2[0:128, :], glo_ref[:, pl.ds(at, 256)])
        out = out * (1.0 / S)
        low = lanes((64, 128)) < 64
        for k in range(2):
            top = out[0:64, 128 * k : 128 * k + 128]
            bottom = out[64:128, 128 * k : 128 * k + 128]
            lp_ref[4 * n + 2 * k] = jnp.where(low, top, pltpu.roll(bottom, 64, 1))
            lp_ref[4 * n + 2 * k + 1] = jnp.where(low, pltpu.roll(top, 64, 1), bottom)
        return carry

    lax.fori_loop(0, 4, left, 0)

    def right(n, carry):
        rows = pl.ds(pl.multiple_of(n * 256, 256), 256)
        both = mm_t(ghi_ref[rows, :], l2[...])
        rp[rows, :] = both[:, :S] + both[:, S:] + mm_t(glo_ref[rows, :], l2[0:128, :])
        return carry

    lax.fori_loop(0, 4, right, 0)
    for p in range(PEERS):
        for t in range(2):
            rp_ref[p, 32 * t : 32 * t + 32, :] = rp[pl.ds(2 * p + t, 32, stride=32), :]


def shapes(*entries):
    return [jax.ShapeDtypeStruct(s, t) for s, t in entries]


def cost(flops, moved):
    return pl.CostEstimate(flops=flops, bytes_accessed=moved, transcendentals=0)


BIG = 2 * 1024 * 1024 * 128


def exchange(x, axes):
    return lax.all_to_all(x, axes, split_axis=0, concat_axis=0, tiled=True)


def gather(x, axes, n):
    return exchange(jnp.broadcast_to(x, (n, *x.shape)), axes)


def other_core(x):
    return lax.ppermute(x, "core", [(0, 1), (1, 0)])


def per_device(left, right, weight, bias, cotangent):
    cot = cotangent.reshape(T * T, CZ)
    left = left.reshape(S, 64)
    left_own = jnp.concatenate([left[:64], left[64:]], axis=1)
    right_own = right.reshape(S, 64).T
    left_all = gather(left_own, COL, PEERS)
    right_all = gather(right_own, ROW, PEERS)

    ghi, glo, bias_part = pl.pallas_call(
        grad_kernel,
        out_shape=shapes(((1024, 1024), BF16), ((1024, 1024), BF16), ((8, CZ), F32)),
        scratch_shapes=[pltpu.VMEM((1024, CZ), BF16)] * 2,
        compiler_params=params(40),
        cost_estimate=cost(3 * BIG, 6 << 20),
        name="grad_outer",
    )(cot, weight)

    fhi, flo, wg, lhi, llo, rt = pl.pallas_call(
        outer_kernel,
        out_shape=shapes(
            ((1024, 1024), BF16),
            ((1024, 1024), BF16),
            ((1024, CZ), F32),
            ((S, 1024), BF16),
            ((S, 1024), BF16),
            ((1024, S), F32),
        ),
        scratch_shapes=[pltpu.VMEM((256, 1024), BF16)],
        compiler_params=params(40),
        cost_estimate=cost(6 * BIG, 8 << 20),
        name="outer_and_weight_grad",
    )(left_all, right_all, cot)

    core = lax.axis_index("core")
    bias_row = jnp.concatenate([bias_part.sum(axis=0, keepdims=True), jnp.zeros((7, CZ), F32)])
    halves = wg.reshape(2, 512, CZ)
    kept = lax.dynamic_index_in_dim(halves, core, 0, keepdims=False)
    sent = lax.dynamic_index_in_dim(halves, 1 - core, 0, keepdims=False)
    chip = jnp.concatenate([kept, bias_row]) + other_core(jnp.concatenate([sent, bias_row]))
    chunks = jnp.concatenate(
        [chip[:512].reshape(16, 32, CZ), jnp.broadcast_to(chip[512:], (16, 8, CZ))], axis=1
    )
    plane_sum = exchange(chunks, PLANE).sum(axis=0)
    total = gather(plane_sum, ("z",), 8).sum(axis=0) * (1.0 / 512)
    half = gather(total[:32], PLANE, 16).reshape(512, CZ)
    half_other = other_core(half)
    first = jnp.where(core == 0, half, half_other)
    second = jnp.where(core == 0, half_other, half)
    weight_grad = jnp.concatenate([first, second])
    bias_grad = total[32]

    pair = pl.pallas_call(
        pair_kernel,
        out_shape=jax.ShapeDtypeStruct((1024, CZ), F32),
        scratch_shapes=[pltpu.VMEM((1024, 256), BF16)],
        compiler_params=params(40),
        cost_estimate=cost(3 * BIG, 6 << 20),
        name="pair_out",
    )(fhi, flo, weight, bias.reshape(1, CZ))

    lp, rp = pl.pallas_call(
        factor_kernel,
        out_shape=shapes(((PEERS, 64, 128), F32), ((PEERS, 64, 128), F32)),
        scratch_shapes=[
            pltpu.VMEM((256, 1024), BF16),
            pltpu.VMEM((256, 1024), BF16),
            pltpu.VMEM((1024, S), F32),
        ],
        compiler_params=params(40),
        cost_estimate=cost(6 * BIG, 8 << 20),
        name="factor_grads",
    )(ghi, glo, lhi, llo, rt)

    left_sum = exchange(lp, COL).sum(axis=0)
    right_sum = exchange(rp, ROW).sum(axis=0)
    left_grad = jnp.concatenate([left_sum[:, :64], left_sum[:, 64:]]).reshape(S, 2, C)
    right_grad = right_sum.T.reshape(S, 2, C)
    return pair.reshape(T, T, CZ), left_grad, right_grad, weight_grad, bias_grad


def solution(mesh):
    fine = Mesh(mesh.devices.reshape(2, 4, 2, 2, 8), ("xh", "y", "core", "xl", "z"))
    in_specs = (P(None, ROW + COL, None), P(None, COL + ROW, None), P(), P(), P(ROW, COL, None))
    out_specs = (P(ROW, COL, None), P(None, ROW + COL, None), P(None, COL + ROW, None), P(), P())
    return jax.shard_map(
        per_device, mesh=fine, in_specs=in_specs, out_specs=out_specs, check_vma=False
    )
```

```python
import jax
import jax.numpy as jnp
from jax import lax
from jax.experimental import pallas as pl
from jax.experimental.pallas import tpu as pltpu
from jax.sharding import Mesh
from jax.sharding import PartitionSpec as P

S = 128
C = 32
CZ = 128
T = 32
PEERS = 16
F32 = jnp.float32
BF16 = jnp.bfloat16
ROW = ("xh", "y", "core")
COL = ("xl", "z")
PLANE = ("xh", "y", "xl")
VMEM_MIB = 24


def params(mib):
    return pltpu.CompilerParams(vmem_limit_bytes=mib << 20)


def split(x):
    hi = x.astype(BF16)
    return hi, (x - hi.astype(F32)).astype(BF16)


def mm(a, b):
    return lax.dot_general(a, b, (((1,), (0,)), ((), ())), preferred_element_type=F32)


def mm_t(a, b):
    return lax.dot_general(a, b, (((1,), (1,)), ((), ())), preferred_element_type=F32)


def lanes(shape):
    return lax.broadcasted_iota(jnp.int32, shape, 1)


def swap_groups(a):
    lane = lanes(a[0].shape)
    low = lane < 64
    even = (lane & 32) == 0
    b = [None] * 4
    for g in (0, 1):
        b[g] = jnp.where(low, a[g], pltpu.roll(a[g + 2], 64, 1))
        b[g + 2] = jnp.where(low, pltpu.roll(a[g], 64, 1), a[g + 2])
    out = [None] * 4
    for g in (0, 2):
        out[g] = jnp.where(even, b[g], pltpu.roll(b[g + 1], 32, 1))
        out[g + 1] = jnp.where(even, pltpu.roll(b[g], 96, 1), b[g + 1])
    return out


def relayout(x, hi_ref, lo_ref, outer):
    for q in range(8):
        pieces = [x[32 * g : 32 * g + 32, 128 * q : 128 * q + 128] for g in range(4)]
        for r, piece in enumerate(swap_groups(pieces)):
            hi, lo = split(piece)
            rows = pl.ds((4 * q + r) * 32, 32)
            hi_ref[rows, pl.ds(outer, 128)] = hi
            lo_ref[rows, pl.ds(outer, 128)] = lo


def by_second(w_ref, hi_ref, lo_ref):
    for d in range(C):
        hi, lo = split(w_ref[pl.ds(d, C, stride=C), :])
        hi_ref[32 * d : 32 * d + 32, :] = hi
        lo_ref[32 * d : 32 * d + 32, :] = lo


def grad_kernel(cot_ref, w_ref, ghi_ref, glo_ref, bias_ref, whi, wlo):
    by_second(w_ref, whi, wlo)
    bias_ref[...] = jnp.zeros_like(bias_ref)

    def step(q, carry):
        at = pl.multiple_of(q * 128, 128)
        cot = cot_ref[pl.ds(at, 128), :]
        bias_ref[...] += cot.reshape(16, 8, CZ).sum(axis=0)
        hi, lo = split(cot)
        g = mm_t(hi, whi[...]) + mm_t(hi, wlo[...]) + mm_t(lo, whi[...])
        relayout(g, ghi_ref, glo_ref, at)
        return carry

    lax.fori_loop(0, 8, step, 0)


def where_index():
    xh, y, core = (lax.axis_index(a) for a in ROW)
    return jnp.stack([xh, y, core]).astype(jnp.int32)


def row_peer(at_ref, k, n, other, sign):
    xh, y, core = at_ref[0], at_ref[1], at_ref[2]
    y = lax.rem(y + (4 + sign * k), 4)
    xh = 1 - xh if n else xh
    core = 1 - core if other else core
    return xh * 8 + y * 2 + core


def outer_kernel(at_ref, gl_ref, r0, r1, r2, r3, o0, o1, o2, o3, cot_ref, bias_ref, fhi_ref, flo_ref, keep_ref, send_ref, l2_ref, rt_ref, lhi, llo, ct, wg):
    for q in range(4):
        rows = pl.ds(256 * q, 256)
        hi, lo = split(gl_ref[rows, :] * (1.0 / S))
        lhi[rows, :] = hi
        llo[rows, :] = lo
        l2_ref[rows, 0:128] = hi
        l2_ref[rows, 128:256] = lo
    for other, refs in enumerate(((r0, r1, r2, r3), (o0, o1, o2, o3))):
        for k, ref in enumerate(refs):
            for n in range(2):
                p = row_peer(at_ref, k, n, other, -1)
                for t in range(2):
                    rt_ref[pl.ds(2 * p + t, 32, stride=32), :] = ref[n, 32 * t : 32 * t + 32, :]

    def step(q, carry):
        at = pl.multiple_of(q * 128, 128)
        hi, lo = split(rt_ref[pl.ds(at, 128), :])
        x = mm_t(hi, lhi[...]) + mm_t(hi, llo[...]) + mm_t(lo, lhi[...])
        relayout(x, fhi_ref, flo_ref, at)
        chi, clo = split(cot_ref[pl.ds(at, 128), :].T)
        ct[0:128, pl.ds(at, 128)] = chi
        ct[128:256, pl.ds(at, 128)] = clo
        return carry

    lax.fori_loop(0, 8, step, 0)

    def wgrad(n, carry):
        at = pl.multiple_of(n * 256, 256)
        both = mm(ct[...], fhi_ref[:, pl.ds(at, 256)])
        out = both[:CZ] + both[CZ:] + mm(ct[0:128, :], flo_ref[:, pl.ds(at, 256)])
        out = out.T
        for k in range(8):
            wg[pl.ds(n * 8 + k, C, stride=C), :] = out[32 * k : 32 * k + 32]
        return carry

    lax.fori_loop(0, 4, wgrad, 0)
    core = at_ref[2]
    for ref, half in ((keep_ref, core), (send_ref, 1 - core)):
        for k in range(16):
            ref[k, 0:32, :] = wg[pl.ds(pl.multiple_of(half * 512 + 32 * k, 32), 32), :]
            ref[k, 32:40, :] = bias_ref[...]


def pair_kernel(fhi_ref, flo_ref, w_ref, bias_ref, out_ref, w2):
    for d in range(C):
        hi, lo = split(w_ref[pl.ds(d, C, stride=C), :])
        w2[32 * d : 32 * d + 32, 0:128] = hi
        w2[32 * d : 32 * d + 32, 128:256] = lo

    def step(n, carry):
        rows = pl.ds(pl.multiple_of(n * 256, 256), 256)
        both = mm(fhi_ref[rows, :], w2[...])
        out = both[:, :CZ] + both[:, CZ:] + mm(flo_ref[rows, :], w2[:, 0:128])
        out_ref[rows, :] = out + bias_ref[...]
        return carry

    lax.fori_loop(0, 4, step, 0)


def factor_kernel(at_ref, ghi_ref, glo_ref, l2_ref, rt_ref, lp_ref, keep_ref, send_ref, r2, rp):
    for q in range(8):
        hi, lo = split(rt_ref[128 * q : 128 * q + 128, :].T * (1.0 / S))
        r2[0:128, 128 * q : 128 * q + 128] = hi
        r2[128:256, 128 * q : 128 * q + 128] = lo

    def right(n, carry):
        rows = pl.ds(pl.multiple_of(n * 256, 256), 256)
        both = mm(ghi_ref[rows, :], l2_ref[...])
        rp[rows, :] = both[:, :S] + both[:, S:] + mm(glo_ref[rows, :], l2_ref[:, 0:128])
        return carry

    lax.fori_loop(0, 4, right, 0)
    for other, ref in enumerate((keep_ref, send_ref)):
        for k in range(4):
            for n in range(2):
                p = row_peer(at_ref, k, n, other, 1)
                for t in range(2):
                    ref[k, n, 32 * t : 32 * t + 32, :] = rp[pl.ds(2 * p + t, 32, stride=32), :]

    def left(n, carry):
        at = pl.multiple_of(n * 256, 256)
        both = mm(r2[...], ghi_ref[:, pl.ds(at, 256)])
        out = both[:S] + both[S:] + mm(r2[0:128, :], glo_ref[:, pl.ds(at, 256)])
        lp_ref[pl.ds(at, 256), :] = out.T
        return carry

    lax.fori_loop(0, 4, left, 0)


def shapes(*entries):
    return [jax.ShapeDtypeStruct(s, t) for s, t in entries]


def cost(flops, moved):
    return pl.CostEstimate(flops=flops, bytes_accessed=moved, transcendentals=0)


BIG = 2 * 1024 * 1024 * 128


def exchange(x, axes):
    return lax.all_to_all(x, axes, split_axis=0, concat_axis=0, tiled=True)


def gather(x, axes, n):
    return exchange(jnp.broadcast_to(x, (n, *x.shape)), axes)


def other_core(x):
    return lax.ppermute(x, "core", [(0, 1), (1, 0)])


def across(x):
    return lax.ppermute(x, "xh", [(0, 1), (1, 0)])


def up(x, k):
    return lax.ppermute(x, "y", [(i, (i + k) % 4) for i in range(4)])


VM = pl.BlockSpec(memory_space=pltpu.VMEM)
SM = pl.BlockSpec(memory_space=pltpu.SMEM)


def per_device(left, right, weight, bias, cotangent):
    at = where_index()
    cot = cotangent.reshape(T * T, CZ)
    left_own = left.transpose(1, 2, 0).reshape(64, S)
    right_own = right.transpose(1, 2, 0).reshape(64, S)
    pair_own = jnp.stack([right_own, across(right_own)])
    near = [pair_own] + [up(pair_own, k) for k in (1, 2, 3)]
    far = [other_core(x) for x in near]
    left_all = gather(left_own, COL, PEERS).reshape(1024, S)

    ghi, glo, bias_part = pl.pallas_call(
        grad_kernel,
        out_shape=shapes(((1024, 1024), BF16), ((1024, 1024), BF16), ((8, CZ), F32)),
        scratch_shapes=[pltpu.VMEM((1024, CZ), BF16)] * 2,
        compiler_params=params(VMEM_MIB),
        cost_estimate=cost(3 * BIG, 6 << 20),
        name="grad_outer",
    )(cot, weight)

    fhi, flo, keep, send, l2, rt = pl.pallas_call(
        outer_kernel,
        out_shape=shapes(
            ((1024, 1024), BF16),
            ((1024, 1024), BF16),
            ((16, 40, CZ), F32),
            ((16, 40, CZ), F32),
            ((1024, 256), BF16),
            ((1024, S), F32),
        ),
        in_specs=[SM] + [VM] * 11,
        scratch_shapes=[
            pltpu.VMEM((1024, S), BF16),
            pltpu.VMEM((1024, S), BF16),
            pltpu.VMEM((256, 1024), BF16),
            pltpu.VMEM((1024, CZ), F32),
        ],
        compiler_params=params(VMEM_MIB),
        cost_estimate=cost(6 * BIG, 8 << 20),
        name="outer_and_weight_grad",
    )(at, left_all, *near, *far, cot, bias_part)

    chunks = keep + other_core(send)
    plane_sum = exchange(chunks, PLANE).sum(axis=0)
    total = gather(plane_sum, ("z",), 8).sum(axis=0) * (1.0 / 512)
    half = gather(total[:32], PLANE, 16).reshape(512, CZ)
    half_other = other_core(half)
    core = lax.axis_index("core")
    first = jnp.where(core == 0, half, half_other)
    second = jnp.where(core == 0, half_other, half)
    weight_grad = jnp.concatenate([first, second])
    bias_grad = total[32:].sum(axis=0)

    pair = pl.pallas_call(
        pair_kernel,
        out_shape=jax.ShapeDtypeStruct((1024, CZ), F32),
        scratch_shapes=[pltpu.VMEM((1024, 256), BF16)],
        compiler_params=params(VMEM_MIB),
        cost_estimate=cost(3 * BIG, 6 << 20),
        name="pair_out",
    )(fhi, flo, weight, bias.reshape(1, CZ))

    lp, rkeep, rsend = pl.pallas_call(
        factor_kernel,
        out_shape=shapes(((1024, S), F32), ((4, 2, 64, S), F32), ((4, 2, 64, S), F32)),
        in_specs=[SM] + [VM] * 4,
        scratch_shapes=[pltpu.VMEM((256, 1024), BF16), pltpu.VMEM((1024, S), F32)],
        compiler_params=params(VMEM_MIB),
        cost_estimate=cost(6 * BIG, 8 << 20),
        name="factor_grads",
    )(at, ghi, glo, l2, rt)

    left_sum = exchange(lp.reshape(PEERS, 64, S), COL).sum(axis=0)
    chip = rkeep + other_core(rsend)
    line = chip[0] + up(chip[1], 1) + up(chip[2], 2) + up(chip[3], 3)
    right_sum = line[0] + across(line[1])
    left_grad = left_sum.reshape(2, C, S).transpose(2, 0, 1)
    right_grad = right_sum.reshape(2, C, S).transpose(2, 0, 1)
    return pair.reshape(T, T, CZ), left_grad, right_grad, weight_grad, bias_grad


def solution(mesh):
    fine = Mesh(mesh.devices.reshape(2, 4, 2, 2, 8), ("xh", "y", "core", "xl", "z"))
    in_specs = (P(None, ROW + COL, None), P(None, COL + ROW, None), P(), P(), P(ROW, COL, None))
    out_specs = (P(ROW, COL, None), P(None, ROW + COL, None), P(None, COL + ROW, None), P(), P())
    return jax.shard_map(
        per_device, mesh=fine, in_specs=in_specs, out_specs=out_specs, check_vma=False
    )
```

```python
import jax
import jax.numpy as jnp
from jax import lax
from jax.experimental import pallas as pl
from jax.experimental.pallas import tpu as pltpu
from jax.sharding import Mesh
from jax.sharding import PartitionSpec as P

S = 128
C = 32
CZ = 128
T = 32
PEERS = 16
F32 = jnp.float32
BF16 = jnp.bfloat16
ROW = ("xh", "y", "core")
COL = ("xl", "z")
PLANE = ("xh", "y", "xl")
GRAD_MIB, OUTER_MIB, FACTOR_MIB, PAIR_MIB = 56, 50, 24, 24
ORDER = (0, 4, 2, 6, 1, 5, 3, 7)


def params(mib):
    return pltpu.CompilerParams(vmem_limit_bytes=mib << 20)


def split(x):
    hi = x.astype(BF16)
    return hi, (x - hi.astype(F32)).astype(BF16)


def mm(a, b):
    return lax.dot_general(a, b, (((1,), (0,)), ((), ())), preferred_element_type=F32)


def mm_t(a, b):
    return lax.dot_general(a, b, (((1,), (1,)), ((), ())), preferred_element_type=F32)


def lanes(shape):
    return lax.broadcasted_iota(jnp.int32, shape, 1)


def swap_groups(a):
    lane = lanes(a[0].shape)
    low = lane < 64
    even = (lane & 32) == 0
    b = [None] * 4
    for g in (0, 1):
        b[g] = jnp.where(low, a[g], pltpu.roll(a[g + 2], 64, 1))
        b[g + 2] = jnp.where(low, pltpu.roll(a[g], 64, 1), a[g + 2])
    out = [None] * 4
    for g in (0, 2):
        out[g] = jnp.where(even, b[g], pltpu.roll(b[g + 1], 32, 1))
        out[g + 1] = jnp.where(even, pltpu.roll(b[g], 96, 1), b[g + 1])
    return out


def relayout(x, hi_ref, lo_ref, outer):
    for q in range(8):
        pieces = [x[32 * g : 32 * g + 32, 128 * q : 128 * q + 128] for g in range(4)]
        for r, piece in enumerate(swap_groups(pieces)):
            hi, lo = split(piece)
            rows = pl.ds((4 * q + r) * 32, 32)
            hi_ref[rows, pl.ds(outer, 128)] = hi
            lo_ref[rows, pl.ds(outer, 128)] = lo


def by_second(w_ref, wide, low):
    for d in range(C):
        hi, lo = split(w_ref[pl.ds(d, C, stride=C), :])
        wide[32 * d : 32 * d + 32, 0:128] = hi
        wide[32 * d : 32 * d + 32, 128:256] = hi
        low[32 * d : 32 * d + 32, :] = lo


def three(hi, lo, wide, low):
    return mm_t(jnp.concatenate([hi, lo], axis=1), wide) + mm_t(hi, low)


def grad_kernel(cot_ref, w_ref, hi_out, lo_out, bias_ref, wide, low, ghi, glo, sems):
    by_second(w_ref, wide, low)
    bias_ref[...] = jnp.zeros_like(bias_ref)

    def copies(q):
        at = pl.ds(q * 128, 128)
        return [
            pltpu.make_async_copy(src.at[:, at], dst.at[:, at], sems.at[q, n])
            for n, (src, dst) in enumerate(((ghi, hi_out), (glo, lo_out)))
        ]

    for q in range(8):
        at = 128 * q
        cot = cot_ref[at : at + 128, :]
        bias_ref[...] += cot.reshape(16, 8, CZ).sum(axis=0)
        hi, lo = split(cot)
        relayout(three(hi, lo, wide[...], low[...]), ghi, glo, at)
        for copy in copies(q):
            copy.start()
    for q in range(8):
        for copy in copies(q):
            copy.wait()


def where_index():
    return jnp.stack([lax.axis_index(a) for a in ROW + COL]).astype(jnp.int32)


def row_peer(at_ref, k, n, other, sign):
    xh, y, core = at_ref[0], at_ref[1], at_ref[2]
    y = lax.rem(y + (4 + sign * k), 4)
    xh = 1 - xh if n else xh
    core = 1 - core if other else core
    return xh * 8 + y * 2 + core


def outer_kernel(
    at_ref, gl_ref, r0, r1, r2, r3, o0, o1, o2, o3, cot_ref, bias_ref,
    fhi_out, flo_out, l2_out, rt_out, keep_ref, send_ref,
    fhi, flo, l2, rt, wide, ct, wg, sems,
):
    for q in range(4):
        rows = pl.ds(256 * q, 256)
        hi, lo = split(gl_ref[rows, :] * (1.0 / S))
        wide[rows, 0:128] = hi
        wide[rows, 128:256] = hi
        l2[rows, 0:128] = hi
        l2[rows, 128:256] = lo
    for other, refs in enumerate(((r0, r1, r2, r3), (o0, o1, o2, o3))):
        for k, ref in enumerate(refs):
            for n in range(2):
                p = row_peer(at_ref, k, n, other, -1)
                for t in range(2):
                    rt[pl.ds(2 * p + t, 32, stride=32), :] = ref[n, 32 * t : 32 * t + 32, :]
    copies = [
        pltpu.make_async_copy(src, dst, sems.at[n])
        for n, (src, dst) in enumerate(((l2, l2_out), (rt, rt_out), (fhi, fhi_out), (flo, flo_out)))
    ]
    copies[0].start()
    copies[1].start()

    def step(q, carry):
        at = pl.multiple_of(q * 128, 128)
        hi, lo = split(rt[pl.ds(at, 128), :])
        relayout(three(hi, lo, wide[...], l2[:, 128:256]), fhi, flo, at)
        chi, clo = split(cot_ref[pl.ds(at, 128), :].T)
        ct[0:128, pl.ds(at, 128)] = chi
        ct[128:256, pl.ds(at, 128)] = clo
        return carry

    lax.fori_loop(0, 8, step, 0)
    copies[2].start()
    copies[3].start()

    def wgrad(n, carry):
        at = pl.multiple_of(n * 256, 256)
        both = mm(ct[...], fhi[:, pl.ds(at, 256)])
        out = both[:CZ] + both[CZ:] + mm(ct[0:128, :], flo[:, pl.ds(at, 256)])
        out = out.T
        for k in range(8):
            wg[pl.ds(n * 8 + k, C, stride=C), :] = out[32 * k : 32 * k + 32]
        return carry

    lax.fori_loop(0, 4, wgrad, 0)
    core = at_ref[2]
    for ref, half in ((keep_ref, core), (send_ref, 1 - core)):
        for k in range(16):
            ref[k, 0:32, :] = wg[pl.ds(pl.multiple_of(half * 512 + 32 * k, 32), 32), :]
            ref[k, 32:40, :] = bias_ref[...]
    for copy in copies:
        copy.wait()


def fetch(sources, targets, sems):
    copies = [
        [
            pltpu.make_async_copy(src.at[256 * n : 256 * n + 256], dst.at[256 * n : 256 * n + 256], sems.at[n, m])
            for m, (src, dst) in enumerate(zip(sources, targets, strict=True))
        ]
        for n in range(4)
    ]
    for rows in copies:
        for copy in rows:
            copy.start()

    def arrived(n):
        for copy in copies[n]:
            copy.wait()

    return arrived


def pair_kernel(fhi_in, flo_in, w_ref, bias_ref, out_ref, fhi, flo, w2, sems):
    arrived = fetch((fhi_in, flo_in), (fhi, flo), sems)
    for d in range(C):
        hi, lo = split(w_ref[pl.ds(d, C, stride=C), :])
        w2[32 * d : 32 * d + 32, 0:128] = hi
        w2[32 * d : 32 * d + 32, 128:256] = lo
    for n in range(4):
        arrived(n)
        rows = slice(256 * n, 256 * n + 256)
        both = mm(fhi[rows, :], w2[...])
        out = both[:, :CZ] + both[:, CZ:] + mm(flo[rows, :], w2[:, 0:128])
        out_ref[rows, :] = out + bias_ref[...]


def factor_kernel(
    at_ref, ghi_in, glo_in, l2_in, rt_in, lkeep_ref, lsend_ref, keep_ref, send_ref,
    ghi, glo, l2, rt, r2, rp, lp, sems,
):
    small = [
        pltpu.make_async_copy(src, dst, sems.at[4, n])
        for n, (src, dst) in enumerate(((l2_in, l2), (rt_in, rt)))
    ]
    for copy in small:
        copy.start()
    arrived = fetch((ghi_in, glo_in), (ghi, glo), sems)
    for copy in small:
        copy.wait()
    for q in range(8):
        hi, lo = split(rt[128 * q : 128 * q + 128, :].T * (1.0 / S))
        r2[0:128, 128 * q : 128 * q + 128] = hi
        r2[128:256, 128 * q : 128 * q + 128] = lo
    for n in range(4):
        arrived(n)
        rows = slice(256 * n, 256 * n + 256)
        both = mm(ghi[rows, :], l2[...])
        rp[rows, :] = both[:, :S] + both[:, S:] + mm(glo[rows, :], l2[:, 0:128])
    for other, ref in enumerate((keep_ref, send_ref)):
        for k in range(4):
            for n in range(2):
                p = row_peer(at_ref, k, n, other, 1)
                for t in range(2):
                    ref[k, n, 32 * t : 32 * t + 32, :] = rp[pl.ds(2 * p + t, 32, stride=32), :]

    def left(n, carry):
        at = pl.multiple_of(n * 256, 256)
        both = mm(r2[...], ghi[:, pl.ds(at, 256)])
        out = both[:S] + both[S:] + mm(r2[0:128, :], glo[:, pl.ds(at, 256)])
        lp[pl.ds(at, 256), :] = out.T
        return carry

    lax.fori_loop(0, 4, left, 0)
    xl, z = at_ref[3], at_ref[4]
    for ref, x in ((lkeep_ref, xl), (lsend_ref, 1 - xl)):
        for n, k in enumerate(ORDER):
            p = x * 8 + lax.rem(z + k, 8)
            ref[n] = lp[pl.ds(pl.multiple_of(p * 64, 64), 64), :]


def shapes(*entries):
    return [jax.ShapeDtypeStruct(s, t) for s, t in entries]


def cost(flops, moved):
    return pl.CostEstimate(flops=flops, bytes_accessed=moved, transcendentals=0)


BIG = 2 * 1024 * 1024 * 128


def exchange(x, axes):
    return lax.all_to_all(x, axes, split_axis=0, concat_axis=0, tiled=True)


def gather(x, axes, n):
    return exchange(jnp.broadcast_to(x, (n, *x.shape)), axes)


def other_core(x):
    return lax.ppermute(x, "core", [(0, 1), (1, 0)])


def across(x):
    return lax.ppermute(x, "xh", [(0, 1), (1, 0)])


def up(x, k):
    return lax.ppermute(x, "y", [(i, (i + k) % 4) for i in range(4)])


def along(x, k):
    return lax.ppermute(x, "z", [(i, (i + k) % 8) for i in range(8)])


def next_x(x):
    return lax.ppermute(x, "xl", [(0, 1), (1, 0)])


VM = pl.BlockSpec(memory_space=pltpu.VMEM)
SM = pl.BlockSpec(memory_space=pltpu.SMEM)
HB = pl.BlockSpec(memory_space=pltpu.HBM)


def per_device(left, right, weight, bias, cotangent):
    at = where_index()
    cot = cotangent.reshape(T * T, CZ)
    left_own = left.transpose(1, 2, 0).reshape(64, S)
    right_own = right.transpose(1, 2, 0).reshape(64, S)
    left_all = gather(left_own, COL, PEERS).reshape(1024, S)
    pair_own = jnp.stack([right_own, across(right_own)])

    ghi, glo, bias_part = pl.pallas_call(
        grad_kernel,
        out_shape=shapes(((1024, 1024), BF16), ((1024, 1024), BF16), ((8, CZ), F32)),
        out_specs=[HB, HB, VM],
        scratch_shapes=[
            pltpu.VMEM((1024, 256), BF16),
            pltpu.VMEM((1024, 128), BF16),
            pltpu.VMEM((1024, 1024), BF16),
            pltpu.VMEM((1024, 1024), BF16),
            pltpu.SemaphoreType.DMA((8, 2)),
        ],
        compiler_params=params(GRAD_MIB),
        cost_estimate=cost(3 * BIG, 6 << 20),
        name="grad_outer",
    )(cot, weight)

    pair_own, bias_part = lax.optimization_barrier((pair_own, bias_part))
    near = [pair_own] + [up(pair_own, k) for k in (1, 2, 3)]
    far = [other_core(x) for x in near]

    fhi, flo, l2, rt, keep, send = pl.pallas_call(
        outer_kernel,
        out_shape=shapes(
            ((1024, 1024), BF16),
            ((1024, 1024), BF16),
            ((1024, 256), BF16),
            ((1024, S), F32),
            ((16, 40, CZ), F32),
            ((16, 40, CZ), F32),
        ),
        in_specs=[SM] + [VM] * 11,
        out_specs=[HB] * 4 + [VM] * 2,
        scratch_shapes=[
            pltpu.VMEM((1024, 1024), BF16),
            pltpu.VMEM((1024, 1024), BF16),
            pltpu.VMEM((1024, 256), BF16),
            pltpu.VMEM((1024, S), F32),
            pltpu.VMEM((1024, 256), BF16),
            pltpu.VMEM((256, 1024), BF16),
            pltpu.VMEM((1024, CZ), F32),
            pltpu.SemaphoreType.DMA((4,)),
        ],
        compiler_params=params(OUTER_MIB),
        cost_estimate=cost(6 * BIG, 8 << 20),
        name="outer_and_weight_grad",
    )(at, left_all, *near, *far, cot, bias_part)

    chunks = keep + other_core(send)
    chunks, l2 = lax.optimization_barrier((chunks, l2))
    lkeep, lsend, rkeep, rsend = pl.pallas_call(
        factor_kernel,
        out_shape=shapes(*[((8, 64, S), F32)] * 2, *[((4, 2, 64, S), F32)] * 2),
        in_specs=[SM] + [HB] * 4,
        scratch_shapes=[
            pltpu.VMEM((1024, 1024), BF16),
            pltpu.VMEM((1024, 1024), BF16),
            pltpu.VMEM((1024, 256), BF16),
            pltpu.VMEM((1024, S), F32),
            pltpu.VMEM((256, 1024), BF16),
            pltpu.VMEM((1024, S), F32),
            pltpu.VMEM((1024, S), F32),
            pltpu.SemaphoreType.DMA((5, 2)),
        ],
        compiler_params=params(FACTOR_MIB),
        cost_estimate=cost(6 * BIG, 8 << 20),
        name="factor_grads",
    )(at, ghi, glo, l2, rt)

    plane_sum = exchange(chunks, PLANE).sum(axis=0)
    plane_sum, rkeep = lax.optimization_barrier((plane_sum, rkeep))
    total = gather(plane_sum, ("z",), 8).sum(axis=0) * (1.0 / 512)
    half = gather(total[:32], PLANE, 16).reshape(512, CZ)
    half_other = other_core(half)
    core = lax.axis_index("core")
    first = jnp.where(core == 0, half, half_other)
    second = jnp.where(core == 0, half_other, half)
    weight_grad = jnp.concatenate([first, second])
    bias_grad = total[32:].sum(axis=0)

    pair = pl.pallas_call(
        pair_kernel,
        out_shape=jax.ShapeDtypeStruct((1024, CZ), F32),
        in_specs=[HB] * 2 + [VM] * 2,
        scratch_shapes=[
            pltpu.VMEM((1024, 1024), BF16),
            pltpu.VMEM((1024, 1024), BF16),
            pltpu.VMEM((1024, 256), BF16),
            pltpu.SemaphoreType.DMA((4, 2)),
        ],
        compiler_params=params(PAIR_MIB),
        cost_estimate=cost(3 * BIG, 6 << 20),
        name="pair_out",
    )(fhi, flo, weight, bias.reshape(1, CZ))

    left_sum = lkeep + next_x(lsend)
    left_sum = left_sum[:4] + along(left_sum[4:], 1)
    left_sum = left_sum[:2] + along(left_sum[2:], 2)
    left_sum = left_sum[0] + along(left_sum[1], 4)
    chip = rkeep + other_core(rsend)
    line = chip[0] + up(chip[1], 1) + up(chip[2], 2) + up(chip[3], 3)
    right_sum = line[0] + across(line[1])
    left_grad = left_sum.reshape(2, C, S).transpose(2, 0, 1)
    right_grad = right_sum.reshape(2, C, S).transpose(2, 0, 1)
    return pair.reshape(T, T, CZ), left_grad, right_grad, weight_grad, bias_grad


def solution(mesh):
    fine = Mesh(mesh.devices.reshape(2, 4, 2, 2, 8), ("xh", "y", "core", "xl", "z"))
    in_specs = (P(None, ROW + COL, None), P(None, COL + ROW, None), P(), P(), P(ROW, COL, None))
    out_specs = (P(ROW, COL, None), P(None, ROW + COL, None), P(None, COL + ROW, None), P(), P())
    return jax.shard_map(
        per_device, mesh=fine, in_specs=in_specs, out_specs=out_specs, check_vma=False
    )
```

```python
import jax
import jax.numpy as jnp
from jax import lax
from jax.experimental import pallas as pl
from jax.experimental.pallas import tpu as pltpu
from jax.sharding import Mesh
from jax.sharding import PartitionSpec as P

S = 128
C = 32
CZ = 128
T = 32
PEERS = 16
F32 = jnp.float32
BF16 = jnp.bfloat16
ROW = ("xh", "y", "core")
COL = ("xl", "z")
PLANE = ("xh", "y", "xl")
OUTER_MIB, FACTOR_MIB, PAIR_MIB = 50, 24, 24
ORDER = (0, 4, 2, 6, 1, 5, 3, 7)


def params(mib):
    return pltpu.CompilerParams(vmem_limit_bytes=mib << 20)


def split(x):
    hi = x.astype(BF16)
    return hi, (x - hi.astype(F32)).astype(BF16)


def mm(a, b):
    return lax.dot_general(a, b, (((1,), (0,)), ((), ())), preferred_element_type=F32)


def mm_t(a, b):
    return lax.dot_general(a, b, (((1,), (1,)), ((), ())), preferred_element_type=F32)


def lanes(shape):
    return lax.broadcasted_iota(jnp.int32, shape, 1)


def swap_groups(a):
    lane = lanes(a[0].shape)
    low = lane < 64
    even = (lane & 32) == 0
    b = [None] * 4
    for g in (0, 1):
        b[g] = jnp.where(low, a[g], pltpu.roll(a[g + 2], 64, 1))
        b[g + 2] = jnp.where(low, pltpu.roll(a[g], 64, 1), a[g + 2])
    out = [None] * 4
    for g in (0, 2):
        out[g] = jnp.where(even, b[g], pltpu.roll(b[g + 1], 32, 1))
        out[g + 1] = jnp.where(even, pltpu.roll(b[g], 96, 1), b[g + 1])
    return out


def relayout(x, hi_ref, lo_ref, n):
    for q in range(8):
        for b in range(2):
            rows = [slice(32 * (4 * q + g), 32 * (4 * q + g) + 32) for g in range(4)]
            pieces = [x[r, 128 * b : 128 * b + 128] for r in rows]
            for r, piece in enumerate(swap_groups(pieces)):
                hi, lo = split(piece)
                to = pl.ds(pl.multiple_of((8 * n + 4 * b + r) * 32, 32), 32)
                hi_ref[to, 128 * q : 128 * q + 128] = hi
                lo_ref[to, 128 * q : 128 * q + 128] = lo


def by_second(w_ref, wide, low):
    for d in range(C):
        hi, lo = split(w_ref[pl.ds(d, C, stride=C), :])
        wide[32 * d : 32 * d + 32, 0:128] = hi
        wide[32 * d : 32 * d + 32, 128:256] = hi
        low[32 * d : 32 * d + 32, :] = lo


def where_index():
    return jnp.stack([lax.axis_index(a) for a in ROW + COL]).astype(jnp.int32)


def row_peer(at_ref, k, n, other, sign):
    xh, y, core = at_ref[0], at_ref[1], at_ref[2]
    y = lax.rem(y + (4 + sign * k), 4)
    xh = 1 - xh if n else xh
    core = 1 - core if other else core
    return xh * 8 + y * 2 + core


def outer_kernel(
    at_ref, gl_ref, r0, r1, r2, r3, o0, o1, o2, o3, cot_ref,
    fhi_out, flo_out, l2_out, rt_out, keep_ref, send_ref,
    fhi, flo, l2, rt, rboth, wide, ct, wg, bias, sems,
):
    for q in range(4):
        rows = pl.ds(256 * q, 256)
        hi, lo = split(gl_ref[rows, :] * (1.0 / S))
        wide[rows, 0:128] = hi
        wide[rows, 128:256] = hi
        l2[rows, 0:128] = hi
        l2[rows, 128:256] = lo
    for other, refs in enumerate(((r0, r1, r2, r3), (o0, o1, o2, o3))):
        for k, ref in enumerate(refs):
            for n in range(2):
                p = row_peer(at_ref, k, n, other, -1)
                for t in range(2):
                    rt[pl.ds(2 * p + t, 32, stride=32), :] = ref[n, 32 * t : 32 * t + 32, :]
    copies = [
        pltpu.make_async_copy(src, dst, sems.at[n])
        for n, (src, dst) in enumerate(((l2, l2_out), (rt, rt_out), (fhi, fhi_out), (flo, flo_out)))
    ]
    copies[0].start()
    copies[1].start()

    for q in range(8):
        at = slice(128 * q, 128 * q + 128)
        cot = cot_ref[at, :]
        part = cot.reshape(16, 8, CZ).sum(axis=0)
        bias[...] = part if q == 0 else bias[...] + part
        chi, clo = split(cot.T)
        ct[0:128, at] = chi
        ct[128:256, at] = clo
        hi, lo = split(rt[at, :])
        rboth[at, 0:128] = hi
        rboth[at, 128:256] = lo

    def step(n, carry):
        rows = pl.ds(pl.multiple_of(n * 256, 256), 256)
        x = mm_t(rboth[...], wide[rows, :]) + mm_t(rboth[:, 0:128], l2[rows, 128:256])
        relayout(x, fhi, flo, n)
        return carry

    lax.fori_loop(0, 4, step, 0)
    copies[2].start()
    copies[3].start()

    def wgrad(n, carry):
        at = pl.multiple_of(n * 256, 256)
        both = mm(ct[...], fhi[:, pl.ds(at, 256)])
        out = both[:CZ] + both[CZ:] + mm(ct[0:128, :], flo[:, pl.ds(at, 256)])
        out = out.T
        for k in range(8):
            wg[pl.ds(n * 8 + k, C, stride=C), :] = out[32 * k : 32 * k + 32]
        return carry

    lax.fori_loop(0, 4, wgrad, 0)
    core = at_ref[2]
    for ref, half in ((keep_ref, core), (send_ref, 1 - core)):
        for k in range(16):
            ref[k, 0:32, :] = wg[pl.ds(pl.multiple_of(half * 512 + 32 * k, 32), 32), :]
            ref[k, 32:40, :] = bias[...]
    for copy in copies:
        copy.wait()


def fetch(sources, targets, sems):
    copies = [
        [
            pltpu.make_async_copy(src.at[256 * n : 256 * n + 256], dst.at[256 * n : 256 * n + 256], sems.at[n, m])
            for m, (src, dst) in enumerate(zip(sources, targets, strict=True))
        ]
        for n in range(4)
    ]
    for rows in copies:
        for copy in rows:
            copy.start()

    def arrived(n):
        for copy in copies[n]:
            copy.wait()

    return arrived


def pair_kernel(fhi_in, flo_in, w_ref, bias_ref, out_ref, fhi, flo, w2, sems):
    arrived = fetch((fhi_in, flo_in), (fhi, flo), sems)
    for d in range(C):
        hi, lo = split(w_ref[pl.ds(d, C, stride=C), :])
        w2[32 * d : 32 * d + 32, 0:128] = hi
        w2[32 * d : 32 * d + 32, 128:256] = lo
    for n in range(2):
        arrived(2 * n)
        arrived(2 * n + 1)
        rows = slice(512 * n, 512 * n + 512)
        both = mm(fhi[rows, :], w2[...])
        out = both[:, :CZ] + both[:, CZ:] + mm(flo[rows, :], w2[:, 0:128])
        out_ref[rows, :] = out + bias_ref[...]


def factor_kernel(
    at_ref, cot_ref, w_ref, l2_in, rt_in, lkeep_ref, lsend_ref, keep_ref, send_ref,
    wide, low, cboth, ghi, glo, l2, rt, r2, rp, lp, sems,
):
    copies = [
        pltpu.make_async_copy(src, dst, sems.at[n])
        for n, (src, dst) in enumerate(((l2_in, l2), (rt_in, rt)))
    ]
    for copy in copies:
        copy.start()
    by_second(w_ref, wide, low)
    for q in range(8):
        at = slice(128 * q, 128 * q + 128)
        hi, lo = split(cot_ref[at, :])
        cboth[at, 0:128] = hi
        cboth[at, 128:256] = lo

    def step(n, carry):
        rows = pl.ds(pl.multiple_of(n * 256, 256), 256)
        g = mm_t(cboth[...], wide[rows, :]) + mm_t(cboth[:, 0:128], low[rows, :])
        relayout(g, ghi, glo, n)
        return carry

    lax.fori_loop(0, 4, step, 0)
    for copy in copies:
        copy.wait()
    for n in range(2):
        rows = slice(512 * n, 512 * n + 512)
        both = mm(ghi[rows, :], l2[...])
        rp[rows, :] = both[:, :S] + both[:, S:] + mm(glo[rows, :], l2[:, 0:128])
    for q in range(8):
        hi, lo = split(rt[128 * q : 128 * q + 128, :].T * (1.0 / S))
        r2[0:128, 128 * q : 128 * q + 128] = hi
        r2[128:256, 128 * q : 128 * q + 128] = lo
    for other, ref in enumerate((keep_ref, send_ref)):
        for k in range(4):
            for n in range(2):
                p = row_peer(at_ref, k, n, other, 1)
                for t in range(2):
                    ref[k, n, 32 * t : 32 * t + 32, :] = rp[pl.ds(2 * p + t, 32, stride=32), :]

    def left(n, carry):
        at = pl.multiple_of(n * 256, 256)
        both = mm(r2[...], ghi[:, pl.ds(at, 256)])
        out = both[:S] + both[S:] + mm(r2[0:128, :], glo[:, pl.ds(at, 256)])
        lp[pl.ds(at, 256), :] = out.T
        return carry

    lax.fori_loop(0, 4, left, 0)
    xl, z = at_ref[3], at_ref[4]
    for ref, x in ((lkeep_ref, xl), (lsend_ref, 1 - xl)):
        for n, k in enumerate(ORDER):
            p = x * 8 + lax.rem(z + k, 8)
            ref[n] = lp[pl.ds(pl.multiple_of(p * 64, 64), 64), :]


def shapes(*entries):
    return [jax.ShapeDtypeStruct(s, t) for s, t in entries]


def cost(flops, moved):
    return pl.CostEstimate(flops=flops, bytes_accessed=moved, transcendentals=0)


BIG = 2 * 1024 * 1024 * 128


def exchange(x, axes):
    return lax.all_to_all(x, axes, split_axis=0, concat_axis=0, tiled=True)


def gather(x, axes, n):
    return exchange(jnp.broadcast_to(x, (n, *x.shape)), axes)


def other_core(x):
    return lax.ppermute(x, "core", [(0, 1), (1, 0)])


def across(x):
    return lax.ppermute(x, "xh", [(0, 1), (1, 0)])


def up(x, k):
    return lax.ppermute(x, "y", [(i, (i + k) % 4) for i in range(4)])


def along(x, k):
    return lax.ppermute(x, "z", [(i, (i + k) % 8) for i in range(8)])


def next_x(x):
    return lax.ppermute(x, "xl", [(0, 1), (1, 0)])


VM = pl.BlockSpec(memory_space=pltpu.VMEM)
SM = pl.BlockSpec(memory_space=pltpu.SMEM)
HB = pl.BlockSpec(memory_space=pltpu.HBM)


def per_device(left, right, weight, bias, cotangent):
    at = where_index()
    cot = cotangent.reshape(T * T, CZ)
    left_own = left.transpose(1, 2, 0).reshape(64, S)
    right_own = right.transpose(1, 2, 0).reshape(64, S)
    left_all = gather(left_own, COL, PEERS).reshape(1024, S)
    pair_own = jnp.stack([right_own, across(right_own)])

    near = [pair_own] + [up(pair_own, k) for k in (1, 2, 3)]
    far = [other_core(x) for x in near]

    fhi, flo, l2, rt, keep, send = pl.pallas_call(
        outer_kernel,
        out_shape=shapes(
            ((1024, 1024), BF16),
            ((1024, 1024), BF16),
            ((1024, 256), BF16),
            ((1024, S), F32),
            ((16, 40, CZ), F32),
            ((16, 40, CZ), F32),
        ),
        in_specs=[SM] + [VM] * 10,
        out_specs=[HB] * 4 + [VM] * 2,
        scratch_shapes=[
            pltpu.VMEM((1024, 1024), BF16),
            pltpu.VMEM((1024, 1024), BF16),
            pltpu.VMEM((1024, 256), BF16),
            pltpu.VMEM((1024, S), F32),
            pltpu.VMEM((1024, 256), BF16),
            pltpu.VMEM((1024, 256), BF16),
            pltpu.VMEM((256, 1024), BF16),
            pltpu.VMEM((1024, CZ), F32),
            pltpu.VMEM((8, CZ), F32),
            pltpu.SemaphoreType.DMA((4,)),
        ],
        compiler_params=params(OUTER_MIB),
        cost_estimate=cost(6 * BIG, 8 << 20),
        name="outer_and_weight_grad",
    )(at, left_all, *near, *far, cot)

    chunks = keep + other_core(send)
    chunks, l2 = lax.optimization_barrier((chunks, l2))
    lkeep, lsend, rkeep, rsend = pl.pallas_call(
        factor_kernel,
        out_shape=shapes(*[((8, 64, S), F32)] * 2, *[((4, 2, 64, S), F32)] * 2),
        in_specs=[SM, VM, VM, HB, HB],
        scratch_shapes=[
            pltpu.VMEM((1024, 256), BF16),
            pltpu.VMEM((1024, 128), BF16),
            pltpu.VMEM((1024, 256), BF16),
            pltpu.VMEM((1024, 1024), BF16),
            pltpu.VMEM((1024, 1024), BF16),
            pltpu.VMEM((1024, 256), BF16),
            pltpu.VMEM((1024, S), F32),
            pltpu.VMEM((256, 1024), BF16),
            pltpu.VMEM((1024, S), F32),
            pltpu.VMEM((1024, S), F32),
            pltpu.SemaphoreType.DMA((2,)),
        ],
        compiler_params=params(FACTOR_MIB),
        cost_estimate=cost(6 * BIG, 8 << 20),
        name="factor_grads",
    )(at, cot, weight, l2, rt)

    plane_sum = exchange(chunks, PLANE).sum(axis=0)
    plane_sum, lkeep, rkeep = lax.optimization_barrier((plane_sum, lkeep, rkeep))
    total = gather(plane_sum, ("z",), 8).sum(axis=0) * (1.0 / 512)
    total, fhi = lax.optimization_barrier((total, fhi))
    half = gather(total[:32], PLANE, 16).reshape(512, CZ)
    pair = pl.pallas_call(
        pair_kernel,
        out_shape=jax.ShapeDtypeStruct((1024, CZ), F32),
        in_specs=[HB] * 2 + [VM] * 2,
        scratch_shapes=[
            pltpu.VMEM((1024, 1024), BF16),
            pltpu.VMEM((1024, 1024), BF16),
            pltpu.VMEM((1024, 256), BF16),
            pltpu.SemaphoreType.DMA((4, 2)),
        ],
        compiler_params=params(PAIR_MIB),
        cost_estimate=cost(3 * BIG, 6 << 20),
        name="pair_out",
    )(fhi, flo, weight, bias.reshape(1, CZ))
    half, pair = lax.optimization_barrier((half, pair))
    half_other = other_core(half)
    core = lax.axis_index("core")
    first = jnp.where(core == 0, half, half_other)
    second = jnp.where(core == 0, half_other, half)
    weight_grad = jnp.concatenate([first, second])
    bias_grad = total[32:].sum(axis=0)

    left_sum = lkeep + next_x(lsend)
    left_sum = left_sum[:4] + along(left_sum[4:], 1)
    chip = rkeep + other_core(rsend)
    left_sum, chip = lax.optimization_barrier((left_sum, chip))
    line = chip[0] + up(chip[1], 1) + up(chip[2], 2) + up(chip[3], 3)
    left_sum = left_sum[:2] + along(left_sum[2:], 2)
    left_sum = left_sum[0] + along(left_sum[1], 4)
    right_sum = line[0] + across(line[1])
    left_grad = left_sum.reshape(2, C, S).transpose(2, 0, 1)
    right_grad = right_sum.reshape(2, C, S).transpose(2, 0, 1)
    return pair.reshape(T, T, CZ), left_grad, right_grad, weight_grad, bias_grad


def solution(mesh):
    fine = Mesh(mesh.devices.reshape(2, 4, 2, 2, 8), ("xh", "y", "core", "xl", "z"))
    in_specs = (P(None, ROW + COL, None), P(None, COL + ROW, None), P(), P(), P(ROW, COL, None))
    out_specs = (P(ROW, COL, None), P(None, ROW + COL, None), P(None, COL + ROW, None), P(), P())
    return jax.shard_map(
        per_device, mesh=fine, in_specs=in_specs, out_specs=out_specs, check_vma=False
    )
```

```python
import jax
import jax.numpy as jnp
from jax import lax
from jax.experimental import pallas as pl
from jax.experimental.pallas import tpu as pltpu
from jax.sharding import Mesh
from jax.sharding import PartitionSpec as P

S = 128
C = 32
CZ = 128
T = 32
PEERS = 16
F32 = jnp.float32
BF16 = jnp.bfloat16
ROW = ("xh", "y", "core")
COL = ("xl", "z")
PLANE = ("xh", "y", "xl")
OUTER_MIB, FACTOR_MIB, PAIR_MIB = 50, 52, 24
ORDER = (0, 4, 2, 6, 1, 5, 3, 7)


def params(mib):
    return pltpu.CompilerParams(vmem_limit_bytes=mib << 20)


def split(x):
    hi = x.astype(BF16)
    return hi, (x - hi.astype(F32)).astype(BF16)


def mm(a, b):
    return lax.dot_general(a, b, (((1,), (0,)), ((), ())), preferred_element_type=F32)


def mm_t(a, b):
    return lax.dot_general(a, b, (((1,), (1,)), ((), ())), preferred_element_type=F32)


def lanes(shape):
    return lax.broadcasted_iota(jnp.int32, shape, 1)


def swap_groups(a):
    lane = lanes(a[0].shape)
    low = lane < 64
    even = (lane & 32) == 0
    b = [None] * 4
    for g in (0, 1):
        b[g] = jnp.where(low, a[g], pltpu.roll(a[g + 2], 64, 1))
        b[g + 2] = jnp.where(low, pltpu.roll(a[g], 64, 1), a[g + 2])
    out = [None] * 4
    for g in (0, 2):
        out[g] = jnp.where(even, b[g], pltpu.roll(b[g + 1], 32, 1))
        out[g + 1] = jnp.where(even, pltpu.roll(b[g], 96, 1), b[g + 1])
    return out


def relayout(x, hi_ref, lo_ref, n):
    for q in range(8):
        for b in range(2):
            rows = [slice(32 * (4 * q + g), 32 * (4 * q + g) + 32) for g in range(4)]
            pieces = [x[r, 128 * b : 128 * b + 128] for r in rows]
            for r, piece in enumerate(swap_groups(pieces)):
                hi, lo = split(piece)
                to = pl.ds(pl.multiple_of((8 * n + 4 * b + r) * 32, 32), 32)
                hi_ref[to, 128 * q : 128 * q + 128] = hi
                lo_ref[to, 128 * q : 128 * q + 128] = lo


def by_second(w_ref, wide, low):
    for d in range(C):
        hi, lo = split(w_ref[pl.ds(d, C, stride=C), :])
        wide[32 * d : 32 * d + 32, 0:128] = hi
        wide[32 * d : 32 * d + 32, 128:256] = hi
        low[32 * d : 32 * d + 32, :] = lo


def where_index():
    return jnp.stack([lax.axis_index(a) for a in ROW + COL]).astype(jnp.int32)


def row_peer(at_ref, k, n, other, sign):
    xh, y, core = at_ref[0], at_ref[1], at_ref[2]
    y = lax.rem(y + (4 + sign * k), 4)
    xh = 1 - xh if n else xh
    core = 1 - core if other else core
    return xh * 8 + y * 2 + core


def outer_kernel(
    at_ref, gl_ref, r0, r1, r2, r3, o0, o1, o2, o3, cot_in,
    fhi_out, flo_out, l2_out, rt_out, keep_ref, send_ref,
    fhi, flo, l2, rt, rboth, wide, ct, wg, bias, cot, sems,
):
    fetched = pltpu.make_async_copy(cot_in, cot, sems.at[4])
    fetched.start()
    for q in range(4):
        rows = pl.ds(256 * q, 256)
        hi, lo = split(gl_ref[rows, :] * (1.0 / S))
        wide[rows, 0:128] = hi
        wide[rows, 128:256] = hi
        l2[rows, 0:128] = hi
        l2[rows, 128:256] = lo
    for other, refs in enumerate(((r0, r1, r2, r3), (o0, o1, o2, o3))):
        for k, ref in enumerate(refs):
            for n in range(2):
                p = row_peer(at_ref, k, n, other, -1)
                for t in range(2):
                    rt[pl.ds(2 * p + t, 32, stride=32), :] = ref[n, 32 * t : 32 * t + 32, :]
    copies = [
        pltpu.make_async_copy(src, dst, sems.at[n])
        for n, (src, dst) in enumerate(((l2, l2_out), (rt, rt_out), (fhi, fhi_out), (flo, flo_out)))
    ]
    copies[0].start()
    copies[1].start()

    for q in range(8):
        at = slice(128 * q, 128 * q + 128)
        hi, lo = split(rt[at, :])
        rboth[at, 0:128] = hi
        rboth[at, 128:256] = lo

    def step(n, carry):
        rows = pl.ds(pl.multiple_of(n * 256, 256), 256)
        x = mm_t(rboth[...], wide[rows, :]) + mm_t(rboth[:, 0:128], l2[rows, 128:256])
        relayout(x, fhi, flo, n)
        return carry

    lax.fori_loop(0, 4, step, 0)
    copies[2].start()
    copies[3].start()
    fetched.wait()
    for q in range(8):
        at = slice(128 * q, 128 * q + 128)
        part = cot[at, :].reshape(16, 8, CZ).sum(axis=0)
        bias[...] = part if q == 0 else bias[...] + part
        chi, clo = split(cot[at, :].T)
        ct[0:128, at] = chi
        ct[128:256, at] = clo

    def wgrad(n, carry):
        at = pl.multiple_of(n * 256, 256)
        both = mm(ct[...], fhi[:, pl.ds(at, 256)])
        out = both[:CZ] + both[CZ:] + mm(ct[0:128, :], flo[:, pl.ds(at, 256)])
        out = out.T
        for k in range(8):
            wg[pl.ds(n * 8 + k, C, stride=C), :] = out[32 * k : 32 * k + 32]
        return carry

    lax.fori_loop(0, 4, wgrad, 0)
    core = at_ref[2]
    for ref, half in ((keep_ref, core), (send_ref, 1 - core)):
        for k in range(16):
            ref[k, 0:32, :] = wg[pl.ds(pl.multiple_of(half * 512 + 32 * k, 32), 32), :]
            ref[k, 32:40, :] = bias[...]
    for copy in copies:
        copy.wait()


def fetch(sources, targets, sems):
    copies = [
        [
            pltpu.make_async_copy(src.at[256 * n : 256 * n + 256], dst.at[256 * n : 256 * n + 256], sems.at[n, m])
            for m, (src, dst) in enumerate(zip(sources, targets, strict=True))
        ]
        for n in range(4)
    ]
    for rows in copies:
        for copy in rows:
            copy.start()

    def arrived(n):
        for copy in copies[n]:
            copy.wait()

    return arrived


def pair_kernel(fhi_in, flo_in, w_ref, bias_ref, out_ref, fhi, flo, w2, sems):
    arrived = fetch((fhi_in, flo_in), (fhi, flo), sems)
    for d in range(C):
        hi, lo = split(w_ref[pl.ds(d, C, stride=C), :])
        w2[32 * d : 32 * d + 32, 0:128] = hi
        w2[32 * d : 32 * d + 32, 128:256] = lo
    for n in range(2):
        arrived(2 * n)
        arrived(2 * n + 1)
        rows = slice(512 * n, 512 * n + 512)
        both = mm(fhi[rows, :], w2[...])
        out = both[:, :CZ] + both[:, CZ:] + mm(flo[rows, :], w2[:, 0:128])
        out_ref[rows, :] = out + bias_ref[...]


def factor_kernel(
    at_ref, w_in, cot_in, l2_in, rt_in, lkeep_ref, lsend_ref, keep_ref, send_ref,
    w, cot, wide, low, cboth, ghi, glo, l2, rt, r2, rp, lp, sems,
):
    copies = [
        pltpu.make_async_copy(src, dst, sems.at[n])
        for n, (src, dst) in enumerate(((w_in, w), (cot_in, cot), (l2_in, l2), (rt_in, rt)))
    ]
    for copy in copies:
        copy.start()
    copies[0].wait()
    by_second(w, wide, low)
    copies[1].wait()
    for q in range(8):
        at = slice(128 * q, 128 * q + 128)
        hi, lo = split(cot[at, :])
        cboth[at, 0:128] = hi
        cboth[at, 128:256] = lo

    def step(n, carry):
        rows = pl.ds(pl.multiple_of(n * 256, 256), 256)
        g = mm_t(cboth[...], wide[rows, :]) + mm_t(cboth[:, 0:128], low[rows, :])
        relayout(g, ghi, glo, n)
        return carry

    lax.fori_loop(0, 4, step, 0)
    copies[2].wait()
    copies[3].wait()
    for n in range(2):
        rows = slice(512 * n, 512 * n + 512)
        both = mm(ghi[rows, :], l2[...])
        rp[rows, :] = both[:, :S] + both[:, S:] + mm(glo[rows, :], l2[:, 0:128])
    for q in range(8):
        hi, lo = split(rt[128 * q : 128 * q + 128, :].T * (1.0 / S))
        r2[0:128, 128 * q : 128 * q + 128] = hi
        r2[128:256, 128 * q : 128 * q + 128] = lo
    for other, ref in enumerate((keep_ref, send_ref)):
        for k in range(4):
            for n in range(2):
                p = row_peer(at_ref, k, n, other, 1)
                for t in range(2):
                    ref[k, n, 32 * t : 32 * t + 32, :] = rp[pl.ds(2 * p + t, 32, stride=32), :]

    def left(n, carry):
        at = pl.multiple_of(n * 256, 256)
        both = mm(r2[...], ghi[:, pl.ds(at, 256)])
        out = both[:S] + both[S:] + mm(r2[0:128, :], glo[:, pl.ds(at, 256)])
        lp[pl.ds(at, 256), :] = out.T
        return carry

    lax.fori_loop(0, 4, left, 0)
    xl, z = at_ref[3], at_ref[4]
    for ref, x in ((lkeep_ref, xl), (lsend_ref, 1 - xl)):
        for n, k in enumerate(ORDER):
            p = x * 8 + lax.rem(z + k, 8)
            ref[n] = lp[pl.ds(pl.multiple_of(p * 64, 64), 64), :]


def copies_kernel(x_ref, out_ref):
    for k in range(out_ref.shape[0]):
        out_ref[k] = x_ref[...]


def add_kernel(x_ref, y_ref, out_ref):
    out_ref[...] = x_ref[...] + y_ref[...]


def sum_kernel(x_ref, out_ref):
    total = x_ref[0]
    for k in range(1, x_ref.shape[0]):
        total = total + x_ref[k]
    for k in range(out_ref.shape[0]):
        out_ref[k] = total


def total_kernel(x_ref, out_ref, bias_ref):
    total = x_ref[0]
    for k in range(1, x_ref.shape[0]):
        total = total + x_ref[k]
    total = total * (1.0 / 512)
    for k in range(out_ref.shape[0]):
        out_ref[k] = total[0:32]
    bias_ref[...] = total[32:40].sum(axis=0, keepdims=True)


def small(kernel, out_shape, name, *args):
    return pl.pallas_call(kernel, out_shape=out_shape, compiler_params=params(2), name=name)(*args)


def shapes(*entries):
    return [jax.ShapeDtypeStruct(s, t) for s, t in entries]


def cost(flops, moved):
    return pl.CostEstimate(flops=flops, bytes_accessed=moved, transcendentals=0)


BIG = 2 * 1024 * 1024 * 128


def exchange(x, axes):
    return lax.all_to_all(x, axes, split_axis=0, concat_axis=0, tiled=True)


def gather(x, axes, n):
    return exchange(jnp.broadcast_to(x, (n, *x.shape)), axes)


def other_core(x):
    return lax.ppermute(x, "core", [(0, 1), (1, 0)])


def across(x):
    return lax.ppermute(x, "xh", [(0, 1), (1, 0)])


def up(x, k):
    return lax.ppermute(x, "y", [(i, (i + k) % 4) for i in range(4)])


def along(x, k):
    return lax.ppermute(x, "z", [(i, (i + k) % 8) for i in range(8)])


def next_x(x):
    return lax.ppermute(x, "xl", [(0, 1), (1, 0)])


def after(event, *arrays):
    return lax.optimization_barrier((*arrays, event))[:-1]


VM = pl.BlockSpec(memory_space=pltpu.VMEM)
SM = pl.BlockSpec(memory_space=pltpu.SMEM)
HB = pl.BlockSpec(memory_space=pltpu.HBM)


def per_device(left, right, weight, bias, cotangent):
    at = where_index()
    cot = cotangent.reshape(T * T, CZ)
    left_own = left.transpose(1, 2, 0).reshape(64, S)
    right_own = right.transpose(1, 2, 0).reshape(64, S)
    left_all = exchange(small(copies_kernel, pltpu.VMEM((PEERS, 64, S), F32), "copies", left_own), COL)
    left_all = left_all.reshape(1024, S)
    pair_own = jnp.stack([right_own, across(right_own)])

    near = [pair_own] + [up(pair_own, k) for k in (1, 2, 3)]
    far = [other_core(x) for x in near]

    fhi, flo, l2, rt, keep, send = pl.pallas_call(
        outer_kernel,
        out_shape=shapes(
            ((1024, 1024), BF16),
            ((1024, 1024), BF16),
            ((1024, 256), BF16),
            ((1024, S), F32),
            ((16, 40, CZ), F32),
            ((16, 40, CZ), F32),
        ),
        in_specs=[SM] + [VM] * 9 + [HB],
        out_specs=[HB] * 4 + [VM] * 2,
        scratch_shapes=[
            pltpu.VMEM((1024, 1024), BF16),
            pltpu.VMEM((1024, 1024), BF16),
            pltpu.VMEM((1024, 256), BF16),
            pltpu.VMEM((1024, S), F32),
            pltpu.VMEM((1024, 256), BF16),
            pltpu.VMEM((1024, 256), BF16),
            pltpu.VMEM((256, 1024), BF16),
            pltpu.VMEM((1024, CZ), F32),
            pltpu.VMEM((8, CZ), F32),
            pltpu.VMEM((1024, CZ), F32),
            pltpu.SemaphoreType.DMA((5,)),
        ],
        compiler_params=params(OUTER_MIB),
        cost_estimate=cost(6 * BIG, 8 << 20),
        name="outer_and_weight_grad",
    )(at, left_all, *near, *far, cot)

    chunks = small(add_kernel, pltpu.VMEM((16, 40, CZ), F32), "chip_sum", keep, other_core(send))
    chunks, l2 = lax.optimization_barrier((chunks, l2))
    lkeep, lsend, rkeep, rsend = pl.pallas_call(
        factor_kernel,
        out_shape=shapes(*[((8, 64, S), F32)] * 2, *[((4, 2, 64, S), F32)] * 2),
        in_specs=[SM] + [HB] * 4,
        scratch_shapes=[
            pltpu.VMEM((1024, CZ), F32),
            pltpu.VMEM((1024, CZ), F32),
            pltpu.VMEM((1024, 256), BF16),
            pltpu.VMEM((1024, 128), BF16),
            pltpu.VMEM((1024, 256), BF16),
            pltpu.VMEM((1024, 1024), BF16),
            pltpu.VMEM((1024, 1024), BF16),
            pltpu.VMEM((1024, 256), BF16),
            pltpu.VMEM((1024, S), F32),
            pltpu.VMEM((256, 1024), BF16),
            pltpu.VMEM((1024, S), F32),
            pltpu.VMEM((1024, S), F32),
            pltpu.SemaphoreType.DMA((4,)),
        ],
        compiler_params=params(FACTOR_MIB),
        cost_estimate=cost(6 * BIG, 8 << 20),
        name="factor_grads",
    )(at, weight, cot, l2, rt)

    plane = exchange(chunks, PLANE)
    plane_sum = small(sum_kernel, pltpu.VMEM((8, 40, CZ), F32), "plane_sum", plane)
    lkeep, rkeep = after(plane_sum, lkeep, rkeep)
    (plane_sum,) = after(lsend, plane_sum)
    total, bias_grad = small(
        total_kernel,
        [pltpu.VMEM((16, 32, CZ), F32), jax.ShapeDtypeStruct((1, CZ), F32)],
        "total",
        exchange(plane_sum, ("z",)),
    )
    (fhi,) = after(total, fhi)
    half = exchange(total, PLANE).reshape(512, CZ)
    pair = pl.pallas_call(
        pair_kernel,
        out_shape=jax.ShapeDtypeStruct((1024, CZ), F32),
        in_specs=[HB] * 2 + [VM] * 2,
        scratch_shapes=[
            pltpu.VMEM((1024, 1024), BF16),
            pltpu.VMEM((1024, 1024), BF16),
            pltpu.VMEM((1024, 256), BF16),
            pltpu.SemaphoreType.DMA((4, 2)),
        ],
        compiler_params=params(PAIR_MIB),
        cost_estimate=cost(3 * BIG, 6 << 20),
        name="pair_out",
    )(fhi, flo, weight, bias.reshape(1, CZ))
    half, pair = lax.optimization_barrier((half, pair))
    half_other = other_core(half)
    core = lax.axis_index("core")
    first = jnp.where(core == 0, half, half_other)
    second = jnp.where(core == 0, half_other, half)
    weight_grad = jnp.concatenate([first, second])

    left_sum = lkeep + next_x(lsend)
    left_sum = left_sum[:4] + along(left_sum[4:], 1)
    chip = rkeep + other_core(rsend)
    left_kept, right_kept = after(total, left_sum[:2], chip[0])
    line = right_kept + up(chip[1], 1) + up(chip[2], 2) + up(chip[3], 3)
    left_sum = left_kept + along(left_sum[2:], 2)
    left_sum = left_sum[0] + along(left_sum[1], 4)
    right_sum = line[0] + across(line[1])
    left_grad = left_sum.reshape(2, C, S).transpose(2, 0, 1)
    right_grad = right_sum.reshape(2, C, S).transpose(2, 0, 1)
    return pair.reshape(T, T, CZ), left_grad, right_grad, weight_grad, bias_grad.reshape(CZ)


def solution(mesh):
    fine = Mesh(mesh.devices.reshape(2, 4, 2, 2, 8), ("xh", "y", "core", "xl", "z"))
    in_specs = (P(None, ROW + COL, None), P(None, COL + ROW, None), P(), P(), P(ROW, COL, None))
    out_specs = (P(ROW, COL, None), P(None, ROW + COL, None), P(None, COL + ROW, None), P(), P())
    return jax.shard_map(
        per_device, mesh=fine, in_specs=in_specs, out_specs=out_specs, check_vma=False
    )
```

```python
import jax
import jax.numpy as jnp
from jax import lax
from jax.experimental import pallas as pl
from jax.experimental.pallas import tpu as pltpu
from jax.sharding import Mesh
from jax.sharding import PartitionSpec as P

S = 128
C = 32
CZ = 128
T = 32
PEERS = 16
F32 = jnp.float32
BF16 = jnp.bfloat16
ROW = ("xh", "y", "core")
COL = ("xl", "z")
PLANE = ("xh", "y", "xl")
OUTER_MIB, FACTOR_MIB, PAIR_MIB = 50, 52, 24
ORDER = (0, 4, 2, 6, 1, 5, 3, 7)


def params(mib):
    return pltpu.CompilerParams(vmem_limit_bytes=mib << 20)


def split(x):
    hi = x.astype(BF16)
    return hi, (x - hi.astype(F32)).astype(BF16)


def mm(a, b):
    return lax.dot_general(a, b, (((1,), (0,)), ((), ())), preferred_element_type=F32)


def mm_t(a, b):
    return lax.dot_general(a, b, (((1,), (1,)), ((), ())), preferred_element_type=F32)


def lanes(shape):
    return lax.broadcasted_iota(jnp.int32, shape, 1)


def swap_groups(a):
    lane = lanes(a[0].shape)
    low = lane < 64
    even = (lane & 32) == 0
    b = [None] * 4
    for g in (0, 1):
        b[g] = jnp.where(low, a[g], pltpu.roll(a[g + 2], 64, 1))
        b[g + 2] = jnp.where(low, pltpu.roll(a[g], 64, 1), a[g + 2])
    out = [None] * 4
    for g in (0, 2):
        out[g] = jnp.where(even, b[g], pltpu.roll(b[g + 1], 32, 1))
        out[g + 1] = jnp.where(even, pltpu.roll(b[g], 96, 1), b[g + 1])
    return out


def relayout(x, hi_ref, lo_ref, n):
    for q in range(8):
        for b in range(2):
            rows = [slice(32 * (4 * q + g), 32 * (4 * q + g) + 32) for g in range(4)]
            pieces = [x[r, 128 * b : 128 * b + 128] for r in rows]
            for r, piece in enumerate(swap_groups(pieces)):
                hi, lo = split(piece)
                to = pl.ds(pl.multiple_of((8 * n + 4 * b + r) * 32, 32), 32)
                hi_ref[to, 128 * q : 128 * q + 128] = hi
                lo_ref[to, 128 * q : 128 * q + 128] = lo


def by_second(w_ref, wide, low):
    for d in range(C):
        hi, lo = split(w_ref[pl.ds(d, C, stride=C), :])
        wide[32 * d : 32 * d + 32, 0:128] = hi
        wide[32 * d : 32 * d + 32, 128:256] = hi
        low[32 * d : 32 * d + 32, :] = lo


def where_index():
    return jnp.stack([lax.axis_index(a) for a in ROW + COL]).astype(jnp.int32)


def row_peer(at_ref, k, n, other, sign):
    xh, y, core = at_ref[0], at_ref[1], at_ref[2]
    y = lax.rem(y + (4 + sign * k), 4)
    xh = 1 - xh if n else xh
    core = 1 - core if other else core
    return xh * 8 + y * 2 + core


def outer_kernel(
    at_ref, gl_ref, r0, r1, r2, r3, o0, o1, o2, o3, cot_in,
    fhi_out, flo_out, l2_out, rt_out, keep_ref, send_ref,
    fhi, flo, l2, rt, rboth, wide, ct, wg, bias, cot, sems,
):
    fetched = pltpu.make_async_copy(cot_in, cot, sems.at[4])
    fetched.start()
    for q in range(4):
        rows = pl.ds(256 * q, 256)
        hi, lo = split(gl_ref[rows, :] * (1.0 / S))
        wide[rows, 0:128] = hi
        wide[rows, 128:256] = hi
        l2[rows, 0:128] = hi
        l2[rows, 128:256] = lo
    for other, refs in enumerate(((r0, r1, r2, r3), (o0, o1, o2, o3))):
        for k, ref in enumerate(refs):
            for n in range(2):
                p = row_peer(at_ref, k, n, other, -1)
                for t in range(2):
                    rt[pl.ds(2 * p + t, 32, stride=32), :] = ref[n, 32 * t : 32 * t + 32, :]
    copies = [
        pltpu.make_async_copy(src, dst, sems.at[n])
        for n, (src, dst) in enumerate(((l2, l2_out), (rt, rt_out), (fhi, fhi_out), (flo, flo_out)))
    ]
    copies[0].start()
    copies[1].start()

    for q in range(8):
        at = slice(128 * q, 128 * q + 128)
        hi, lo = split(rt[at, :])
        rboth[at, 0:128] = hi
        rboth[at, 128:256] = lo

    def step(n, carry):
        rows = pl.ds(pl.multiple_of(n * 256, 256), 256)
        x = mm_t(rboth[...], wide[rows, :]) + mm_t(rboth[:, 0:128], l2[rows, 128:256])
        relayout(x, fhi, flo, n)
        return carry

    lax.fori_loop(0, 4, step, 0)
    copies[2].start()
    copies[3].start()
    fetched.wait()
    for q in range(8):
        at = slice(128 * q, 128 * q + 128)
        part = cot[at, :].reshape(16, 8, CZ).sum(axis=0)
        bias[...] = part if q == 0 else bias[...] + part
        chi, clo = split(cot[at, :].T)
        ct[0:128, at] = chi
        ct[128:256, at] = clo

    def wgrad(n, carry):
        at = pl.multiple_of(n * 256, 256)
        both = mm(ct[...], fhi[:, pl.ds(at, 256)])
        out = both[:CZ] + both[CZ:] + mm(ct[0:128, :], flo[:, pl.ds(at, 256)])
        out = out.T
        for k in range(8):
            wg[pl.ds(n * 8 + k, C, stride=C), :] = out[32 * k : 32 * k + 32]
        return carry

    lax.fori_loop(0, 4, wgrad, 0)
    core = at_ref[2]
    for ref, half in ((keep_ref, core), (send_ref, 1 - core)):
        for k in range(16):
            ref[k, 0:32, :] = wg[pl.ds(pl.multiple_of(half * 512 + 32 * k, 32), 32), :]
            ref[k, 32:40, :] = bias[...]
    for copy in copies:
        copy.wait()


def fetch(sources, targets, sems):
    copies = [
        [
            pltpu.make_async_copy(src.at[256 * n : 256 * n + 256], dst.at[256 * n : 256 * n + 256], sems.at[n, m])
            for m, (src, dst) in enumerate(zip(sources, targets, strict=True))
        ]
        for n in range(4)
    ]
    for rows in copies:
        for copy in rows:
            copy.start()

    def arrived(n):
        for copy in copies[n]:
            copy.wait()

    return arrived


def pair_kernel(fhi_in, flo_in, w_in, bias_ref, out_ref, fhi, flo, w, w2, sems):
    fetched = pltpu.make_async_copy(w_in, w, sems.at[4, 0])
    fetched.start()
    arrived = fetch((fhi_in, flo_in), (fhi, flo), sems)
    fetched.wait()
    for d in range(C):
        hi, lo = split(w[pl.ds(d, C, stride=C), :])
        w2[32 * d : 32 * d + 32, 0:128] = hi
        w2[32 * d : 32 * d + 32, 128:256] = lo
    for n in range(2):
        arrived(2 * n)
        arrived(2 * n + 1)
        rows = slice(512 * n, 512 * n + 512)
        both = mm(fhi[rows, :], w2[...])
        out = both[:, :CZ] + both[:, CZ:] + mm(flo[rows, :], w2[:, 0:128])
        out_ref[rows, :] = out + bias_ref[...]


def factor_kernel(
    at_ref, w_in, cot_in, l2_in, rt_in, lkeep_ref, lsend_ref, keep_ref, send_ref,
    w, cot, wide, low, cboth, ghi, glo, l2, rt, r2, rp, lp, sems,
):
    copies = [
        pltpu.make_async_copy(src, dst, sems.at[n])
        for n, (src, dst) in enumerate(((w_in, w), (cot_in, cot), (l2_in, l2), (rt_in, rt)))
    ]
    for copy in copies:
        copy.start()
    copies[0].wait()
    by_second(w, wide, low)
    copies[1].wait()
    for q in range(8):
        at = slice(128 * q, 128 * q + 128)
        hi, lo = split(cot[at, :])
        cboth[at, 0:128] = hi
        cboth[at, 128:256] = lo

    def step(n, carry):
        rows = pl.ds(pl.multiple_of(n * 256, 256), 256)
        g = mm_t(cboth[...], wide[rows, :]) + mm_t(cboth[:, 0:128], low[rows, :])
        relayout(g, ghi, glo, n)
        return carry

    lax.fori_loop(0, 4, step, 0)
    copies[2].wait()
    copies[3].wait()
    for n in range(2):
        rows = slice(512 * n, 512 * n + 512)
        both = mm(ghi[rows, :], l2[...])
        rp[rows, :] = both[:, :S] + both[:, S:] + mm(glo[rows, :], l2[:, 0:128])
    for q in range(8):
        hi, lo = split(rt[128 * q : 128 * q + 128, :].T * (1.0 / S))
        r2[0:128, 128 * q : 128 * q + 128] = hi
        r2[128:256, 128 * q : 128 * q + 128] = lo
    for other, ref in enumerate((keep_ref, send_ref)):
        for k in range(4):
            for n in range(2):
                p = row_peer(at_ref, k, n, other, 1)
                for t in range(2):
                    ref[k, n, 32 * t : 32 * t + 32, :] = rp[pl.ds(2 * p + t, 32, stride=32), :]

    def left(n, carry):
        at = pl.multiple_of(n * 256, 256)
        both = mm(r2[...], ghi[:, pl.ds(at, 256)])
        out = both[:S] + both[S:] + mm(r2[0:128, :], glo[:, pl.ds(at, 256)])
        lp[pl.ds(at, 256), :] = out.T
        return carry

    lax.fori_loop(0, 4, left, 0)
    xl, z = at_ref[3], at_ref[4]
    for ref, x in ((lkeep_ref, xl), (lsend_ref, 1 - xl)):
        for n, k in enumerate(ORDER):
            p = x * 8 + lax.rem(z + k, 8)
            ref[n] = lp[pl.ds(pl.multiple_of(p * 64, 64), 64), :]


def copies_kernel(x_ref, out_ref, sems):
    copies = [pltpu.make_async_copy(x_ref, out_ref.at[k], sems.at[k]) for k in range(PEERS)]
    for copy in copies:
        copy.start()
    for copy in copies:
        copy.wait()


def parts_kernel(x_ref, y_ref, *outs):
    at = 0
    for out_ref in outs:
        n = out_ref.shape[0]
        out_ref[...] = x_ref[at : at + n] + y_ref[at : at + n]
        at += n


def add_kernel(x_ref, y_ref, out_ref):
    out_ref[...] = x_ref[...] + y_ref[...]


def sum_kernel(x_ref, out_ref):
    total = x_ref[0]
    for k in range(1, x_ref.shape[0]):
        total = total + x_ref[k]
    for k in range(out_ref.shape[0]):
        out_ref[k] = total


def total_kernel(x_ref, out_ref, bias_ref):
    total = x_ref[0]
    for k in range(1, x_ref.shape[0]):
        total = total + x_ref[k]
    total = total * (1.0 / 512)
    for k in range(out_ref.shape[0]):
        out_ref[k] = total[0:32]
    bias_ref[...] = total[32:40].sum(axis=0, keepdims=True)


def small(kernel, out_shape, name, *args):
    return pl.pallas_call(
        kernel,
        out_shape=out_shape,
        compiler_params=params(2),
        cost_estimate=cost(1 << 18, 3 << 20),
        name=name,
    )(*args)


def shapes(*entries):
    return [jax.ShapeDtypeStruct(s, t) for s, t in entries]


def cost(flops, moved):
    return pl.CostEstimate(flops=flops, bytes_accessed=moved, transcendentals=0)


BIG = 2 * 1024 * 1024 * 128


def exchange(x, axes):
    return lax.all_to_all(x, axes, split_axis=0, concat_axis=0, tiled=True)


def gather(x, axes, n):
    return exchange(jnp.broadcast_to(x, (n, *x.shape)), axes)


def other_core(x):
    return lax.ppermute(x, "core", [(0, 1), (1, 0)])


def across(x):
    return lax.ppermute(x, "xh", [(0, 1), (1, 0)])


def up(x, k):
    return lax.ppermute(x, "y", [(i, (i + k) % 4) for i in range(4)])


def along(x, k):
    return lax.ppermute(x, "z", [(i, (i + k) % 8) for i in range(8)])


def next_x(x):
    return lax.ppermute(x, "xl", [(0, 1), (1, 0)])


def in_hbm(x):
    return pltpu.with_memory_space_constraint(x, pltpu.HBM)


def after(event, *arrays):
    return lax.optimization_barrier((*arrays, event))[:-1]


VM = pl.BlockSpec(memory_space=pltpu.VMEM)
SM = pl.BlockSpec(memory_space=pltpu.SMEM)
HB = pl.BlockSpec(memory_space=pltpu.HBM)


def per_device(left, right, weight, bias, cotangent):
    at = where_index()
    cot = in_hbm(cotangent.reshape(T * T, CZ))
    weight = in_hbm(weight)
    left_own = left.transpose(1, 2, 0).reshape(64, S)
    right_own = right.transpose(1, 2, 0).reshape(64, S)
    left_copies = pl.pallas_call(
        copies_kernel,
        out_shape=pltpu.VMEM((PEERS, 64, S), F32),
        in_specs=[HB],
        scratch_shapes=[pltpu.SemaphoreType.DMA((PEERS,))],
        compiler_params=params(2),
        name="copies",
    )(in_hbm(left_own))
    left_all = exchange(left_copies, COL)
    left_all = left_all.reshape(1024, S)
    pair_own = jnp.stack([right_own, across(right_own)])

    near = [pair_own] + [up(pair_own, k) for k in (1, 2, 3)]
    far = [other_core(x) for x in near]

    fhi, flo, l2, rt, keep, send = pl.pallas_call(
        outer_kernel,
        out_shape=[
            pltpu.HBM((1024, 1024), BF16),
            pltpu.HBM((1024, 1024), BF16),
            pltpu.HBM((1024, 256), BF16),
            pltpu.HBM((1024, S), F32),
            pltpu.VMEM((16, 40, CZ), F32),
            pltpu.VMEM((16, 40, CZ), F32),
        ],
        in_specs=[SM] + [VM] * 9 + [HB],
        out_specs=[HB] * 4 + [VM] * 2,
        scratch_shapes=[
            pltpu.VMEM((1024, 1024), BF16),
            pltpu.VMEM((1024, 1024), BF16),
            pltpu.VMEM((1024, 256), BF16),
            pltpu.VMEM((1024, S), F32),
            pltpu.VMEM((1024, 256), BF16),
            pltpu.VMEM((1024, 256), BF16),
            pltpu.VMEM((256, 1024), BF16),
            pltpu.VMEM((1024, CZ), F32),
            pltpu.VMEM((8, CZ), F32),
            pltpu.VMEM((1024, CZ), F32),
            pltpu.SemaphoreType.DMA((5,)),
        ],
        compiler_params=params(OUTER_MIB),
        cost_estimate=cost(6 * BIG, 8 << 20),
        name="outer_and_weight_grad",
    )(at, left_all, *near, *far, cot)

    chunks = small(add_kernel, pltpu.VMEM((16, 40, CZ), F32), "chip_sum", keep, other_core(send))
    chunks, l2 = lax.optimization_barrier((chunks, l2))
    lkeep, lsend, rkeep, rsend = pl.pallas_call(
        factor_kernel,
        out_shape=[pltpu.VMEM((8, 64, S), F32)] * 2 + [pltpu.VMEM((4, 2, 64, S), F32)] * 2,
        in_specs=[SM] + [HB] * 4,
        scratch_shapes=[
            pltpu.VMEM((1024, CZ), F32),
            pltpu.VMEM((1024, CZ), F32),
            pltpu.VMEM((1024, 256), BF16),
            pltpu.VMEM((1024, 128), BF16),
            pltpu.VMEM((1024, 256), BF16),
            pltpu.VMEM((1024, 1024), BF16),
            pltpu.VMEM((1024, 1024), BF16),
            pltpu.VMEM((1024, 256), BF16),
            pltpu.VMEM((1024, S), F32),
            pltpu.VMEM((256, 1024), BF16),
            pltpu.VMEM((1024, S), F32),
            pltpu.VMEM((1024, S), F32),
            pltpu.SemaphoreType.DMA((4,)),
        ],
        compiler_params=params(FACTOR_MIB),
        cost_estimate=cost(6 * BIG, 8 << 20),
        name="factor_grads",
    )(at, weight, cot, in_hbm(l2), in_hbm(rt))

    plane = exchange(chunks, PLANE)
    plane_sum = small(sum_kernel, pltpu.VMEM((8, 40, CZ), F32), "plane_sum", plane)
    lkeep, rkeep = after(plane_sum, lkeep, rkeep)
    (plane_sum,) = after(lsend, plane_sum)
    total, bias_grad = small(
        total_kernel,
        [pltpu.VMEM((16, 32, CZ), F32), jax.ShapeDtypeStruct((1, CZ), F32)],
        "total",
        exchange(plane_sum, ("z",)),
    )
    (fhi,) = after(total, fhi)
    half = exchange(total, PLANE).reshape(512, CZ)
    pair = pl.pallas_call(
        pair_kernel,
        out_shape=jax.ShapeDtypeStruct((1024, CZ), F32),
        in_specs=[HB] * 3 + [VM],
        scratch_shapes=[
            pltpu.VMEM((1024, 1024), BF16),
            pltpu.VMEM((1024, 1024), BF16),
            pltpu.VMEM((1024, CZ), F32),
            pltpu.VMEM((1024, 256), BF16),
            pltpu.SemaphoreType.DMA((5, 2)),
        ],
        compiler_params=params(PAIR_MIB),
        cost_estimate=cost(3 * BIG, 6 << 20),
        name="pair_out",
    )(in_hbm(fhi), in_hbm(flo), weight, bias.reshape(1, CZ))
    half, pair = lax.optimization_barrier((half, pair))
    half_other = other_core(half)
    core = lax.axis_index("core")
    first = jnp.where(core == 0, half, half_other)
    second = jnp.where(core == 0, half_other, half)
    weight_grad = jnp.concatenate([first, second])

    left_sum, sent = small(
        parts_kernel, [pltpu.VMEM((4, 64, S), F32)] * 2, "left_x", lkeep, next_x(lsend)
    )
    left_sum = left_sum + along(sent, 1)
    chip = rkeep + other_core(rsend)
    left_kept, right_kept = after(total, left_sum[:2], chip[0])
    line = right_kept + up(chip[1], 1) + up(chip[2], 2) + up(chip[3], 3)
    left_sum = left_kept + along(left_sum[2:], 2)
    left_sum = left_sum[0] + along(left_sum[1], 4)
    right_sum = line[0] + across(line[1])
    left_grad = left_sum.reshape(2, C, S).transpose(2, 0, 1)
    right_grad = right_sum.reshape(2, C, S).transpose(2, 0, 1)
    return pair.reshape(T, T, CZ), left_grad, right_grad, weight_grad, bias_grad.reshape(CZ)


def solution(mesh):
    fine = Mesh(mesh.devices.reshape(2, 4, 2, 2, 8), ("xh", "y", "core", "xl", "z"))
    in_specs = (P(None, ROW + COL, None), P(None, COL + ROW, None), P(), P(), P(ROW, COL, None))
    out_specs = (P(ROW, COL, None), P(None, ROW + COL, None), P(None, COL + ROW, None), P(), P())
    return jax.shard_map(
        per_device, mesh=fine, in_specs=in_specs, out_specs=out_specs, check_vma=False
    )
```

```python
import jax
import jax.numpy as jnp
from jax import lax
from jax.experimental import pallas as pl
from jax.experimental.pallas import tpu as pltpu
from jax.sharding import Mesh
from jax.sharding import PartitionSpec as P

S = 128
C = 32
CZ = 128
T = 32
PEERS = 16
F32 = jnp.float32
BF16 = jnp.bfloat16
ROW = ("xh", "y", "core")
COL = ("xl", "z")
PLANE = ("xh", "y", "xl")
OUTER_MIB, FACTOR_MIB, PAIR_MIB = 50, 52, 56
ORDER = (0, 4, 2, 6, 1, 5, 3, 7)


def params(mib):
    return pltpu.CompilerParams(vmem_limit_bytes=mib << 20)


def split(x):
    hi = x.astype(BF16)
    return hi, (x - hi.astype(F32)).astype(BF16)


def mm(a, b):
    return lax.dot_general(a, b, (((1,), (0,)), ((), ())), preferred_element_type=F32)


def mm_t(a, b):
    return lax.dot_general(a, b, (((1,), (1,)), ((), ())), preferred_element_type=F32)


def lanes(shape):
    return lax.broadcasted_iota(jnp.int32, shape, 1)


def swap_groups(a):
    lane = lanes(a[0].shape)
    low = lane < 64
    even = (lane & 32) == 0
    b = [None] * 4
    for g in (0, 1):
        turned = pltpu.roll(jnp.where(low, a[g + 2], a[g]), 64, 1)
        b[g] = jnp.where(low, a[g], turned)
        b[g + 2] = jnp.where(low, turned, a[g + 2])
    out = [None] * 4
    for g in (0, 2):
        out[g] = jnp.where(even, b[g], pltpu.roll(b[g + 1], 32, 1))
        out[g + 1] = jnp.where(even, pltpu.roll(b[g], 96, 1), b[g + 1])
    return out


def relayout(x, hi_ref, lo_ref, n):
    for q in range(8):
        for b in range(2):
            rows = [slice(32 * (4 * q + g), 32 * (4 * q + g) + 32) for g in range(4)]
            pieces = [x[r, 128 * b : 128 * b + 128] for r in rows]
            for r, piece in enumerate(swap_groups(pieces)):
                hi, lo = split(piece)
                to = pl.ds(pl.multiple_of((8 * n + 4 * b + r) * 32, 32), 32)
                hi_ref[to, 128 * q : 128 * q + 128] = hi
                lo_ref[to, 128 * q : 128 * q + 128] = lo


def by_second(w_ref, wide, low):
    for d in range(C):
        hi, lo = split(w_ref[pl.ds(d, C, stride=C), :])
        wide[32 * d : 32 * d + 32, 0:128] = hi
        wide[32 * d : 32 * d + 32, 128:256] = hi
        low[32 * d : 32 * d + 32, :] = lo


def where_index():
    return jnp.stack([lax.axis_index(a) for a in ROW + COL]).astype(jnp.int32)


def row_peer(at_ref, k, n, other, sign):
    xh, y, core = at_ref[0], at_ref[1], at_ref[2]
    y = lax.rem(y + (4 + sign * k), 4)
    xh = 1 - xh if n else xh
    core = 1 - core if other else core
    return xh * 8 + y * 2 + core


def outer_kernel(
    at_ref, gl_ref, r0, r1, r2, r3, o0, o1, o2, o3, cot_in,
    fhi_out, flo_out, l2_out, rt_out, keep_ref, send_ref,
    fhi, flo, l2, rt, rboth, wide, ct, wg, bias, cot, sems,
):
    fetched = pltpu.make_async_copy(cot_in, cot, sems.at[4])
    fetched.start()
    for q in range(4):
        rows = pl.ds(256 * q, 256)
        hi, lo = split(gl_ref[rows, :] * (1.0 / S))
        wide[rows, 0:128] = hi
        wide[rows, 128:256] = hi
        l2[rows, 0:128] = hi
        l2[rows, 128:256] = lo
    for other, refs in enumerate(((r0, r1, r2, r3), (o0, o1, o2, o3))):
        for k, ref in enumerate(refs):
            for n in range(2):
                p = row_peer(at_ref, k, n, other, -1)
                for t in range(2):
                    rt[pl.ds(2 * p + t, 32, stride=32), :] = ref[n, 32 * t : 32 * t + 32, :]
    copies = [
        pltpu.make_async_copy(src, dst, sems.at[n])
        for n, (src, dst) in enumerate(((l2, l2_out), (rt, rt_out), (fhi, fhi_out), (flo, flo_out)))
    ]
    copies[0].start()
    copies[1].start()

    for q in range(8):
        at = slice(128 * q, 128 * q + 128)
        hi, lo = split(rt[at, :])
        rboth[at, 0:128] = hi
        rboth[at, 128:256] = lo

    def step(n, carry):
        rows = pl.ds(pl.multiple_of(n * 256, 256), 256)
        x = mm_t(rboth[...], wide[rows, :]) + mm_t(rboth[:, 0:128], l2[rows, 128:256])
        relayout(x, fhi, flo, n)
        return carry

    lax.fori_loop(0, 4, step, 0)
    copies[2].start()
    copies[3].start()
    fetched.wait()
    for q in range(8):
        at = slice(128 * q, 128 * q + 128)
        part = cot[at, :].reshape(16, 8, CZ).sum(axis=0)
        bias[...] = part if q == 0 else bias[...] + part
        chi, clo = split(cot[at, :].T)
        ct[0:128, at] = chi
        ct[128:256, at] = clo

    def wgrad(n, carry):
        at = pl.multiple_of(n * 256, 256)
        both = mm(ct[...], fhi[:, pl.ds(at, 256)])
        out = both[:CZ] + both[CZ:] + mm(ct[0:128, :], flo[:, pl.ds(at, 256)])
        out = out.T
        for k in range(8):
            wg[pl.ds(n * 8 + k, C, stride=C), :] = out[32 * k : 32 * k + 32]
        return carry

    lax.fori_loop(0, 4, wgrad, 0, unroll=True)
    core = at_ref[2]
    for ref, half in ((keep_ref, core), (send_ref, 1 - core)):
        for k in range(16):
            ref[k, 0:32, :] = wg[pl.ds(pl.multiple_of(half * 512 + 32 * k, 32), 32), :]
            ref[k, 32:40, :] = bias[...]
    for copy in copies:
        copy.wait()


def fetch(sources, targets, sems):
    copies = [
        [
            pltpu.make_async_copy(src.at[256 * n : 256 * n + 256], dst.at[256 * n : 256 * n + 256], sems.at[n, m])
            for m, (src, dst) in enumerate(zip(sources, targets, strict=True))
        ]
        for n in range(4)
    ]
    for rows in copies:
        for copy in rows:
            copy.start()

    def arrived(n):
        for copy in copies[n]:
            copy.wait()

    return arrived


def pair_kernel(fhi_in, flo_in, w_in, bias_ref, out_ref, fhi, flo, w, w2, sems):
    fetched = pltpu.make_async_copy(w_in, w, sems.at[4, 0])
    fetched.start()
    arrived = fetch((fhi_in, flo_in), (fhi, flo), sems)
    fetched.wait()
    for d in range(C):
        hi, lo = split(w[pl.ds(d, C, stride=C), :])
        w2[32 * d : 32 * d + 32, 0:128] = hi
        w2[32 * d : 32 * d + 32, 128:256] = lo
    for n in range(4):
        arrived(n)
        rows = slice(256 * n, 256 * n + 256)
        both = mm(fhi[rows, :], w2[...])
        out = both[:, :CZ] + both[:, CZ:] + mm(flo[rows, :], w2[:, 0:128])
        out_ref[rows, :] = out + bias_ref[...]


def factor_kernel(
    at_ref, w_in, cot_in, l2_in, rt_in, lkeep_ref, lsend_ref, keep_ref, send_ref,
    w, cot, wide, low, cboth, ghi, glo, l2, rt, r2, rp, lp, sems,
):
    copies = [
        pltpu.make_async_copy(src, dst, sems.at[n])
        for n, (src, dst) in enumerate(((w_in, w), (cot_in, cot), (l2_in, l2), (rt_in, rt)))
    ]
    for copy in copies:
        copy.start()
    copies[0].wait()
    by_second(w, wide, low)
    copies[1].wait()
    for q in range(8):
        at = slice(128 * q, 128 * q + 128)
        hi, lo = split(cot[at, :])
        cboth[at, 0:128] = hi
        cboth[at, 128:256] = lo

    def step(n, carry):
        rows = pl.ds(pl.multiple_of(n * 256, 256), 256)
        g = mm_t(cboth[...], wide[rows, :]) + mm_t(cboth[:, 0:128], low[rows, :])
        relayout(g, ghi, glo, n)
        return carry

    lax.fori_loop(0, 4, step, 0)
    copies[2].wait()
    copies[3].wait()
    for n in range(2):
        rows = slice(512 * n, 512 * n + 512)
        both = mm(ghi[rows, :], l2[...])
        rp[rows, :] = both[:, :S] + both[:, S:] + mm(glo[rows, :], l2[:, 0:128])
    for q in range(8):
        hi, lo = split(rt[128 * q : 128 * q + 128, :].T * (1.0 / S))
        r2[0:128, 128 * q : 128 * q + 128] = hi
        r2[128:256, 128 * q : 128 * q + 128] = lo
    for other, ref in enumerate((keep_ref, send_ref)):
        for k in range(4):
            for n in range(2):
                p = row_peer(at_ref, k, n, other, 1)
                for t in range(2):
                    ref[k, n, 32 * t : 32 * t + 32, :] = rp[pl.ds(2 * p + t, 32, stride=32), :]

    def left(n, carry):
        at = pl.multiple_of(n * 256, 256)
        both = mm(r2[...], ghi[:, pl.ds(at, 256)])
        out = both[:S] + both[S:] + mm(r2[0:128, :], glo[:, pl.ds(at, 256)])
        lp[pl.ds(at, 256), :] = out.T
        return carry

    lax.fori_loop(0, 4, left, 0, unroll=True)
    xl, z = at_ref[3], at_ref[4]
    for ref, x in ((lkeep_ref, xl), (lsend_ref, 1 - xl)):
        for n, k in enumerate(ORDER):
            p = x * 8 + lax.rem(z + k, 8)
            ref[n] = lp[pl.ds(pl.multiple_of(p * 64, 64), 64), :]


def copies_kernel(x_ref, y_ref, copies_ref, y_out):
    y_out[...] = y_ref[...]
    x = x_ref[...]
    for k in range(PEERS):
        copies_ref[k] = x


def parts_kernel(x_ref, y_ref, *outs):
    at = 0
    for out_ref in outs:
        n = out_ref.shape[0]
        out_ref[...] = x_ref[at : at + n] + y_ref[at : at + n]
        at += n


def add_kernel(x_ref, y_ref, out_ref):
    out_ref[...] = x_ref[...] + y_ref[...]


def sum_kernel(x_ref, out_ref):
    total = x_ref[0]
    for k in range(1, x_ref.shape[0]):
        total = total + x_ref[k]
    for k in range(out_ref.shape[0]):
        out_ref[k] = total


def total_kernel(x_ref, out_ref, bias_ref):
    total = x_ref[0]
    for k in range(1, x_ref.shape[0]):
        total = total + x_ref[k]
    total = total * (1.0 / 512)
    for k in range(out_ref.shape[0]):
        out_ref[k] = total[0:32]
    bias_ref[...] = total[32:40].sum(axis=0, keepdims=True)


def small(kernel, out_shape, name, *args):
    return pl.pallas_call(
        kernel,
        out_shape=out_shape,
        compiler_params=params(2),
        cost_estimate=cost(1 << 18, 3 << 20),
        name=name,
    )(*args)


def shapes(*entries):
    return [jax.ShapeDtypeStruct(s, t) for s, t in entries]


def cost(flops, moved):
    return pl.CostEstimate(flops=flops, bytes_accessed=moved, transcendentals=0)


BIG = 2 * 1024 * 1024 * 128


def exchange(x, axes):
    return lax.all_to_all(x, axes, split_axis=0, concat_axis=0, tiled=True)


def gather(x, axes, n):
    return exchange(jnp.broadcast_to(x, (n, *x.shape)), axes)


def other_core(x):
    return lax.ppermute(x, "core", [(0, 1), (1, 0)])


def across(x):
    return lax.ppermute(x, "xh", [(0, 1), (1, 0)])


def up(x, k):
    return lax.ppermute(x, "y", [(i, (i + k) % 4) for i in range(4)])


def along(x, k):
    return lax.ppermute(x, "z", [(i, (i + k) % 8) for i in range(8)])


def next_x(x):
    return lax.ppermute(x, "xl", [(0, 1), (1, 0)])


def in_hbm(x):
    return pltpu.with_memory_space_constraint(x, pltpu.HBM)


def after(event, *arrays):
    return lax.optimization_barrier((*arrays, event))[:-1]


VM = pl.BlockSpec(memory_space=pltpu.VMEM)
SM = pl.BlockSpec(memory_space=pltpu.SMEM)
HB = pl.BlockSpec(memory_space=pltpu.HBM)


def per_device(left, right, weight, bias, cotangent):
    at = where_index()
    cot = in_hbm(cotangent.reshape(T * T, CZ))
    weight = in_hbm(weight)
    left_own = left.transpose(1, 2, 0).reshape(64, S)
    right_own = right.transpose(1, 2, 0).reshape(64, S)
    left_copies, right_own = pl.pallas_call(
        copies_kernel,
        out_shape=[pltpu.VMEM((PEERS, 64, S), F32), pltpu.VMEM((64, S), F32)],
        compiler_params=params(2),
        name="copies",
    )(in_hbm(left_own), in_hbm(right_own))
    left_all = exchange(left_copies, COL)
    left_all = left_all.reshape(1024, S)
    pair_own = jnp.stack([right_own, across(right_own)])

    near = [pair_own] + [up(pair_own, k) for k in (1, 2, 3)]
    far = [other_core(x) for x in near]

    fhi, flo, l2, rt, keep, send = pl.pallas_call(
        outer_kernel,
        out_shape=[
            pltpu.HBM((1024, 1024), BF16),
            pltpu.HBM((1024, 1024), BF16),
            pltpu.HBM((1024, 256), BF16),
            pltpu.HBM((1024, S), F32),
            pltpu.VMEM((16, 40, CZ), F32),
            pltpu.VMEM((16, 40, CZ), F32),
        ],
        in_specs=[SM] + [VM] * 9 + [HB],
        out_specs=[HB] * 4 + [VM] * 2,
        scratch_shapes=[
            pltpu.VMEM((1024, 1024), BF16),
            pltpu.VMEM((1024, 1024), BF16),
            pltpu.VMEM((1024, 256), BF16),
            pltpu.VMEM((1024, S), F32),
            pltpu.VMEM((1024, 256), BF16),
            pltpu.VMEM((1024, 256), BF16),
            pltpu.VMEM((256, 1024), BF16),
            pltpu.VMEM((1024, CZ), F32),
            pltpu.VMEM((8, CZ), F32),
            pltpu.VMEM((1024, CZ), F32),
            pltpu.SemaphoreType.DMA((5,)),
        ],
        compiler_params=params(OUTER_MIB),
        cost_estimate=cost(6 * BIG, 8 << 20),
        name="outer_and_weight_grad",
    )(at, left_all, *near, *far, cot)

    chunks = small(add_kernel, pltpu.VMEM((16, 40, CZ), F32), "chip_sum", keep, other_core(send))
    chunks, l2 = lax.optimization_barrier((chunks, l2))
    lkeep, lsend, rkeep, rsend = pl.pallas_call(
        factor_kernel,
        out_shape=[pltpu.VMEM((8, 64, S), F32)] * 2 + [pltpu.VMEM((4, 2, 64, S), F32)] * 2,
        in_specs=[SM] + [HB] * 4,
        scratch_shapes=[
            pltpu.VMEM((1024, CZ), F32),
            pltpu.VMEM((1024, CZ), F32),
            pltpu.VMEM((1024, 256), BF16),
            pltpu.VMEM((1024, 128), BF16),
            pltpu.VMEM((1024, 256), BF16),
            pltpu.VMEM((1024, 1024), BF16),
            pltpu.VMEM((1024, 1024), BF16),
            pltpu.VMEM((1024, 256), BF16),
            pltpu.VMEM((1024, S), F32),
            pltpu.VMEM((256, 1024), BF16),
            pltpu.VMEM((1024, S), F32),
            pltpu.VMEM((1024, S), F32),
            pltpu.SemaphoreType.DMA((4,)),
        ],
        compiler_params=params(FACTOR_MIB),
        cost_estimate=cost(6 * BIG, 8 << 20),
        name="factor_grads",
    )(at, weight, cot, in_hbm(l2), in_hbm(rt))

    plane = exchange(chunks, PLANE)
    plane_sum = small(sum_kernel, pltpu.VMEM((8, 40, CZ), F32), "plane_sum", plane)
    lkeep, rkeep = after(plane_sum, lkeep, rkeep)
    (plane_sum,) = after(lsend, plane_sum)
    total, bias_grad = small(
        total_kernel,
        [pltpu.VMEM((16, 32, CZ), F32), jax.ShapeDtypeStruct((1, CZ), F32)],
        "total",
        exchange(plane_sum, ("z",)),
    )
    (fhi,) = after(total, fhi)
    half = exchange(total, PLANE).reshape(512, CZ)
    pair = pl.pallas_call(
        pair_kernel,
        out_shape=jax.ShapeDtypeStruct((1024, CZ), F32),
        in_specs=[HB] * 3 + [VM],
        scratch_shapes=[
            pltpu.VMEM((1024, 1024), BF16),
            pltpu.VMEM((1024, 1024), BF16),
            pltpu.VMEM((1024, CZ), F32),
            pltpu.VMEM((1024, 256), BF16),
            pltpu.SemaphoreType.DMA((5, 2)),
        ],
        compiler_params=params(PAIR_MIB),
        cost_estimate=cost(3 * BIG, 6 << 20),
        name="pair_out",
    )(in_hbm(fhi), in_hbm(flo), weight, bias.reshape(1, CZ))
    half, pair = lax.optimization_barrier((half, pair))
    half_other = other_core(half)
    core = lax.axis_index("core")
    first = jnp.where(core == 0, half, half_other)
    second = jnp.where(core == 0, half_other, half)
    weight_grad = jnp.concatenate([first, second])

    left_sum, sent = small(
        parts_kernel, [pltpu.VMEM((4, 64, S), F32)] * 2, "left_x", lkeep, next_x(lsend)
    )
    left_sum = left_sum + along(sent, 1)
    chip = rkeep + other_core(rsend)
    left_kept, right_kept = after(total, left_sum[:2], chip[0])
    line = right_kept + up(chip[1], 1) + up(chip[2], 2) + up(chip[3], 3)
    left_sum = left_kept + along(left_sum[2:], 2)
    left_sum = left_sum[0] + along(left_sum[1], 4)
    right_sum = line[0] + across(line[1])
    left_grad = left_sum.reshape(2, C, S).transpose(2, 0, 1)
    right_grad = right_sum.reshape(2, C, S).transpose(2, 0, 1)
    return pair.reshape(T, T, CZ), left_grad, right_grad, weight_grad, bias_grad.reshape(CZ)


def solution(mesh):
    fine = Mesh(mesh.devices.reshape(2, 4, 2, 2, 8), ("xh", "y", "core", "xl", "z"))
    in_specs = (P(None, ROW + COL, None), P(None, COL + ROW, None), P(), P(), P(ROW, COL, None))
    out_specs = (P(ROW, COL, None), P(None, ROW + COL, None), P(None, COL + ROW, None), P(), P())
    return jax.shard_map(
        per_device, mesh=fine, in_specs=in_specs, out_specs=out_specs, check_vma=False
    )
```

```python
import jax
import jax.numpy as jnp
from jax import lax
from jax.experimental import pallas as pl
from jax.experimental.pallas import tpu as pltpu
from jax.sharding import Mesh
from jax.sharding import PartitionSpec as P

S = 128
C = 32
CZ = 128
T = 32
PEERS = 16
F32 = jnp.float32
BF16 = jnp.bfloat16
ROW = ("xh", "y", "core")
COL = ("xl", "z")
PLANE = ("xh", "y", "xl")
OUTER_MIB, FACTOR_MIB, PAIR_MIB = 50, 52, 56
ORDER = (0, 4, 2, 6, 1, 5, 3, 7)


def params(mib):
    return pltpu.CompilerParams(vmem_limit_bytes=mib << 20)


def split(x):
    hi = x.astype(BF16)
    return hi, (x - hi.astype(F32)).astype(BF16)


def mm(a, b):
    return lax.dot_general(a, b, (((1,), (0,)), ((), ())), preferred_element_type=F32)


def mm_t(a, b):
    return lax.dot_general(a, b, (((1,), (1,)), ((), ())), preferred_element_type=F32)


def lanes(shape):
    return lax.broadcasted_iota(jnp.int32, shape, 1)


def swap_groups(a):
    lane = lanes(a[0].shape)
    low = lane < 64
    even = (lane & 32) == 0
    b = [None] * 4
    for g in (0, 1):
        turned = pltpu.roll(jnp.where(low, a[g + 2], a[g]), 64, 1)
        b[g] = jnp.where(low, a[g], turned)
        b[g + 2] = jnp.where(low, turned, a[g + 2])
    out = [None] * 4
    for g in (0, 2):
        out[g] = jnp.where(even, b[g], pltpu.roll(b[g + 1], 32, 1))
        out[g + 1] = jnp.where(even, pltpu.roll(b[g], 96, 1), b[g + 1])
    return out


def relayout(x, hi_ref, lo_ref, n):
    for q in range(8):
        for b in range(2):
            rows = [slice(32 * (4 * q + g), 32 * (4 * q + g) + 32) for g in range(4)]
            pieces = [x[r, 128 * b : 128 * b + 128] for r in rows]
            for r, piece in enumerate(swap_groups(pieces)):
                hi, lo = split(piece)
                to = pl.ds(pl.multiple_of((8 * n + 4 * b + r) * 32, 32), 32)
                hi_ref[to, 128 * q : 128 * q + 128] = hi
                lo_ref[to, 128 * q : 128 * q + 128] = lo


def by_second(w_ref, wide, low):
    for d in range(C):
        hi, lo = split(w_ref[pl.ds(d, C, stride=C), :])
        wide[32 * d : 32 * d + 32, 0:128] = hi
        wide[32 * d : 32 * d + 32, 128:256] = hi
        low[32 * d : 32 * d + 32, :] = lo


def where_index():
    return jnp.stack([lax.axis_index(a) for a in ROW + COL]).astype(jnp.int32)


def row_peer(at_ref, k, n, other, sign):
    xh, y, core = at_ref[0], at_ref[1], at_ref[2]
    y = lax.rem(y + (4 + sign * k), 4)
    xh = 1 - xh if n else xh
    core = 1 - core if other else core
    return xh * 8 + y * 2 + core


def outer_kernel(
    at_ref, gl_ref, r0, r1, r2, r3, o0, o1, o2, o3, cot_in,
    fhi_out, flo_out, l2_out, rt_out, keep_ref, send_ref,
    fhi, flo, l2, rt, rboth, wide, ct, wg, bias, cot, sems,
):
    fetched = pltpu.make_async_copy(cot_in, cot, sems.at[4])
    fetched.start()
    for q in range(4):
        rows = pl.ds(256 * q, 256)
        hi, lo = split(gl_ref[rows, :] * (1.0 / S))
        wide[rows, 0:128] = hi
        wide[rows, 128:256] = hi
        l2[rows, 0:128] = hi
        l2[rows, 128:256] = lo
    for other, refs in enumerate(((r0, r1, r2, r3), (o0, o1, o2, o3))):
        for k, ref in enumerate(refs):
            for n in range(2):
                p = row_peer(at_ref, k, n, other, -1)
                for t in range(2):
                    rt[pl.ds(2 * p + t, 32, stride=32), :] = ref[n, 32 * t : 32 * t + 32, :]
    copies = [
        pltpu.make_async_copy(src, dst, sems.at[n])
        for n, (src, dst) in enumerate(((l2, l2_out), (rt, rt_out), (fhi, fhi_out), (flo, flo_out)))
    ]
    copies[0].start()
    copies[1].start()

    for q in range(8):
        at = slice(128 * q, 128 * q + 128)
        hi, lo = split(rt[at, :])
        rboth[at, 0:128] = hi
        rboth[at, 128:256] = lo

    def step(n, carry):
        rows = pl.ds(pl.multiple_of(n * 256, 256), 256)
        x = mm_t(rboth[...], wide[rows, :]) + mm_t(rboth[:, 0:128], l2[rows, 128:256])
        relayout(x, fhi, flo, n)
        return carry

    lax.fori_loop(0, 4, step, 0)
    copies[2].start()
    copies[3].start()
    fetched.wait()
    for q in range(8):
        at = slice(128 * q, 128 * q + 128)
        part = cot[at, :].reshape(16, 8, CZ).sum(axis=0)
        bias[...] = part if q == 0 else bias[...] + part
        chi, clo = split(cot[at, :].T)
        ct[0:128, at] = chi
        ct[128:256, at] = clo

    def wgrad(n, carry):
        at = pl.multiple_of(n * 256, 256)
        both = mm(ct[...], fhi[:, pl.ds(at, 256)])
        out = both[:CZ] + both[CZ:] + mm(ct[0:128, :], flo[:, pl.ds(at, 256)])
        out = out.T
        for k in range(8):
            wg[pl.ds(n * 8 + k, C, stride=C), :] = out[32 * k : 32 * k + 32]
        return carry

    lax.fori_loop(0, 4, wgrad, 0, unroll=True)
    core = at_ref[2]
    for ref, half in ((keep_ref, core), (send_ref, 1 - core)):
        for k in range(16):
            ref[k, 0:32, :] = wg[pl.ds(pl.multiple_of(half * 512 + 32 * k, 32), 32), :]
            ref[k, 32:40, :] = bias[...]
    for copy in copies:
        copy.wait()


def fetch(sources, targets, sems):
    copies = [
        [
            pltpu.make_async_copy(src.at[256 * n : 256 * n + 256], dst.at[256 * n : 256 * n + 256], sems.at[n, m])
            for m, (src, dst) in enumerate(zip(sources, targets, strict=True))
        ]
        for n in range(4)
    ]
    for rows in copies:
        for copy in rows:
            copy.start()

    def arrived(n):
        for copy in copies[n]:
            copy.wait()

    return arrived


def pair_kernel(fhi_in, flo_in, w_in, bias_ref, out_ref, fhi, flo, w, w2, sems):
    fetched = pltpu.make_async_copy(w_in, w, sems.at[4, 0])
    fetched.start()
    arrived = fetch((fhi_in, flo_in), (fhi, flo), sems)
    fetched.wait()
    for d in range(C):
        hi, lo = split(w[pl.ds(d, C, stride=C), :])
        w2[32 * d : 32 * d + 32, 0:128] = hi
        w2[32 * d : 32 * d + 32, 128:256] = lo
    for n in range(2):
        arrived(2 * n)
        arrived(2 * n + 1)
        rows = slice(512 * n, 512 * n + 512)
        both = mm(fhi[rows, :], w2[...])
        out = both[:, :CZ] + both[:, CZ:] + mm(flo[rows, :], w2[:, 0:128])
        out_ref[rows, :] = out + bias_ref[...]


def factor_kernel(
    at_ref, w_in, cot_in, l2_in, rt_in, lkeep_ref, lsend_ref, keep_ref, send_ref,
    w, cot, wide, low, cboth, ghi, glo, l2, rt, r2, rp, lp, sems,
):
    copies = [
        pltpu.make_async_copy(src, dst, sems.at[n])
        for n, (src, dst) in enumerate(((w_in, w), (cot_in, cot), (l2_in, l2), (rt_in, rt)))
    ]
    for copy in copies:
        copy.start()
    copies[0].wait()
    by_second(w, wide, low)
    copies[1].wait()
    for q in range(8):
        at = slice(128 * q, 128 * q + 128)
        hi, lo = split(cot[at, :])
        cboth[at, 0:128] = hi
        cboth[at, 128:256] = lo

    def step(n, carry):
        rows = pl.ds(pl.multiple_of(n * 256, 256), 256)
        g = mm_t(cboth[...], wide[rows, :]) + mm_t(cboth[:, 0:128], low[rows, :])
        relayout(g, ghi, glo, n)
        return carry

    lax.fori_loop(0, 4, step, 0)
    copies[2].wait()
    copies[3].wait()
    for n in range(2):
        rows = slice(512 * n, 512 * n + 512)
        both = mm(ghi[rows, :], l2[...])
        rp[rows, :] = both[:, :S] + both[:, S:] + mm(glo[rows, :], l2[:, 0:128])
    for q in range(8):
        hi, lo = split(rt[128 * q : 128 * q + 128, :].T * (1.0 / S))
        r2[0:128, 128 * q : 128 * q + 128] = hi
        r2[128:256, 128 * q : 128 * q + 128] = lo
    for other, ref in enumerate((keep_ref, send_ref)):
        for k in range(4):
            for n in range(2):
                p = row_peer(at_ref, k, n, other, 1)
                for t in range(2):
                    ref[k, n, 32 * t : 32 * t + 32, :] = rp[pl.ds(2 * p + t, 32, stride=32), :]

    def left(n, carry):
        at = pl.multiple_of(n * 256, 256)
        both = mm(r2[...], ghi[:, pl.ds(at, 256)])
        out = both[:S] + both[S:] + mm(r2[0:128, :], glo[:, pl.ds(at, 256)])
        lp[pl.ds(at, 256), :] = out.T
        return carry

    lax.fori_loop(0, 4, left, 0, unroll=True)
    xl, z = at_ref[3], at_ref[4]
    for ref, x in ((lkeep_ref, xl), (lsend_ref, 1 - xl)):
        for n, k in enumerate(ORDER):
            p = x * 8 + lax.rem(z + k, 8)
            ref[n] = lp[pl.ds(pl.multiple_of(p * 64, 64), 64), :]


def copies_kernel(x_ref, y_ref, copies_ref, y_out):
    y_out[...] = y_ref[...]
    x = x_ref[...]
    for k in range(PEERS):
        copies_ref[k] = x


def parts_kernel(x_ref, y_ref, *outs):
    at = 0
    for out_ref in outs:
        n = out_ref.shape[0]
        out_ref[...] = x_ref[at : at + n] + y_ref[at : at + n]
        at += n


def add_kernel(x_ref, y_ref, out_ref):
    out_ref[...] = x_ref[...] + y_ref[...]


def sum_kernel(x_ref, out_ref):
    total = x_ref[0]
    for k in range(1, x_ref.shape[0]):
        total = total + x_ref[k]
    for k in range(out_ref.shape[0]):
        out_ref[k] = total


def total_kernel(x_ref, out_ref, bias_ref):
    total = x_ref[0]
    for k in range(1, x_ref.shape[0]):
        total = total + x_ref[k]
    total = total * (1.0 / 512)
    for k in range(out_ref.shape[0]):
        out_ref[k] = total[0:32]
    bias_ref[...] = total[32:40].sum(axis=0, keepdims=True)


def small(kernel, out_shape, name, *args):
    return pl.pallas_call(
        kernel,
        out_shape=out_shape,
        compiler_params=params(2),
        cost_estimate=cost(1 << 18, 3 << 20),
        name=name,
    )(*args)


def shapes(*entries):
    return [jax.ShapeDtypeStruct(s, t) for s, t in entries]


def cost(flops, moved):
    return pl.CostEstimate(flops=flops, bytes_accessed=moved, transcendentals=0)


BIG = 2 * 1024 * 1024 * 128


def exchange(x, axes):
    return lax.all_to_all(x, axes, split_axis=0, concat_axis=0, tiled=True)


def gather(x, axes, n):
    return exchange(jnp.broadcast_to(x, (n, *x.shape)), axes)


def other_core(x):
    return lax.ppermute(x, "core", [(0, 1), (1, 0)])


def across(x):
    return lax.ppermute(x, "xh", [(0, 1), (1, 0)])


def up(x, k):
    return lax.ppermute(x, "y", [(i, (i + k) % 4) for i in range(4)])


def along(x, k):
    return lax.ppermute(x, "z", [(i, (i + k) % 8) for i in range(8)])


def next_x(x):
    return lax.ppermute(x, "xl", [(0, 1), (1, 0)])


def in_hbm(x):
    return pltpu.with_memory_space_constraint(x, pltpu.HBM)


def after(event, *arrays):
    return lax.optimization_barrier((*arrays, event))[:-1]


VM = pl.BlockSpec(memory_space=pltpu.VMEM)
SM = pl.BlockSpec(memory_space=pltpu.SMEM)
HB = pl.BlockSpec(memory_space=pltpu.HBM)


def per_device(left, right, weight, bias, cotangent):
    at = where_index()
    cot = in_hbm(cotangent.reshape(T * T, CZ))
    weight = in_hbm(weight)
    left_own = left.transpose(1, 2, 0).reshape(64, S)
    right_own = right.transpose(1, 2, 0).reshape(64, S)
    left_copies, right_own = pl.pallas_call(
        copies_kernel,
        out_shape=[pltpu.VMEM((PEERS, 64, S), F32), pltpu.VMEM((64, S), F32)],
        compiler_params=params(2),
        name="copies",
    )(in_hbm(left_own), in_hbm(right_own))
    left_all = exchange(left_copies, COL)
    left_all = left_all.reshape(1024, S)
    pair_own = jnp.stack([right_own, across(right_own)])

    near = [pair_own] + [up(pair_own, k) for k in (1, 2, 3)]
    far = [other_core(x) for x in near]

    fhi, flo, l2, rt, keep, send = pl.pallas_call(
        outer_kernel,
        out_shape=[
            pltpu.HBM((1024, 1024), BF16),
            pltpu.HBM((1024, 1024), BF16),
            pltpu.HBM((1024, 256), BF16),
            pltpu.HBM((1024, S), F32),
            pltpu.VMEM((16, 40, CZ), F32),
            pltpu.VMEM((16, 40, CZ), F32),
        ],
        in_specs=[SM] + [VM] * 9 + [HB],
        out_specs=[HB] * 4 + [VM] * 2,
        scratch_shapes=[
            pltpu.VMEM((1024, 1024), BF16),
            pltpu.VMEM((1024, 1024), BF16),
            pltpu.VMEM((1024, 256), BF16),
            pltpu.VMEM((1024, S), F32),
            pltpu.VMEM((1024, 256), BF16),
            pltpu.VMEM((1024, 256), BF16),
            pltpu.VMEM((256, 1024), BF16),
            pltpu.VMEM((1024, CZ), F32),
            pltpu.VMEM((8, CZ), F32),
            pltpu.VMEM((1024, CZ), F32),
            pltpu.SemaphoreType.DMA((5,)),
        ],
        compiler_params=params(OUTER_MIB),
        cost_estimate=cost(6 * BIG, 8 << 20),
        name="outer_and_weight_grad",
    )(at, left_all, *near, *far, cot)

    chunks = small(add_kernel, pltpu.VMEM((16, 40, CZ), F32), "chip_sum", keep, other_core(send))
    chunks, l2 = lax.optimization_barrier((chunks, l2))
    lkeep, lsend, rkeep, rsend = pl.pallas_call(
        factor_kernel,
        out_shape=[pltpu.VMEM((8, 64, S), F32)] * 2 + [pltpu.VMEM((4, 2, 64, S), F32)] * 2,
        in_specs=[SM] + [HB] * 4,
        scratch_shapes=[
            pltpu.VMEM((1024, CZ), F32),
            pltpu.VMEM((1024, CZ), F32),
            pltpu.VMEM((1024, 256), BF16),
            pltpu.VMEM((1024, 128), BF16),
            pltpu.VMEM((1024, 256), BF16),
            pltpu.VMEM((1024, 1024), BF16),
            pltpu.VMEM((1024, 1024), BF16),
            pltpu.VMEM((1024, 256), BF16),
            pltpu.VMEM((1024, S), F32),
            pltpu.VMEM((256, 1024), BF16),
            pltpu.VMEM((1024, S), F32),
            pltpu.VMEM((1024, S), F32),
            pltpu.SemaphoreType.DMA((4,)),
        ],
        compiler_params=params(FACTOR_MIB),
        cost_estimate=cost(6 * BIG, 8 << 20),
        name="factor_grads",
    )(at, weight, cot, in_hbm(l2), in_hbm(rt))

    plane = exchange(chunks, PLANE)
    plane_sum = small(sum_kernel, pltpu.VMEM((8, 40, CZ), F32), "plane_sum", plane)
    lkeep, rkeep = after(plane_sum, lkeep, rkeep)
    (plane_sum,) = after(lsend, plane_sum)
    left_sum, sent = small(
        parts_kernel, [pltpu.VMEM((4, 64, S), F32)] * 2, "left_x", lkeep, next_x(lsend)
    )
    left_sum = left_sum + along(sent, 1)
    chip = rkeep + other_core(rsend)
    total, bias_grad = small(
        total_kernel,
        [pltpu.VMEM((16, 32, CZ), F32), jax.ShapeDtypeStruct((1, CZ), F32)],
        "total",
        exchange(plane_sum, ("z",)),
    )
    (fhi,) = after(sent, fhi)
    pair = pl.pallas_call(
        pair_kernel,
        out_shape=jax.ShapeDtypeStruct((1024, CZ), F32),
        in_specs=[HB] * 3 + [VM],
        scratch_shapes=[
            pltpu.VMEM((1024, 1024), BF16),
            pltpu.VMEM((1024, 1024), BF16),
            pltpu.VMEM((1024, CZ), F32),
            pltpu.VMEM((1024, 256), BF16),
            pltpu.SemaphoreType.DMA((5, 2)),
        ],
        compiler_params=params(PAIR_MIB),
        cost_estimate=cost(3 * BIG, 6 << 20),
        name="pair_out",
    )(in_hbm(fhi), in_hbm(flo), weight, bias.reshape(1, CZ))
    (ready,) = after(pair, total)
    half = exchange(ready, PLANE).reshape(512, CZ)
    half_other = other_core(half)
    core = lax.axis_index("core")
    first = jnp.where(core == 0, half, half_other)
    second = jnp.where(core == 0, half_other, half)
    weight_grad = jnp.concatenate([first, second])

    left_kept, right_kept = after(total, left_sum[:2], chip[0])
    line = right_kept + up(chip[1], 1) + up(chip[2], 2) + up(chip[3], 3)
    left_sum = left_kept + along(left_sum[2:], 2)
    left_sum = left_sum[0] + along(left_sum[1], 4)
    right_sum = line[0] + across(line[1])
    left_grad = left_sum.reshape(2, C, S).transpose(2, 0, 1)
    right_grad = right_sum.reshape(2, C, S).transpose(2, 0, 1)
    return pair.reshape(T, T, CZ), left_grad, right_grad, weight_grad, bias_grad.reshape(CZ)


def solution(mesh):
    fine = Mesh(mesh.devices.reshape(2, 4, 2, 2, 8), ("xh", "y", "core", "xl", "z"))
    in_specs = (P(None, ROW + COL, None), P(None, COL + ROW, None), P(), P(), P(ROW, COL, None))
    out_specs = (P(ROW, COL, None), P(None, ROW + COL, None), P(None, COL + ROW, None), P(), P())
    return jax.shard_map(
        per_device, mesh=fine, in_specs=in_specs, out_specs=out_specs, check_vma=False
    )
```

```python
import jax
import jax.numpy as jnp
from jax import lax
from jax.experimental import pallas as pl
from jax.experimental.pallas import tpu as pltpu
from jax.sharding import Mesh
from jax.sharding import PartitionSpec as P

S = 128
C = 32
CZ = 128
T = 32
PEERS = 16
F32 = jnp.float32
BF16 = jnp.bfloat16
ROW = ("xh", "y", "core")
COL = ("xl", "z")
PLANE = ("xh", "y", "xl")
OUTER_MIB, FACTOR_MIB, PAIR_MIB = 50, 52, 16
ORDER = (0, 4, 2, 6, 1, 5, 3, 7)


def params(mib):
    return pltpu.CompilerParams(vmem_limit_bytes=mib << 20)


def split(x):
    hi = x.astype(BF16)
    return hi, (x - hi.astype(F32)).astype(BF16)


def mm(a, b):
    return lax.dot_general(a, b, (((1,), (0,)), ((), ())), preferred_element_type=F32)


def mm_t(a, b):
    return lax.dot_general(a, b, (((1,), (1,)), ((), ())), preferred_element_type=F32)


def lanes(shape):
    return lax.broadcasted_iota(jnp.int32, shape, 1)


def swap_groups(a):
    lane = lanes(a[0].shape)
    low = lane < 64
    even = (lane & 32) == 0
    b = [None] * 4
    for g in (0, 1):
        turned = pltpu.roll(jnp.where(low, a[g + 2], a[g]), 64, 1)
        b[g] = jnp.where(low, a[g], turned)
        b[g + 2] = jnp.where(low, turned, a[g + 2])
    out = [None] * 4
    for g in (0, 2):
        out[g] = jnp.where(even, b[g], pltpu.roll(b[g + 1], 32, 1))
        out[g + 1] = jnp.where(even, pltpu.roll(b[g], 96, 1), b[g + 1])
    return out


def relayout(x, hi_ref, lo_ref, n):
    for q in range(8):
        for b in range(2):
            rows = [slice(32 * (4 * q + g), 32 * (4 * q + g) + 32) for g in range(4)]
            pieces = [x[r, 128 * b : 128 * b + 128] for r in rows]
            for r, piece in enumerate(swap_groups(pieces)):
                hi, lo = split(piece)
                to = pl.ds(pl.multiple_of((8 * n + 4 * b + r) * 32, 32), 32)
                hi_ref[to, 128 * q : 128 * q + 128] = hi
                lo_ref[to, 128 * q : 128 * q + 128] = lo


def by_second(w_ref, wide, low):
    for d in range(C):
        hi, lo = split(w_ref[pl.ds(d, C, stride=C), :])
        wide[32 * d : 32 * d + 32, 0:128] = hi
        wide[32 * d : 32 * d + 32, 128:256] = hi
        low[32 * d : 32 * d + 32, :] = lo


def where_index():
    return jnp.stack([lax.axis_index(a) for a in ROW + COL]).astype(jnp.int32)


def row_peer(at_ref, k, n, other, sign):
    xh, y, core = at_ref[0], at_ref[1], at_ref[2]
    y = lax.rem(y + (4 + sign * k), 4)
    xh = 1 - xh if n else xh
    core = 1 - core if other else core
    return xh * 8 + y * 2 + core


def outer_kernel(
    at_ref, gl_ref, r0, r1, r2, r3, o0, o1, o2, o3, cot_in,
    fhi_out, flo_out, l2_out, rt_out, keep_ref, send_ref,
    fhi, flo, l2, rt, rboth, wide, ct, wg, bias, cot, sems,
):
    fetched = pltpu.make_async_copy(cot_in, cot, sems.at[4])
    fetched.start()
    for q in range(4):
        rows = pl.ds(256 * q, 256)
        hi, lo = split(gl_ref[rows, :] * (1.0 / S))
        wide[rows, 0:128] = hi
        wide[rows, 128:256] = hi
        l2[rows, 0:128] = hi
        l2[rows, 128:256] = lo
    for other, refs in enumerate(((r0, r1, r2, r3), (o0, o1, o2, o3))):
        for k, ref in enumerate(refs):
            for n in range(2):
                p = row_peer(at_ref, k, n, other, -1)
                for t in range(2):
                    rt[pl.ds(2 * p + t, 32, stride=32), :] = ref[n, 32 * t : 32 * t + 32, :]
    copies = [
        pltpu.make_async_copy(src, dst, sems.at[n])
        for n, (src, dst) in enumerate(((l2, l2_out), (rt, rt_out), (fhi, fhi_out), (flo, flo_out)))
    ]
    copies[0].start()
    copies[1].start()

    for q in range(8):
        at = slice(128 * q, 128 * q + 128)
        hi, lo = split(rt[at, :])
        rboth[at, 0:128] = hi
        rboth[at, 128:256] = lo

    def step(n, carry):
        rows = pl.ds(pl.multiple_of(n * 256, 256), 256)
        x = mm_t(rboth[...], wide[rows, :]) + mm_t(rboth[:, 0:128], l2[rows, 128:256])
        relayout(x, fhi, flo, n)
        return carry

    lax.fori_loop(0, 4, step, 0)
    copies[2].start()
    copies[3].start()
    fetched.wait()
    for q in range(8):
        at = slice(128 * q, 128 * q + 128)
        part = cot[at, :].reshape(16, 8, CZ).sum(axis=0)
        bias[...] = part if q == 0 else bias[...] + part
        chi, clo = split(cot[at, :].T)
        ct[0:128, at] = chi
        ct[128:256, at] = clo

    def wgrad(n, carry):
        at = pl.multiple_of(n * 256, 256)
        both = mm(ct[...], fhi[:, pl.ds(at, 256)])
        out = both[:CZ] + both[CZ:] + mm(ct[0:128, :], flo[:, pl.ds(at, 256)])
        out = out.T
        for k in range(8):
            wg[pl.ds(n * 8 + k, C, stride=C), :] = out[32 * k : 32 * k + 32]
        return carry

    lax.fori_loop(0, 4, wgrad, 0, unroll=True)
    core = at_ref[2]
    for ref, half in ((keep_ref, core), (send_ref, 1 - core)):
        for k in range(16):
            ref[k, 0:32, :] = wg[pl.ds(pl.multiple_of(half * 512 + 32 * k, 32), 32), :]
            ref[k, 32:40, :] = bias[...]
    for copy in copies:
        copy.wait()


def pair_kernel(fhi, flo_in, w, bias_ref, out_ref, flo, w2, sem):
    fetched = pltpu.make_async_copy(flo_in, flo, sem)
    fetched.start()
    for d in range(C):
        hi, lo = split(w[pl.ds(d, C, stride=C), :])
        w2[32 * d : 32 * d + 32, 0:128] = hi
        w2[32 * d : 32 * d + 32, 128:256] = lo
    for n in range(2):
        rows = slice(512 * n, 512 * n + 512)
        both = mm(fhi[rows, :], w2[...])
        out_ref[rows, :] = both[:, :CZ] + both[:, CZ:] + bias_ref[...]
    fetched.wait()
    for n in range(2):
        rows = slice(512 * n, 512 * n + 512)
        out_ref[rows, :] += mm(flo[rows, :], w2[:, 0:128])


def factor_kernel(
    at_ref, w_in, cot_in, l2_in, rt_in, lkeep_ref, lsend_ref, keep_ref, send_ref,
    w, cot, wide, low, cboth, ghi, glo, l2, rt, r2, rp, lp, sems,
):
    copies = [
        pltpu.make_async_copy(src, dst, sems.at[n])
        for n, (src, dst) in enumerate(((w_in, w), (cot_in, cot), (l2_in, l2), (rt_in, rt)))
    ]
    for copy in copies:
        copy.start()
    copies[0].wait()
    by_second(w, wide, low)
    copies[1].wait()
    for q in range(8):
        at = slice(128 * q, 128 * q + 128)
        hi, lo = split(cot[at, :])
        cboth[at, 0:128] = hi
        cboth[at, 128:256] = lo

    def step(n, carry):
        rows = pl.ds(pl.multiple_of(n * 256, 256), 256)
        g = mm_t(cboth[...], wide[rows, :]) + mm_t(cboth[:, 0:128], low[rows, :])
        relayout(g, ghi, glo, n)
        return carry

    lax.fori_loop(0, 4, step, 0)
    copies[2].wait()
    copies[3].wait()
    for n in range(2):
        rows = slice(512 * n, 512 * n + 512)
        both = mm(ghi[rows, :], l2[...])
        rp[rows, :] = both[:, :S] + both[:, S:] + mm(glo[rows, :], l2[:, 0:128])
    for q in range(8):
        hi, lo = split(rt[128 * q : 128 * q + 128, :].T * (1.0 / S))
        r2[0:128, 128 * q : 128 * q + 128] = hi
        r2[128:256, 128 * q : 128 * q + 128] = lo
    for other, ref in enumerate((keep_ref, send_ref)):
        for k in range(4):
            for n in range(2):
                p = row_peer(at_ref, k, n, other, 1)
                for t in range(2):
                    ref[k, n, 32 * t : 32 * t + 32, :] = rp[pl.ds(2 * p + t, 32, stride=32), :]

    def left(n, carry):
        at = pl.multiple_of(n * 256, 256)
        both = mm(r2[...], ghi[:, pl.ds(at, 256)])
        out = both[:S] + both[S:] + mm(r2[0:128, :], glo[:, pl.ds(at, 256)])
        lp[pl.ds(at, 256), :] = out.T
        return carry

    lax.fori_loop(0, 4, left, 0, unroll=True)
    xl, z = at_ref[3], at_ref[4]
    for ref, x in ((lkeep_ref, xl), (lsend_ref, 1 - xl)):
        for n, k in enumerate(ORDER):
            p = x * 8 + lax.rem(z + k, 8)
            ref[n] = lp[pl.ds(pl.multiple_of(p * 64, 64), 64), :]


def copies_kernel(x_ref, y_ref, copies_ref, y_out):
    y_out[...] = y_ref[...]
    x = x_ref[...]
    for k in range(PEERS):
        copies_ref[k] = x


def parts_kernel(x_ref, y_ref, *outs):
    at = 0
    for out_ref in outs:
        n = out_ref.shape[0]
        out_ref[...] = x_ref[at : at + n] + y_ref[at : at + n]
        at += n


def add_kernel(x_ref, y_ref, out_ref):
    out_ref[...] = x_ref[...] + y_ref[...]


def sum_kernel(x_ref, out_ref):
    total = x_ref[0]
    for k in range(1, x_ref.shape[0]):
        total = total + x_ref[k]
    for k in range(out_ref.shape[0]):
        out_ref[k] = total


def total_kernel(x_ref, out_ref, bias_ref):
    total = x_ref[0]
    for k in range(1, x_ref.shape[0]):
        total = total + x_ref[k]
    total = total * (1.0 / 512)
    for k in range(out_ref.shape[0]):
        out_ref[k] = total[0:32]
    bias_ref[...] = total[32:40].sum(axis=0, keepdims=True)


def small(kernel, out_shape, name, *args):
    return pl.pallas_call(
        kernel,
        out_shape=out_shape,
        compiler_params=params(2),
        cost_estimate=cost(1 << 18, 3 << 20),
        name=name,
    )(*args)


def shapes(*entries):
    return [jax.ShapeDtypeStruct(s, t) for s, t in entries]


def cost(flops, moved):
    return pl.CostEstimate(flops=flops, bytes_accessed=moved, transcendentals=0)


BIG = 2 * 1024 * 1024 * 128


def exchange(x, axes):
    return lax.all_to_all(x, axes, split_axis=0, concat_axis=0, tiled=True)


def gather(x, axes, n):
    return exchange(jnp.broadcast_to(x, (n, *x.shape)), axes)


def other_core(x):
    return lax.ppermute(x, "core", [(0, 1), (1, 0)])


def across(x):
    return lax.ppermute(x, "xh", [(0, 1), (1, 0)])


def up(x, k):
    return lax.ppermute(x, "y", [(i, (i + k) % 4) for i in range(4)])


def along(x, k):
    return lax.ppermute(x, "z", [(i, (i + k) % 8) for i in range(8)])


def next_x(x):
    return lax.ppermute(x, "xl", [(0, 1), (1, 0)])


def in_hbm(x):
    return pltpu.with_memory_space_constraint(x, pltpu.HBM)


def after(event, *arrays):
    return lax.optimization_barrier((*arrays, event))[:-1]


VM = pl.BlockSpec(memory_space=pltpu.VMEM)
SM = pl.BlockSpec(memory_space=pltpu.SMEM)
HB = pl.BlockSpec(memory_space=pltpu.HBM)


def per_device(left, right, weight, bias, cotangent):
    at = where_index()
    cot = in_hbm(cotangent.reshape(T * T, CZ))
    weight_arg = weight
    weight = in_hbm(weight)
    left_own = left.transpose(1, 2, 0).reshape(64, S)
    right_own = right.transpose(1, 2, 0).reshape(64, S)
    left_copies, right_own = pl.pallas_call(
        copies_kernel,
        out_shape=[pltpu.VMEM((PEERS, 64, S), F32), pltpu.VMEM((64, S), F32)],
        compiler_params=params(2),
        name="copies",
    )(in_hbm(left_own), in_hbm(right_own))
    left_all = exchange(left_copies, COL)
    left_all = left_all.reshape(1024, S)
    pair_own = jnp.stack([right_own, across(right_own)])

    near = [pair_own] + [up(pair_own, k) for k in (1, 2, 3)]
    far = [other_core(x) for x in near]

    fhi, flo, l2, rt, keep, send = pl.pallas_call(
        outer_kernel,
        out_shape=[
            pltpu.HBM((1024, 1024), BF16),
            pltpu.HBM((1024, 1024), BF16),
            pltpu.HBM((1024, 256), BF16),
            pltpu.HBM((1024, S), F32),
            pltpu.VMEM((16, 40, CZ), F32),
            pltpu.VMEM((16, 40, CZ), F32),
        ],
        in_specs=[SM] + [VM] * 9 + [HB],
        out_specs=[HB] * 4 + [VM] * 2,
        scratch_shapes=[
            pltpu.VMEM((1024, 1024), BF16),
            pltpu.VMEM((1024, 1024), BF16),
            pltpu.VMEM((1024, 256), BF16),
            pltpu.VMEM((1024, S), F32),
            pltpu.VMEM((1024, 256), BF16),
            pltpu.VMEM((1024, 256), BF16),
            pltpu.VMEM((256, 1024), BF16),
            pltpu.VMEM((1024, CZ), F32),
            pltpu.VMEM((8, CZ), F32),
            pltpu.VMEM((1024, CZ), F32),
            pltpu.SemaphoreType.DMA((5,)),
        ],
        compiler_params=params(OUTER_MIB),
        cost_estimate=cost(6 * BIG, 8 << 20),
        name="outer_and_weight_grad",
    )(at, left_all, *near, *far, cot)

    chunks = small(add_kernel, pltpu.VMEM((16, 40, CZ), F32), "chip_sum", keep, other_core(send))
    chunks, l2 = lax.optimization_barrier((chunks, l2))
    lkeep, lsend, rkeep, rsend = pl.pallas_call(
        factor_kernel,
        out_shape=[pltpu.VMEM((8, 64, S), F32)] * 2 + [pltpu.VMEM((4, 2, 64, S), F32)] * 2,
        in_specs=[SM] + [HB] * 4,
        scratch_shapes=[
            pltpu.VMEM((1024, CZ), F32),
            pltpu.VMEM((1024, CZ), F32),
            pltpu.VMEM((1024, 256), BF16),
            pltpu.VMEM((1024, 128), BF16),
            pltpu.VMEM((1024, 256), BF16),
            pltpu.VMEM((1024, 1024), BF16),
            pltpu.VMEM((1024, 1024), BF16),
            pltpu.VMEM((1024, 256), BF16),
            pltpu.VMEM((1024, S), F32),
            pltpu.VMEM((256, 1024), BF16),
            pltpu.VMEM((1024, S), F32),
            pltpu.VMEM((1024, S), F32),
            pltpu.SemaphoreType.DMA((4,)),
        ],
        compiler_params=params(FACTOR_MIB),
        cost_estimate=cost(6 * BIG, 8 << 20),
        name="factor_grads",
    )(at, weight, cot, in_hbm(l2), in_hbm(rt))

    plane = exchange(chunks, PLANE)
    plane_sum = small(sum_kernel, pltpu.VMEM((8, 40, CZ), F32), "plane_sum", plane)
    lkeep, rkeep = after(plane_sum, lkeep, rkeep)
    (plane_sum,) = after(lsend, plane_sum)
    left_sum, sent = small(
        parts_kernel, [pltpu.VMEM((4, 64, S), F32)] * 2, "left_x", lkeep, next_x(lsend)
    )
    left_sum = left_sum + along(sent, 1)
    chip = rkeep + other_core(rsend)
    total, bias_grad = small(
        total_kernel,
        [pltpu.VMEM((16, 32, CZ), F32), jax.ShapeDtypeStruct((1, CZ), F32)],
        "total",
        exchange(plane_sum, ("z",)),
    )
    (fhi,) = after(sent, fhi)
    pair = pl.pallas_call(
        pair_kernel,
        out_shape=jax.ShapeDtypeStruct((1024, CZ), F32),
        in_specs=[VM, HB, VM, VM],
        scratch_shapes=[
            pltpu.VMEM((1024, 1024), BF16),
            pltpu.VMEM((1024, 256), BF16),
            pltpu.SemaphoreType.DMA,
        ],
        compiler_params=params(PAIR_MIB),
        cost_estimate=cost(3 * BIG, 6 << 20),
        name="pair_out",
    )(fhi, in_hbm(flo), weight_arg, bias.reshape(1, CZ))
    (ready,) = after(pair, total)
    half = exchange(ready, PLANE).reshape(512, CZ)
    half_other = other_core(half)
    core = lax.axis_index("core")
    first = jnp.where(core == 0, half, half_other)
    second = jnp.where(core == 0, half_other, half)
    weight_grad = jnp.concatenate([first, second])

    left_kept, right_kept = after(total, left_sum[:2], chip[0])
    line = right_kept + up(chip[1], 1) + up(chip[2], 2) + up(chip[3], 3)
    left_sum = left_kept + along(left_sum[2:], 2)
    left_sum = left_sum[0] + along(left_sum[1], 4)
    right_sum = line[0] + across(line[1])
    left_grad = left_sum.reshape(2, C, S).transpose(2, 0, 1)
    right_grad = right_sum.reshape(2, C, S).transpose(2, 0, 1)
    return pair.reshape(T, T, CZ), left_grad, right_grad, weight_grad, bias_grad.reshape(CZ)


def solution(mesh):
    fine = Mesh(mesh.devices.reshape(2, 4, 2, 2, 8), ("xh", "y", "core", "xl", "z"))
    in_specs = (P(None, ROW + COL, None), P(None, COL + ROW, None), P(), P(), P(ROW, COL, None))
    out_specs = (P(ROW, COL, None), P(None, ROW + COL, None), P(None, COL + ROW, None), P(), P())
    return jax.shard_map(
        per_device, mesh=fine, in_specs=in_specs, out_specs=out_specs, check_vma=False
    )
```

```python
import jax
import jax.numpy as jnp
from jax import lax
from jax.experimental import pallas as pl
from jax.experimental.pallas import tpu as pltpu
from jax.sharding import Mesh
from jax.sharding import PartitionSpec as P

S = 128
C = 32
CZ = 128
T = 32
PEERS = 16
F32 = jnp.float32
BF16 = jnp.bfloat16
ROW = ("xh", "y", "core")
COL = ("xl", "z")
PLANE = ("xh", "y", "xl")
OUTER_MIB, FACTOR_MIB, PAIR_MIB = 50, 52, 56
ORDER = (0, 4, 2, 6, 1, 5, 3, 7)


def params(mib):
    return pltpu.CompilerParams(vmem_limit_bytes=mib << 20)


def split(x):
    hi = x.astype(BF16)
    return hi, (x - hi.astype(F32)).astype(BF16)


def mm(a, b):
    return lax.dot_general(a, b, (((1,), (0,)), ((), ())), preferred_element_type=F32)


def mm_t(a, b):
    return lax.dot_general(a, b, (((1,), (1,)), ((), ())), preferred_element_type=F32)


def lanes(shape):
    return lax.broadcasted_iota(jnp.int32, shape, 1)


def swap_groups(a):
    lane = lanes(a[0].shape)
    low = lane < 64
    even = (lane & 32) == 0
    b = [None] * 4
    for g in (0, 1):
        turned = pltpu.roll(jnp.where(low, a[g + 2], a[g]), 64, 1)
        b[g] = jnp.where(low, a[g], turned)
        b[g + 2] = jnp.where(low, turned, a[g + 2])
    out = [None] * 4
    for g in (0, 2):
        out[g] = jnp.where(even, b[g], pltpu.roll(b[g + 1], 32, 1))
        out[g + 1] = jnp.where(even, pltpu.roll(b[g], 96, 1), b[g + 1])
    return out


def relayout(x, hi_ref, lo_ref, n):
    for q in range(8):
        for b in range(2):
            rows = [slice(32 * (4 * q + g), 32 * (4 * q + g) + 32) for g in range(4)]
            pieces = [x[r, 128 * b : 128 * b + 128] for r in rows]
            for r, piece in enumerate(swap_groups(pieces)):
                hi, lo = split(piece)
                to = pl.ds(pl.multiple_of((8 * n + 4 * b + r) * 32, 32), 32)
                hi_ref[to, 128 * q : 128 * q + 128] = hi
                lo_ref[to, 128 * q : 128 * q + 128] = lo


def by_second(w_ref, wide, low):
    for d in range(C):
        hi, lo = split(w_ref[pl.ds(d, C, stride=C), :])
        wide[32 * d : 32 * d + 32, 0:128] = hi
        wide[32 * d : 32 * d + 32, 128:256] = hi
        low[32 * d : 32 * d + 32, :] = lo


def where_index():
    return jnp.stack([lax.axis_index(a) for a in ROW + COL]).astype(jnp.int32)


def row_peer(at_ref, k, n, other, sign):
    xh, y, core = at_ref[0], at_ref[1], at_ref[2]
    y = lax.rem(y + (4 + sign * k), 4)
    xh = 1 - xh if n else xh
    core = 1 - core if other else core
    return xh * 8 + y * 2 + core


def outer_kernel(
    at_ref, gl_ref, r0, r1, r2, r3, o0, o1, o2, o3, cot_in,
    fhi_out, flo_out, l2_out, rt_out, keep_ref, send_ref,
    fhi, flo, l2, rt, rboth, wide, ct, wg, bias, cot, sems,
):
    fetched = pltpu.make_async_copy(cot_in, cot, sems.at[4])
    fetched.start()
    for q in range(4):
        rows = pl.ds(256 * q, 256)
        hi, lo = split(gl_ref[rows, :] * (1.0 / S))
        wide[rows, 0:128] = hi
        wide[rows, 128:256] = hi
        l2[rows, 0:128] = hi
        l2[rows, 128:256] = lo
    for other, refs in enumerate(((r0, r1, r2, r3), (o0, o1, o2, o3))):
        for k, ref in enumerate(refs):
            for n in range(2):
                p = row_peer(at_ref, k, n, other, -1)
                for t in range(2):
                    rt[pl.ds(2 * p + t, 32, stride=32), :] = ref[n, 32 * t : 32 * t + 32, :]
    copies = [
        pltpu.make_async_copy(src, dst, sems.at[n])
        for n, (src, dst) in enumerate(((l2, l2_out), (rt, rt_out), (fhi, fhi_out), (flo, flo_out)))
    ]
    copies[0].start()
    copies[1].start()

    for q in range(8):
        at = slice(128 * q, 128 * q + 128)
        hi, lo = split(rt[at, :])
        rboth[at, 0:128] = hi
        rboth[at, 128:256] = lo

    def step(n, carry):
        rows = pl.ds(pl.multiple_of(n * 256, 256), 256)
        x = mm_t(rboth[...], wide[rows, :]) + mm_t(rboth[:, 0:128], l2[rows, 128:256])
        relayout(x, fhi, flo, n)
        return carry

    lax.fori_loop(0, 4, step, 0)
    copies[2].start()
    copies[3].start()
    fetched.wait()
    for q in range(8):
        at = slice(128 * q, 128 * q + 128)
        part = cot[at, :].reshape(16, 8, CZ).sum(axis=0)
        bias[...] = part if q == 0 else bias[...] + part
        chi, clo = split(cot[at, :].T)
        ct[0:128, at] = chi
        ct[128:256, at] = clo

    def wgrad(n, carry):
        at = pl.multiple_of(n * 256, 256)
        both = mm(ct[...], fhi[:, pl.ds(at, 256)])
        out = both[:CZ] + both[CZ:] + mm(ct[0:128, :], flo[:, pl.ds(at, 256)])
        out = out.T
        for k in range(8):
            wg[pl.ds(n * 8 + k, C, stride=C), :] = out[32 * k : 32 * k + 32]
        return carry

    lax.fori_loop(0, 4, wgrad, 0, unroll=True)
    core = at_ref[2]
    for ref, half in ((keep_ref, core), (send_ref, 1 - core)):
        for k in range(16):
            ref[k, 0:32, :] = wg[pl.ds(pl.multiple_of(half * 512 + 32 * k, 32), 32), :]
            ref[k, 32:40, :] = bias[...]
    for copy in copies:
        copy.wait()


def fetch(sources, targets, sems):
    copies = [
        [
            pltpu.make_async_copy(src.at[256 * n : 256 * n + 256], dst.at[256 * n : 256 * n + 256], sems.at[n, m])
            for m, (src, dst) in enumerate(zip(sources, targets, strict=True))
        ]
        for n in range(4)
    ]
    for rows in copies:
        for copy in rows:
            copy.start()

    def arrived(n):
        for copy in copies[n]:
            copy.wait()

    return arrived


def pair_kernel(fhi_in, flo_in, w_in, bias_ref, out_ref, fhi, flo, w, w2, sems):
    fetched = pltpu.make_async_copy(w_in, w, sems.at[4, 0])
    fetched.start()
    arrived = fetch((fhi_in, flo_in), (fhi, flo), sems)
    fetched.wait()
    for d in range(C):
        hi, lo = split(w[pl.ds(d, C, stride=C), :])
        w2[32 * d : 32 * d + 32, 0:128] = hi
        w2[32 * d : 32 * d + 32, 128:256] = lo
    for n in range(2):
        arrived(2 * n)
        arrived(2 * n + 1)
        rows = slice(512 * n, 512 * n + 512)
        both = mm(fhi[rows, :], w2[...])
        out = both[:, :CZ] + both[:, CZ:] + mm(flo[rows, :], w2[:, 0:128])
        out_ref[rows, :] = out + bias_ref[...]


def factor_kernel(
    at_ref, w_in, cot_in, l2_in, rt_in, lkeep_ref, lsend_ref, keep_ref, send_ref,
    w, cot, wide, low, cboth, ghi, glo, l2, rt, r2, rp, lp, sems,
):
    copies = [
        pltpu.make_async_copy(src, dst, sems.at[n])
        for n, (src, dst) in enumerate(((w_in, w), (cot_in, cot), (l2_in, l2), (rt_in, rt)))
    ]
    for copy in copies:
        copy.start()
    copies[0].wait()
    by_second(w, wide, low)
    copies[1].wait()
    for q in range(8):
        at = slice(128 * q, 128 * q + 128)
        hi, lo = split(cot[at, :])
        cboth[at, 0:128] = hi
        cboth[at, 128:256] = lo

    def step(n, carry):
        rows = pl.ds(pl.multiple_of(n * 256, 256), 256)
        g = mm_t(cboth[...], wide[rows, :]) + mm_t(cboth[:, 0:128], low[rows, :])
        relayout(g, ghi, glo, n)
        return carry

    lax.fori_loop(0, 4, step, 0)
    copies[2].wait()
    copies[3].wait()
    for n in range(2):
        rows = slice(512 * n, 512 * n + 512)
        both = mm(ghi[rows, :], l2[...])
        rp[rows, :] = both[:, :S] + both[:, S:] + mm(glo[rows, :], l2[:, 0:128])
    for q in range(8):
        hi, lo = split(rt[128 * q : 128 * q + 128, :].T * (1.0 / S))
        r2[0:128, 128 * q : 128 * q + 128] = hi
        r2[128:256, 128 * q : 128 * q + 128] = lo
    for other, ref in enumerate((keep_ref, send_ref)):
        for k in range(4):
            for n in range(2):
                p = row_peer(at_ref, k, n, other, 1)
                for t in range(2):
                    ref[k, n, 32 * t : 32 * t + 32, :] = rp[pl.ds(2 * p + t, 32, stride=32), :]

    def left(n, carry):
        at = pl.multiple_of(n * 256, 256)
        both = mm(r2[...], ghi[:, pl.ds(at, 256)])
        out = both[:S] + both[S:] + mm(r2[0:128, :], glo[:, pl.ds(at, 256)])
        lp[pl.ds(at, 256), :] = out.T
        return carry

    lax.fori_loop(0, 4, left, 0, unroll=True)
    xl, z = at_ref[3], at_ref[4]
    for ref, x in ((lkeep_ref, xl), (lsend_ref, 1 - xl)):
        for n, k in enumerate(ORDER):
            p = x * 8 + lax.rem(z + k, 8)
            ref[n] = lp[pl.ds(pl.multiple_of(p * 64, 64), 64), :]


def copies_kernel(x_ref, y_ref, copies_ref, y_out):
    y_out[...] = y_ref[...]
    x = x_ref[...]
    for k in range(PEERS):
        copies_ref[k] = x


def parts_kernel(x_ref, y_ref, *outs):
    at = 0
    for out_ref in outs:
        n = out_ref.shape[0]
        out_ref[...] = x_ref[at : at + n] + y_ref[at : at + n]
        at += n


def add_kernel(x_ref, y_ref, out_ref):
    out_ref[...] = x_ref[...] + y_ref[...]


def sum_kernel(x_ref, out_ref):
    total = x_ref[0]
    for k in range(1, x_ref.shape[0]):
        total = total + x_ref[k]
    for k in range(out_ref.shape[0]):
        out_ref[k] = total


def total_kernel(x_ref, out_ref, bias_ref):
    total = x_ref[0]
    for k in range(1, x_ref.shape[0]):
        total = total + x_ref[k]
    total = total * (1.0 / 512)
    for k in range(out_ref.shape[0]):
        out_ref[k] = total[0:32]
    bias_ref[...] = total[32:40].sum(axis=0, keepdims=True)


def small(kernel, out_shape, name, *args):
    return pl.pallas_call(
        kernel,
        out_shape=out_shape,
        compiler_params=params(2),
        cost_estimate=cost(1 << 18, 3 << 20),
        name=name,
    )(*args)


def shapes(*entries):
    return [jax.ShapeDtypeStruct(s, t) for s, t in entries]


def cost(flops, moved):
    return pl.CostEstimate(flops=flops, bytes_accessed=moved, transcendentals=0)


BIG = 2 * 1024 * 1024 * 128


def exchange(x, axes):
    return lax.all_to_all(x, axes, split_axis=0, concat_axis=0, tiled=True)


def gather(x, axes, n):
    return exchange(jnp.broadcast_to(x, (n, *x.shape)), axes)


def other_core(x):
    return lax.ppermute(x, "core", [(0, 1), (1, 0)])


def across(x):
    return lax.ppermute(x, "xh", [(0, 1), (1, 0)])


def up(x, k):
    return lax.ppermute(x, "y", [(i, (i + k) % 4) for i in range(4)])


def along(x, k):
    return lax.ppermute(x, "z", [(i, (i + k) % 8) for i in range(8)])


def next_x(x):
    return lax.ppermute(x, "xl", [(0, 1), (1, 0)])


def in_hbm(x):
    return pltpu.with_memory_space_constraint(x, pltpu.HBM)


def after(event, *arrays):
    return lax.optimization_barrier((*arrays, event))[:-1]


VM = pl.BlockSpec(memory_space=pltpu.VMEM)
SM = pl.BlockSpec(memory_space=pltpu.SMEM)
HB = pl.BlockSpec(memory_space=pltpu.HBM)


def per_device(left, right, weight, bias, cotangent):
    at = where_index()
    cot = in_hbm(cotangent.reshape(T * T, CZ))
    weight = in_hbm(weight)
    left_own = left.transpose(1, 2, 0).reshape(64, S)
    right_own = right.transpose(1, 2, 0).reshape(64, S)
    left_copies, right_own = pl.pallas_call(
        copies_kernel,
        out_shape=[pltpu.VMEM((PEERS, 64, S), F32), pltpu.VMEM((64, S), F32)],
        compiler_params=params(2),
        name="copies",
    )(in_hbm(left_own), in_hbm(right_own))
    left_all = exchange(left_copies, COL)
    left_all = left_all.reshape(1024, S)
    pair_own = jnp.stack([right_own, across(right_own)])

    near = [pair_own] + [up(pair_own, k) for k in (1, 2, 3)]
    far = [other_core(x) for x in near]

    fhi, flo, l2, rt, keep, send = pl.pallas_call(
        outer_kernel,
        out_shape=[
            pltpu.HBM((1024, 1024), BF16),
            pltpu.HBM((1024, 1024), BF16),
            pltpu.HBM((1024, 256), BF16),
            pltpu.HBM((1024, S), F32),
            pltpu.VMEM((16, 40, CZ), F32),
            pltpu.VMEM((16, 40, CZ), F32),
        ],
        in_specs=[SM] + [VM] * 9 + [HB],
        out_specs=[HB] * 4 + [VM] * 2,
        scratch_shapes=[
            pltpu.VMEM((1024, 1024), BF16),
            pltpu.VMEM((1024, 1024), BF16),
            pltpu.VMEM((1024, 256), BF16),
            pltpu.VMEM((1024, S), F32),
            pltpu.VMEM((1024, 256), BF16),
            pltpu.VMEM((1024, 256), BF16),
            pltpu.VMEM((256, 1024), BF16),
            pltpu.VMEM((1024, CZ), F32),
            pltpu.VMEM((8, CZ), F32),
            pltpu.VMEM((1024, CZ), F32),
            pltpu.SemaphoreType.DMA((5,)),
        ],
        compiler_params=params(OUTER_MIB),
        cost_estimate=cost(6 * BIG, 8 << 20),
        name="outer_and_weight_grad",
    )(at, left_all, *near, *far, cot)

    chunks = small(add_kernel, pltpu.VMEM((16, 40, CZ), F32), "chip_sum", keep, other_core(send))
    chunks, l2 = lax.optimization_barrier((chunks, l2))
    lkeep, lsend, rkeep, rsend = pl.pallas_call(
        factor_kernel,
        out_shape=[pltpu.VMEM((8, 64, S), F32)] * 2 + [pltpu.VMEM((4, 2, 64, S), F32)] * 2,
        in_specs=[SM] + [HB] * 4,
        scratch_shapes=[
            pltpu.VMEM((1024, CZ), F32),
            pltpu.VMEM((1024, CZ), F32),
            pltpu.VMEM((1024, 256), BF16),
            pltpu.VMEM((1024, 128), BF16),
            pltpu.VMEM((1024, 256), BF16),
            pltpu.VMEM((1024, 1024), BF16),
            pltpu.VMEM((1024, 1024), BF16),
            pltpu.VMEM((1024, 256), BF16),
            pltpu.VMEM((1024, S), F32),
            pltpu.VMEM((256, 1024), BF16),
            pltpu.VMEM((1024, S), F32),
            pltpu.VMEM((1024, S), F32),
            pltpu.SemaphoreType.DMA((4,)),
        ],
        compiler_params=params(FACTOR_MIB),
        cost_estimate=cost(6 * BIG, 8 << 20),
        name="factor_grads",
    )(at, weight, cot, in_hbm(l2), in_hbm(rt))

    plane = exchange(chunks, PLANE)
    plane_sum = small(sum_kernel, pltpu.VMEM((8, 40, CZ), F32), "plane_sum", plane)
    lkeep, rkeep = after(plane_sum, lkeep, rkeep)
    (plane_sum,) = after(lsend, plane_sum)
    left_sum, sent = small(
        parts_kernel, [pltpu.VMEM((4, 64, S), F32)] * 2, "left_x", lkeep, next_x(lsend)
    )
    left_sum = left_sum + along(sent, 1)
    chip = rkeep + other_core(rsend)
    total, bias_grad = small(
        total_kernel,
        [pltpu.VMEM((16, 32, CZ), F32), jax.ShapeDtypeStruct((1, CZ), F32)],
        "total",
        exchange(plane_sum, ("z",)),
    )
    (fhi,) = after(sent, fhi)
    pair = pl.pallas_call(
        pair_kernel,
        out_shape=jax.ShapeDtypeStruct((1024, CZ), F32),
        in_specs=[HB] * 3 + [VM],
        scratch_shapes=[
            pltpu.VMEM((1024, 1024), BF16),
            pltpu.VMEM((1024, 1024), BF16),
            pltpu.VMEM((1024, CZ), F32),
            pltpu.VMEM((1024, 256), BF16),
            pltpu.SemaphoreType.DMA((5, 2)),
        ],
        compiler_params=params(PAIR_MIB),
        cost_estimate=cost(3 * BIG, 6 << 20),
        name="pair_out",
    )(in_hbm(fhi), in_hbm(flo), weight, bias.reshape(1, CZ))
    (ready,) = after(pair, total)
    half = exchange(ready, PLANE).reshape(512, CZ)
    half_other = other_core(half)
    core = lax.axis_index("core")
    first = jnp.where(core == 0, half, half_other)
    second = jnp.where(core == 0, half_other, half)
    weight_grad = jnp.concatenate([first, second])

    left_kept, right_kept = after(total, left_sum[:2], chip[0])
    line = right_kept + up(chip[1], 1) + up(chip[2], 2) + up(chip[3], 3)
    (sent,) = after(pair, left_sum[2:])
    left_sum = left_kept + along(sent, 2)
    last = left_sum
    left_sum = last[0] + along(last[1], 4)
    (line,) = after(last, line)
    right_sum = line[0] + across(line[1])
    left_grad = left_sum.reshape(2, C, S).transpose(2, 0, 1)
    right_grad = right_sum.reshape(2, C, S).transpose(2, 0, 1)
    return pair.reshape(T, T, CZ), left_grad, right_grad, weight_grad, bias_grad.reshape(CZ)


def solution(mesh):
    fine = Mesh(mesh.devices.reshape(2, 4, 2, 2, 8), ("xh", "y", "core", "xl", "z"))
    in_specs = (P(None, ROW + COL, None), P(None, COL + ROW, None), P(), P(), P(ROW, COL, None))
    out_specs = (P(ROW, COL, None), P(None, ROW + COL, None), P(None, COL + ROW, None), P(), P())
    return jax.shard_map(
        per_device, mesh=fine, in_specs=in_specs, out_specs=out_specs, check_vma=False
    )
```

```python
import jax
import jax.numpy as jnp
from jax import lax
from jax.experimental import pallas as pl
from jax.experimental.pallas import tpu as pltpu
from jax.sharding import Mesh
from jax.sharding import PartitionSpec as P

S = 128
C = 32
CZ = 128
T = 32
PEERS = 16
F32 = jnp.float32
BF16 = jnp.bfloat16
ROW = ("xh", "y", "core")
COL = ("xl", "z")
PLANE = ("xh", "y", "xl")
OUTER_MIB, FACTOR_MIB, PAIR_MIB = 50, 52, 56
ORDER = (0, 4, 2, 6, 1, 5, 3, 7)


def params(mib):
    return pltpu.CompilerParams(vmem_limit_bytes=mib << 20)


def split(x):
    hi = x.astype(BF16)
    return hi, (x - hi.astype(F32)).astype(BF16)


def mm(a, b):
    return lax.dot_general(a, b, (((1,), (0,)), ((), ())), preferred_element_type=F32)


def mm_t(a, b):
    return lax.dot_general(a, b, (((1,), (1,)), ((), ())), preferred_element_type=F32)


def lanes(shape):
    return lax.broadcasted_iota(jnp.int32, shape, 1)


def swap_groups(a):
    lane = lanes(a[0].shape)
    low = lane < 64
    even = (lane & 32) == 0
    b = [None] * 4
    for g in (0, 1):
        turned = pltpu.roll(jnp.where(low, a[g + 2], a[g]), 64, 1)
        b[g] = jnp.where(low, a[g], turned)
        b[g + 2] = jnp.where(low, turned, a[g + 2])
    out = [None] * 4
    for g in (0, 2):
        out[g] = jnp.where(even, b[g], pltpu.roll(b[g + 1], 32, 1))
        out[g + 1] = jnp.where(even, pltpu.roll(b[g], 96, 1), b[g + 1])
    return out


def relayout(x, hi_ref, lo_ref, n):
    for q in range(8):
        for b in range(2):
            rows = [slice(32 * (4 * q + g), 32 * (4 * q + g) + 32) for g in range(4)]
            pieces = [x[r, 128 * b : 128 * b + 128] for r in rows]
            for r, piece in enumerate(swap_groups(pieces)):
                hi, lo = split(piece)
                to = pl.ds(pl.multiple_of((8 * n + 4 * b + r) * 32, 32), 32)
                hi_ref[to, 128 * q : 128 * q + 128] = hi
                lo_ref[to, 128 * q : 128 * q + 128] = lo


def by_second(w_ref, wide, low):
    for d in range(C):
        hi, lo = split(w_ref[pl.ds(d, C, stride=C), :])
        wide[32 * d : 32 * d + 32, 0:128] = hi
        wide[32 * d : 32 * d + 32, 128:256] = hi
        low[32 * d : 32 * d + 32, :] = lo


def where_index():
    return jnp.stack([lax.axis_index(a) for a in ROW + COL]).astype(jnp.int32)


def row_peer(at_ref, k, n, other, sign):
    xh, y, core = at_ref[0], at_ref[1], at_ref[2]
    y = lax.rem(y + (4 + sign * k), 4)
    xh = 1 - xh if n else xh
    core = 1 - core if other else core
    return xh * 8 + y * 2 + core


def outer_kernel(
    at_ref, gl_ref, r0, r1, r2, r3, o0, o1, o2, o3, cot_in,
    fhi_out, flo_out, l2_out, rt_out, keep_ref, send_ref,
    fhi, flo, l2, rt, rboth, wide, ct, wg, bias, cot, sems,
):
    fetched = pltpu.make_async_copy(cot_in, cot, sems.at[4])
    fetched.start()
    for q in range(4):
        rows = pl.ds(256 * q, 256)
        hi, lo = split(gl_ref[rows, :] * (1.0 / S))
        wide[rows, 0:128] = hi
        wide[rows, 128:256] = hi
        l2[rows, 0:128] = hi
        l2[rows, 128:256] = lo
    for other, refs in enumerate(((r0, r1, r2, r3), (o0, o1, o2, o3))):
        for k, ref in enumerate(refs):
            for n in range(2):
                p = row_peer(at_ref, k, n, other, -1)
                for t in range(2):
                    rt[pl.ds(2 * p + t, 32, stride=32), :] = ref[n, 32 * t : 32 * t + 32, :]
    copies = [
        pltpu.make_async_copy(src, dst, sems.at[n])
        for n, (src, dst) in enumerate(((l2, l2_out), (rt, rt_out), (fhi, fhi_out), (flo, flo_out)))
    ]
    copies[0].start()
    copies[1].start()

    for q in range(8):
        at = slice(128 * q, 128 * q + 128)
        hi, lo = split(rt[at, :])
        rboth[at, 0:128] = hi
        rboth[at, 128:256] = lo

    def step(n, carry):
        rows = pl.ds(pl.multiple_of(n * 256, 256), 256)
        x = mm_t(rboth[...], wide[rows, :]) + mm_t(rboth[:, 0:128], l2[rows, 128:256])
        relayout(x, fhi, flo, n)
        return carry

    lax.fori_loop(0, 4, step, 0)
    copies[2].start()
    copies[3].start()
    fetched.wait()
    for q in range(8):
        at = slice(128 * q, 128 * q + 128)
        part = cot[at, :].reshape(16, 8, CZ).sum(axis=0)
        bias[...] = part if q == 0 else bias[...] + part
        chi, clo = split(cot[at, :].T)
        ct[0:128, at] = chi
        ct[128:256, at] = clo

    def wgrad(n, carry):
        at = pl.multiple_of(n * 256, 256)
        both = mm(ct[...], fhi[:, pl.ds(at, 256)])
        out = both[:CZ] + both[CZ:] + mm(ct[0:128, :], flo[:, pl.ds(at, 256)])
        out = out.T
        for k in range(8):
            wg[pl.ds(n * 8 + k, C, stride=C), :] = out[32 * k : 32 * k + 32]
        return carry

    lax.fori_loop(0, 4, wgrad, 0, unroll=True)
    core = at_ref[2]
    for ref, half in ((keep_ref, core), (send_ref, 1 - core)):
        for k in range(16):
            ref[k, 0:32, :] = wg[pl.ds(pl.multiple_of(half * 512 + 32 * k, 32), 32), :]
            ref[k, 32:40, :] = bias[...]
    for copy in copies:
        copy.wait()


def fetch(sources, targets, sems):
    copies = [
        [
            pltpu.make_async_copy(src.at[256 * n : 256 * n + 256], dst.at[256 * n : 256 * n + 256], sems.at[n, m])
            for m, (src, dst) in enumerate(zip(sources, targets, strict=True))
        ]
        for n in range(4)
    ]
    for rows in copies:
        for copy in rows:
            copy.start()

    def arrived(n):
        for copy in copies[n]:
            copy.wait()

    return arrived


def pair_kernel(fhi_in, flo_in, w_in, bias_ref, out_ref, fhi, flo, w, w2, sems):
    fetched = pltpu.make_async_copy(w_in, w, sems.at[4, 0])
    fetched.start()
    arrived = fetch((fhi_in, flo_in), (fhi, flo), sems)
    fetched.wait()
    for d in range(C):
        hi, lo = split(w[pl.ds(d, C, stride=C), :])
        w2[32 * d : 32 * d + 32, 0:128] = hi
        w2[32 * d : 32 * d + 32, 128:256] = lo
    for n in range(2):
        arrived(2 * n)
        arrived(2 * n + 1)
        rows = slice(512 * n, 512 * n + 512)
        both = mm(fhi[rows, :], w2[...])
        out = both[:, :CZ] + both[:, CZ:] + mm(flo[rows, :], w2[:, 0:128])
        out_ref[rows, :] = out + bias_ref[...]


def factor_kernel(
    at_ref, w_in, cot_in, l2_in, rt_in, lkeep_ref, lsend_ref, keep_ref, send_ref,
    w, cot, wide, low, cboth, ghi, glo, l2, rt, r2, rp, lp, sems,
):
    copies = [
        pltpu.make_async_copy(src, dst, sems.at[n])
        for n, (src, dst) in enumerate(((w_in, w), (cot_in, cot), (l2_in, l2), (rt_in, rt)))
    ]
    for copy in copies:
        copy.start()
    copies[0].wait()
    by_second(w, wide, low)
    copies[1].wait()
    for q in range(8):
        at = slice(128 * q, 128 * q + 128)
        hi, lo = split(cot[at, :])
        cboth[at, 0:128] = hi
        cboth[at, 128:256] = lo

    def step(n, carry):
        rows = pl.ds(pl.multiple_of(n * 256, 256), 256)
        g = mm_t(cboth[...], wide[rows, :]) + mm_t(cboth[:, 0:128], low[rows, :])
        relayout(g, ghi, glo, n)
        return carry

    lax.fori_loop(0, 4, step, 0)
    copies[2].wait()
    copies[3].wait()
    for n in range(2):
        rows = slice(512 * n, 512 * n + 512)
        both = mm(ghi[rows, :], l2[...])
        rp[rows, :] = both[:, :S] + both[:, S:] + mm(glo[rows, :], l2[:, 0:128])
    for q in range(8):
        hi, lo = split(rt[128 * q : 128 * q + 128, :].T * (1.0 / S))
        r2[0:128, 128 * q : 128 * q + 128] = hi
        r2[128:256, 128 * q : 128 * q + 128] = lo
    for other, ref in enumerate((keep_ref, send_ref)):
        for k in range(4):
            for n in range(2):
                p = row_peer(at_ref, k, n, other, 1)
                for t in range(2):
                    ref[k, n, 32 * t : 32 * t + 32, :] = rp[pl.ds(2 * p + t, 32, stride=32), :]

    def left(n, carry):
        at = pl.multiple_of(n * 256, 256)
        both = mm(r2[...], ghi[:, pl.ds(at, 256)])
        out = both[:S] + both[S:] + mm(r2[0:128, :], glo[:, pl.ds(at, 256)])
        lp[pl.ds(at, 256), :] = out.T
        return carry

    lax.fori_loop(0, 4, left, 0, unroll=True)
    xl, z = at_ref[3], at_ref[4]
    for ref, x in ((lkeep_ref, xl), (lsend_ref, 1 - xl)):
        for n, k in enumerate(ORDER):
            p = x * 8 + lax.rem(z + k, 8)
            ref[n] = lp[pl.ds(pl.multiple_of(p * 64, 64), 64), :]


def copies_kernel(x_ref, y_ref, copies_ref, y_out):
    y_out[...] = y_ref[...]
    x = x_ref[...]
    for k in range(PEERS):
        copies_ref[k] = x


def parts_kernel(x_ref, y_ref, *outs):
    at = 0
    for out_ref in outs:
        n = out_ref.shape[0]
        out_ref[...] = x_ref[at : at + n] + y_ref[at : at + n]
        at += n


def add_kernel(x_ref, y_ref, out_ref):
    out_ref[...] = x_ref[...] + y_ref[...]


def sum_kernel(x_ref, out_ref):
    total = x_ref[0]
    for k in range(1, x_ref.shape[0]):
        total = total + x_ref[k]
    for k in range(out_ref.shape[0]):
        out_ref[k] = total


def total_kernel(x_ref, out_ref, bias_ref):
    total = x_ref[0]
    for k in range(1, x_ref.shape[0]):
        total = total + x_ref[k]
    total = total * (1.0 / 512)
    for k in range(out_ref.shape[0]):
        out_ref[k] = total[0:32]
    bias_ref[...] = total[32:40].sum(axis=0, keepdims=True)


def final_kernel(at_ref, half_in, other_in, l_ref, l_got, r_ref, r_got, w_out, left_ref, right_ref, sems):
    core = at_ref[2]
    copies = [
        pltpu.make_async_copy(src, w_out.at[pl.ds(pl.multiple_of(half * 512, 512), 512), :], sems.at[n])
        for n, (src, half) in enumerate(((half_in, core), (other_in, 1 - core)))
    ]
    for copy in copies:
        copy.start()
    left_ref[...] = l_ref[0] + l_got[...]
    right_ref[...] = r_ref[0] + r_got[...]
    for copy in copies:
        copy.wait()


def small(kernel, out_shape, name, *args):
    return pl.pallas_call(
        kernel,
        out_shape=out_shape,
        compiler_params=params(2),
        cost_estimate=cost(1 << 18, 3 << 20),
        name=name,
    )(*args)


def shapes(*entries):
    return [jax.ShapeDtypeStruct(s, t) for s, t in entries]


def cost(flops, moved):
    return pl.CostEstimate(flops=flops, bytes_accessed=moved, transcendentals=0)


BIG = 2 * 1024 * 1024 * 128


def exchange(x, axes):
    return lax.all_to_all(x, axes, split_axis=0, concat_axis=0, tiled=True)


def gather(x, axes, n):
    return exchange(jnp.broadcast_to(x, (n, *x.shape)), axes)


def other_core(x):
    return lax.ppermute(x, "core", [(0, 1), (1, 0)])


def across(x):
    return lax.ppermute(x, "xh", [(0, 1), (1, 0)])


def up(x, k):
    return lax.ppermute(x, "y", [(i, (i + k) % 4) for i in range(4)])


def along(x, k):
    return lax.ppermute(x, "z", [(i, (i + k) % 8) for i in range(8)])


def next_x(x):
    return lax.ppermute(x, "xl", [(0, 1), (1, 0)])


def in_hbm(x):
    return pltpu.with_memory_space_constraint(x, pltpu.HBM)


def after(event, *arrays):
    return lax.optimization_barrier((*arrays, event))[:-1]


VM = pl.BlockSpec(memory_space=pltpu.VMEM)
SM = pl.BlockSpec(memory_space=pltpu.SMEM)
HB = pl.BlockSpec(memory_space=pltpu.HBM)


def per_device(left, right, weight, bias, cotangent):
    at = where_index()
    cot = in_hbm(cotangent.reshape(T * T, CZ))
    weight = in_hbm(weight)
    left_own = left.transpose(1, 2, 0).reshape(64, S)
    right_own = right.transpose(1, 2, 0).reshape(64, S)
    left_copies, right_own = pl.pallas_call(
        copies_kernel,
        out_shape=[pltpu.VMEM((PEERS, 64, S), F32), pltpu.VMEM((64, S), F32)],
        compiler_params=params(2),
        name="copies",
    )(in_hbm(left_own), in_hbm(right_own))
    left_all = exchange(left_copies, COL)
    left_all = left_all.reshape(1024, S)
    pair_own = jnp.stack([right_own, across(right_own)])

    near = [pair_own] + [up(pair_own, k) for k in (1, 2, 3)]
    far = [other_core(x) for x in near]

    fhi, flo, l2, rt, keep, send = pl.pallas_call(
        outer_kernel,
        out_shape=[
            pltpu.HBM((1024, 1024), BF16),
            pltpu.HBM((1024, 1024), BF16),
            pltpu.HBM((1024, 256), BF16),
            pltpu.HBM((1024, S), F32),
            pltpu.VMEM((16, 40, CZ), F32),
            pltpu.VMEM((16, 40, CZ), F32),
        ],
        in_specs=[SM] + [VM] * 9 + [HB],
        out_specs=[HB] * 4 + [VM] * 2,
        scratch_shapes=[
            pltpu.VMEM((1024, 1024), BF16),
            pltpu.VMEM((1024, 1024), BF16),
            pltpu.VMEM((1024, 256), BF16),
            pltpu.VMEM((1024, S), F32),
            pltpu.VMEM((1024, 256), BF16),
            pltpu.VMEM((1024, 256), BF16),
            pltpu.VMEM((256, 1024), BF16),
            pltpu.VMEM((1024, CZ), F32),
            pltpu.VMEM((8, CZ), F32),
            pltpu.VMEM((1024, CZ), F32),
            pltpu.SemaphoreType.DMA((5,)),
        ],
        compiler_params=params(OUTER_MIB),
        cost_estimate=cost(6 * BIG, 8 << 20),
        name="outer_and_weight_grad",
    )(at, left_all, *near, *far, cot)

    chunks = small(add_kernel, pltpu.VMEM((16, 40, CZ), F32), "chip_sum", keep, other_core(send))
    chunks, l2 = lax.optimization_barrier((chunks, l2))
    lkeep, lsend, rkeep, rsend = pl.pallas_call(
        factor_kernel,
        out_shape=[pltpu.VMEM((8, 64, S), F32)] * 2 + [pltpu.VMEM((4, 2, 64, S), F32)] * 2,
        in_specs=[SM] + [HB] * 4,
        scratch_shapes=[
            pltpu.VMEM((1024, CZ), F32),
            pltpu.VMEM((1024, CZ), F32),
            pltpu.VMEM((1024, 256), BF16),
            pltpu.VMEM((1024, 128), BF16),
            pltpu.VMEM((1024, 256), BF16),
            pltpu.VMEM((1024, 1024), BF16),
            pltpu.VMEM((1024, 1024), BF16),
            pltpu.VMEM((1024, 256), BF16),
            pltpu.VMEM((1024, S), F32),
            pltpu.VMEM((256, 1024), BF16),
            pltpu.VMEM((1024, S), F32),
            pltpu.VMEM((1024, S), F32),
            pltpu.SemaphoreType.DMA((4,)),
        ],
        compiler_params=params(FACTOR_MIB),
        cost_estimate=cost(6 * BIG, 8 << 20),
        name="factor_grads",
    )(at, weight, cot, in_hbm(l2), in_hbm(rt))

    plane = exchange(chunks, PLANE)
    plane_sum = small(sum_kernel, pltpu.VMEM((8, 40, CZ), F32), "plane_sum", plane)
    lkeep, rkeep = after(plane_sum, lkeep, rkeep)
    (plane_sum,) = after(lsend, plane_sum)
    left_sum, sent = small(
        parts_kernel, [pltpu.VMEM((4, 64, S), F32)] * 2, "left_x", lkeep, next_x(lsend)
    )
    left_sum = left_sum + along(sent, 1)
    chip = rkeep + other_core(rsend)
    total, bias_grad = small(
        total_kernel,
        [pltpu.VMEM((16, 32, CZ), F32), jax.ShapeDtypeStruct((1, CZ), F32)],
        "total",
        exchange(plane_sum, ("z",)),
    )
    (fhi,) = after(sent, fhi)
    pair = pl.pallas_call(
        pair_kernel,
        out_shape=jax.ShapeDtypeStruct((1024, CZ), F32),
        in_specs=[HB] * 3 + [VM],
        scratch_shapes=[
            pltpu.VMEM((1024, 1024), BF16),
            pltpu.VMEM((1024, 1024), BF16),
            pltpu.VMEM((1024, CZ), F32),
            pltpu.VMEM((1024, 256), BF16),
            pltpu.SemaphoreType.DMA((5, 2)),
        ],
        compiler_params=params(PAIR_MIB),
        cost_estimate=cost(3 * BIG, 6 << 20),
        name="pair_out",
    )(in_hbm(fhi), in_hbm(flo), weight, bias.reshape(1, CZ))
    (ready,) = after(pair, total)
    half = exchange(ready, PLANE).reshape(512, CZ)
    half_other = other_core(half)

    left_kept, right_kept = after(total, left_sum[:2], chip[0])
    line = right_kept + up(chip[1], 1) + up(chip[2], 2) + up(chip[3], 3)
    (sent,) = after(pair, left_sum[2:])
    left_sum = left_kept + along(sent, 2)
    last = left_sum
    (line,) = after(last, line)
    weight_grad, left_sum, right_sum = pl.pallas_call(
        final_kernel,
        out_shape=shapes(((1024, CZ), F32), ((64, S), F32), ((64, S), F32)),
        in_specs=[SM] + [pl.BlockSpec(memory_space=pl.ANY)] * 2 + [VM] * 4,
        out_specs=[HB, VM, VM],
        scratch_shapes=[pltpu.SemaphoreType.DMA((2,))],
        compiler_params=params(2),
        name="final",
    )(at, half, half_other, last, along(last[1], 4), line, across(line[1]))
    left_grad = left_sum.reshape(2, C, S).transpose(2, 0, 1)
    right_grad = right_sum.reshape(2, C, S).transpose(2, 0, 1)
    return pair.reshape(T, T, CZ), left_grad, right_grad, weight_grad, bias_grad.reshape(CZ)


def solution(mesh):
    fine = Mesh(mesh.devices.reshape(2, 4, 2, 2, 8), ("xh", "y", "core", "xl", "z"))
    in_specs = (P(None, ROW + COL, None), P(None, COL + ROW, None), P(), P(), P(ROW, COL, None))
    out_specs = (P(ROW, COL, None), P(None, ROW + COL, None), P(None, COL + ROW, None), P(), P())
    return jax.shard_map(
        per_device, mesh=fine, in_specs=in_specs, out_specs=out_specs, check_vma=False
    )
```

```python
import jax
import jax.numpy as jnp
from jax import lax
from jax.experimental import pallas as pl
from jax.experimental.pallas import tpu as pltpu
from jax.sharding import Mesh
from jax.sharding import PartitionSpec as P

S = 128
C = 32
CZ = 128
T = 32
PEERS = 16
F32 = jnp.float32
BF16 = jnp.bfloat16
ROW = ("xh", "y", "core")
COL = ("xl", "z")
PLANE = ("xh", "y", "xl")
OUTER_MIB, FACTOR_MIB, PAIR_MIB = 50, 52, 56
ORDER = (0, 4, 2, 6, 1, 5, 3, 7)


def params(mib):
    return pltpu.CompilerParams(vmem_limit_bytes=mib << 20)


def split(x):
    hi = x.astype(BF16)
    return hi, (x - hi.astype(F32)).astype(BF16)


def mm(a, b):
    return lax.dot_general(a, b, (((1,), (0,)), ((), ())), preferred_element_type=F32)


def mm_t(a, b):
    return lax.dot_general(a, b, (((1,), (1,)), ((), ())), preferred_element_type=F32)


def lanes(shape):
    return lax.broadcasted_iota(jnp.int32, shape, 1)


def swap_groups(a):
    lane = lanes(a[0].shape)
    low = lane < 64
    even = (lane & 32) == 0
    b = [None] * 4
    for g in (0, 1):
        turned = pltpu.roll(jnp.where(low, a[g + 2], a[g]), 64, 1)
        b[g] = jnp.where(low, a[g], turned)
        b[g + 2] = jnp.where(low, turned, a[g + 2])
    out = [None] * 4
    for g in (0, 2):
        out[g] = jnp.where(even, b[g], pltpu.roll(b[g + 1], 32, 1))
        out[g + 1] = jnp.where(even, pltpu.roll(b[g], 96, 1), b[g + 1])
    return out


def relayout(x, hi_ref, lo_ref, n):
    for q in range(8):
        for b in range(2):
            rows = [slice(32 * (4 * q + g), 32 * (4 * q + g) + 32) for g in range(4)]
            pieces = [x[r, 128 * b : 128 * b + 128] for r in rows]
            for r, piece in enumerate(swap_groups(pieces)):
                hi, lo = split(piece)
                to = pl.ds(pl.multiple_of((8 * n + 4 * b + r) * 32, 32), 32)
                hi_ref[to, 128 * q : 128 * q + 128] = hi
                lo_ref[to, 128 * q : 128 * q + 128] = lo


def by_second(w_ref, wide, low):
    for d in range(C):
        hi, lo = split(w_ref[pl.ds(d, C, stride=C), :])
        wide[32 * d : 32 * d + 32, 0:128] = hi
        wide[32 * d : 32 * d + 32, 128:256] = hi
        low[32 * d : 32 * d + 32, :] = lo


def where_index():
    return jnp.stack([lax.axis_index(a) for a in ROW + COL]).astype(jnp.int32)


def row_peer(at_ref, k, n, other, sign):
    xh, y, core = at_ref[0], at_ref[1], at_ref[2]
    y = lax.rem(y + (4 + sign * k), 4)
    xh = 1 - xh if n else xh
    core = 1 - core if other else core
    return xh * 8 + y * 2 + core


def outer_kernel(
    at_ref, gl_ref, r0, r1, r2, r3, o0, o1, o2, o3, cot_in,
    fhi_out, flo_out, l2_out, rt_out, keep_ref, send_ref,
    fhi, flo, l2, rt, rboth, wide, ct, wg, bias, cot, sems,
):
    fetched = pltpu.make_async_copy(cot_in, cot, sems.at[4])
    fetched.start()
    for q in range(4):
        rows = pl.ds(256 * q, 256)
        hi, lo = split(gl_ref[rows, :] * (1.0 / S))
        wide[rows, 0:128] = hi
        wide[rows, 128:256] = hi
        l2[rows, 0:128] = hi
        l2[rows, 128:256] = lo
    for other, refs in enumerate(((r0, r1, r2, r3), (o0, o1, o2, o3))):
        for k, ref in enumerate(refs):
            for n in range(2):
                p = row_peer(at_ref, k, n, other, -1)
                for t in range(2):
                    rt[pl.ds(2 * p + t, 32, stride=32), :] = ref[n, 32 * t : 32 * t + 32, :]
    copies = [
        pltpu.make_async_copy(src, dst, sems.at[n])
        for n, (src, dst) in enumerate(((l2, l2_out), (rt, rt_out), (fhi, fhi_out), (flo, flo_out)))
    ]
    copies[0].start()
    copies[1].start()

    for q in range(8):
        at = slice(128 * q, 128 * q + 128)
        hi, lo = split(rt[at, :])
        rboth[at, 0:128] = hi
        rboth[at, 128:256] = lo

    def step(n, carry):
        rows = pl.ds(pl.multiple_of(n * 256, 256), 256)
        x = mm_t(rboth[...], wide[rows, :]) + mm_t(rboth[:, 0:128], l2[rows, 128:256])
        relayout(x, fhi, flo, n)
        return carry

    lax.fori_loop(0, 4, step, 0)
    copies[2].start()
    copies[3].start()
    fetched.wait()
    for q in range(8):
        at = slice(128 * q, 128 * q + 128)
        part = cot[at, :].reshape(16, 8, CZ).sum(axis=0)
        bias[...] = part if q == 0 else bias[...] + part
        chi, clo = split(cot[at, :].T)
        ct[0:128, at] = chi
        ct[128:256, at] = clo

    def wgrad(n, carry):
        at = pl.multiple_of(n * 256, 256)
        both = mm(ct[...], fhi[:, pl.ds(at, 256)])
        out = both[:CZ] + both[CZ:] + mm(ct[0:128, :], flo[:, pl.ds(at, 256)])
        out = out.T
        for k in range(8):
            wg[pl.ds(n * 8 + k, C, stride=C), :] = out[32 * k : 32 * k + 32]
        return carry

    lax.fori_loop(0, 4, wgrad, 0, unroll=True)
    core = at_ref[2]
    for ref, half in ((keep_ref, core), (send_ref, 1 - core)):
        for k in range(16):
            ref[k, 0:32, :] = wg[pl.ds(pl.multiple_of(half * 512 + 32 * k, 32), 32), :]
            ref[k, 32:40, :] = bias[...]
    for copy in copies:
        copy.wait()


def fetch(sources, targets, sems):
    copies = [
        [
            pltpu.make_async_copy(src.at[256 * n : 256 * n + 256], dst.at[256 * n : 256 * n + 256], sems.at[n, m])
            for m, (src, dst) in enumerate(zip(sources, targets, strict=True))
        ]
        for n in range(4)
    ]
    for rows in copies:
        for copy in rows:
            copy.start()

    def arrived(n):
        for copy in copies[n]:
            copy.wait()

    return arrived


def pair_kernel(fhi_in, flo_in, w_in, bias_ref, out_ref, fhi, flo, w, w2, sems):
    fetched = pltpu.make_async_copy(w_in, w, sems.at[4, 0])
    fetched.start()
    arrived = fetch((fhi_in, flo_in), (fhi, flo), sems)
    fetched.wait()
    for d in range(C):
        hi, lo = split(w[pl.ds(d, C, stride=C), :])
        w2[32 * d : 32 * d + 32, 0:128] = hi
        w2[32 * d : 32 * d + 32, 128:256] = lo
    for n in range(2):
        arrived(2 * n)
        arrived(2 * n + 1)
        rows = slice(512 * n, 512 * n + 512)
        both = mm(fhi[rows, :], w2[...])
        out = both[:, :CZ] + both[:, CZ:] + mm(flo[rows, :], w2[:, 0:128])
        out_ref[rows, :] = out + bias_ref[...]


def factor_kernel(
    at_ref, w_in, cot_in, l2_in, rt_in, lkeep_ref, lsend_ref, keep_ref, send_ref,
    w, cot, wide, low, cboth, ghi, glo, l2, rt, r2, rp, lp, sems,
):
    copies = [
        pltpu.make_async_copy(src, dst, sems.at[n])
        for n, (src, dst) in enumerate(((w_in, w), (cot_in, cot), (l2_in, l2), (rt_in, rt)))
    ]
    for copy in copies:
        copy.start()
    copies[0].wait()
    by_second(w, wide, low)
    copies[1].wait()
    for q in range(8):
        at = slice(128 * q, 128 * q + 128)
        hi, lo = split(cot[at, :])
        cboth[at, 0:128] = hi
        cboth[at, 128:256] = lo

    def step(n, carry):
        rows = pl.ds(pl.multiple_of(n * 256, 256), 256)
        g = mm_t(cboth[...], wide[rows, :]) + mm_t(cboth[:, 0:128], low[rows, :])
        relayout(g, ghi, glo, n)
        return carry

    lax.fori_loop(0, 4, step, 0)
    copies[2].wait()
    copies[3].wait()
    for n in range(2):
        rows = slice(512 * n, 512 * n + 512)
        both = mm(ghi[rows, :], l2[...])
        rp[rows, :] = both[:, :S] + both[:, S:] + mm(glo[rows, :], l2[:, 0:128])
    for q in range(8):
        hi, lo = split(rt[128 * q : 128 * q + 128, :].T * (1.0 / S))
        r2[0:128, 128 * q : 128 * q + 128] = hi
        r2[128:256, 128 * q : 128 * q + 128] = lo
    for other, ref in enumerate((keep_ref, send_ref)):
        for k in range(4):
            for n in range(2):
                p = row_peer(at_ref, k, n, other, 1)
                for t in range(2):
                    ref[k, n, 32 * t : 32 * t + 32, :] = rp[pl.ds(2 * p + t, 32, stride=32), :]

    def left(n, carry):
        at = pl.multiple_of(n * 256, 256)
        both = mm(r2[...], ghi[:, pl.ds(at, 256)])
        out = both[:S] + both[S:] + mm(r2[0:128, :], glo[:, pl.ds(at, 256)])
        lp[pl.ds(at, 256), :] = out.T
        return carry

    lax.fori_loop(0, 4, left, 0, unroll=True)
    xl, z = at_ref[3], at_ref[4]
    for ref, x in ((lkeep_ref, xl), (lsend_ref, 1 - xl)):
        for n, k in enumerate(ORDER):
            p = x * 8 + lax.rem(z + k, 8)
            ref[n] = lp[pl.ds(pl.multiple_of(p * 64, 64), 64), :]


def copies_kernel(x_ref, y_ref, copies_out, y_out, sems):
    copies = [pltpu.make_async_copy(x_ref, copies_out.at[k], sems.at[k]) for k in range(PEERS)]
    for copy in copies:
        copy.start()
    y_out[...] = y_ref[...]
    for copy in copies:
        copy.wait()


def parts_kernel(x_ref, y_ref, *outs):
    at = 0
    for out_ref in outs:
        n = out_ref.shape[0]
        out_ref[...] = x_ref[at : at + n] + y_ref[at : at + n]
        at += n


def add_kernel(x_ref, y_ref, out_ref):
    out_ref[...] = x_ref[...] + y_ref[...]


def sum_kernel(x_ref, out_ref):
    total = x_ref[0]
    for k in range(1, x_ref.shape[0]):
        total = total + x_ref[k]
    for k in range(out_ref.shape[0]):
        out_ref[k] = total


def total_kernel(x_ref, out_ref, bias_ref):
    total = x_ref[0]
    for k in range(1, x_ref.shape[0]):
        total = total + x_ref[k]
    total = total * (1.0 / 512)
    for k in range(out_ref.shape[0]):
        out_ref[k] = total[0:32]
    bias_ref[...] = total[32:40].sum(axis=0, keepdims=True)


def small(kernel, out_shape, name, *args):
    return pl.pallas_call(
        kernel,
        out_shape=out_shape,
        compiler_params=params(2),
        cost_estimate=cost(1 << 18, 3 << 20),
        name=name,
    )(*args)


def shapes(*entries):
    return [jax.ShapeDtypeStruct(s, t) for s, t in entries]


def cost(flops, moved):
    return pl.CostEstimate(flops=flops, bytes_accessed=moved, transcendentals=0)


BIG = 2 * 1024 * 1024 * 128


def exchange(x, axes):
    return lax.all_to_all(x, axes, split_axis=0, concat_axis=0, tiled=True)


def gather(x, axes, n):
    return exchange(jnp.broadcast_to(x, (n, *x.shape)), axes)


def other_core(x):
    return lax.ppermute(x, "core", [(0, 1), (1, 0)])


def across(x):
    return lax.ppermute(x, "xh", [(0, 1), (1, 0)])


def up(x, k):
    return lax.ppermute(x, "y", [(i, (i + k) % 4) for i in range(4)])


def along(x, k):
    return lax.ppermute(x, "z", [(i, (i + k) % 8) for i in range(8)])


def next_x(x):
    return lax.ppermute(x, "xl", [(0, 1), (1, 0)])


def in_hbm(x):
    return pltpu.with_memory_space_constraint(x, pltpu.HBM)


def after(event, *arrays):
    return lax.optimization_barrier((*arrays, event))[:-1]


VM = pl.BlockSpec(memory_space=pltpu.VMEM)
SM = pl.BlockSpec(memory_space=pltpu.SMEM)
HB = pl.BlockSpec(memory_space=pltpu.HBM)


def per_device(left, right, weight, bias, cotangent):
    at = where_index()
    cot = in_hbm(cotangent.reshape(T * T, CZ))
    weight = in_hbm(weight)
    left_own = left.transpose(1, 2, 0).reshape(64, S)
    right_own = right.transpose(1, 2, 0).reshape(64, S)
    left_copies, right_own = pl.pallas_call(
        copies_kernel,
        out_shape=[pltpu.HBM((PEERS, 64, S), F32), pltpu.VMEM((64, S), F32)],
        out_specs=[HB, VM],
        scratch_shapes=[pltpu.SemaphoreType.DMA((PEERS,))],
        compiler_params=params(2),
        name="copies",
    )(in_hbm(left_own), in_hbm(right_own))
    left_all = exchange(left_copies, COL)
    left_all = left_all.reshape(1024, S)
    pair_own = jnp.stack([right_own, across(right_own)])

    near = [pair_own] + [up(pair_own, k) for k in (1, 2, 3)]
    far = [other_core(x) for x in near]

    fhi, flo, l2, rt, keep, send = pl.pallas_call(
        outer_kernel,
        out_shape=[
            pltpu.HBM((1024, 1024), BF16),
            pltpu.HBM((1024, 1024), BF16),
            pltpu.HBM((1024, 256), BF16),
            pltpu.HBM((1024, S), F32),
            pltpu.VMEM((16, 40, CZ), F32),
            pltpu.VMEM((16, 40, CZ), F32),
        ],
        in_specs=[SM] + [VM] * 9 + [HB],
        out_specs=[HB] * 4 + [VM] * 2,
        scratch_shapes=[
            pltpu.VMEM((1024, 1024), BF16),
            pltpu.VMEM((1024, 1024), BF16),
            pltpu.VMEM((1024, 256), BF16),
            pltpu.VMEM((1024, S), F32),
            pltpu.VMEM((1024, 256), BF16),
            pltpu.VMEM((1024, 256), BF16),
            pltpu.VMEM((256, 1024), BF16),
            pltpu.VMEM((1024, CZ), F32),
            pltpu.VMEM((8, CZ), F32),
            pltpu.VMEM((1024, CZ), F32),
            pltpu.SemaphoreType.DMA((5,)),
        ],
        compiler_params=params(OUTER_MIB),
        cost_estimate=cost(6 * BIG, 8 << 20),
        name="outer_and_weight_grad",
    )(at, left_all, *near, *far, cot)

    chunks = small(add_kernel, pltpu.VMEM((16, 40, CZ), F32), "chip_sum", keep, other_core(send))
    chunks, l2 = lax.optimization_barrier((chunks, l2))
    lkeep, lsend, rkeep, rsend = pl.pallas_call(
        factor_kernel,
        out_shape=[pltpu.VMEM((8, 64, S), F32)] * 2 + [pltpu.VMEM((4, 2, 64, S), F32)] * 2,
        in_specs=[SM] + [HB] * 4,
        scratch_shapes=[
            pltpu.VMEM((1024, CZ), F32),
            pltpu.VMEM((1024, CZ), F32),
            pltpu.VMEM((1024, 256), BF16),
            pltpu.VMEM((1024, 128), BF16),
            pltpu.VMEM((1024, 256), BF16),
            pltpu.VMEM((1024, 1024), BF16),
            pltpu.VMEM((1024, 1024), BF16),
            pltpu.VMEM((1024, 256), BF16),
            pltpu.VMEM((1024, S), F32),
            pltpu.VMEM((256, 1024), BF16),
            pltpu.VMEM((1024, S), F32),
            pltpu.VMEM((1024, S), F32),
            pltpu.SemaphoreType.DMA((4,)),
        ],
        compiler_params=params(FACTOR_MIB),
        cost_estimate=cost(6 * BIG, 8 << 20),
        name="factor_grads",
    )(at, weight, cot, in_hbm(l2), in_hbm(rt))

    plane = exchange(chunks, PLANE)
    plane_sum = small(sum_kernel, pltpu.VMEM((8, 40, CZ), F32), "plane_sum", plane)
    lkeep, rkeep = after(plane_sum, lkeep, rkeep)
    (plane_sum,) = after(lsend, plane_sum)
    left_sum, sent = small(
        parts_kernel, [pltpu.VMEM((4, 64, S), F32)] * 2, "left_x", lkeep, next_x(lsend)
    )
    left_sum = left_sum + along(sent, 1)
    chip = rkeep + other_core(rsend)
    total, bias_grad = small(
        total_kernel,
        [pltpu.VMEM((16, 32, CZ), F32), jax.ShapeDtypeStruct((1, CZ), F32)],
        "total",
        exchange(plane_sum, ("z",)),
    )
    (fhi,) = after(sent, fhi)
    pair = pl.pallas_call(
        pair_kernel,
        out_shape=jax.ShapeDtypeStruct((1024, CZ), F32),
        in_specs=[HB] * 3 + [VM],
        scratch_shapes=[
            pltpu.VMEM((1024, 1024), BF16),
            pltpu.VMEM((1024, 1024), BF16),
            pltpu.VMEM((1024, CZ), F32),
            pltpu.VMEM((1024, 256), BF16),
            pltpu.SemaphoreType.DMA((5, 2)),
        ],
        compiler_params=params(PAIR_MIB),
        cost_estimate=cost(3 * BIG, 6 << 20),
        name="pair_out",
    )(in_hbm(fhi), in_hbm(flo), weight, bias.reshape(1, CZ))
    (ready,) = after(pair, total)
    half = exchange(ready, PLANE).reshape(512, CZ)
    half_other = other_core(half)
    core = lax.axis_index("core")
    first = jnp.where(core == 0, half, half_other)
    second = jnp.where(core == 0, half_other, half)
    weight_grad = jnp.concatenate([first, second])

    left_kept, right_kept = after(total, left_sum[:2], chip[0])
    line = right_kept + up(chip[1], 1) + up(chip[2], 2) + up(chip[3], 3)
    (sent,) = after(pair, left_sum[2:])
    left_sum = left_kept + along(sent, 2)
    last = left_sum
    left_sum = last[0] + along(last[1], 4)
    (line,) = after(last, line)
    right_sum = line[0] + across(line[1])
    left_grad = left_sum.reshape(2, C, S).transpose(2, 0, 1)
    right_grad = right_sum.reshape(2, C, S).transpose(2, 0, 1)
    return pair.reshape(T, T, CZ), left_grad, right_grad, weight_grad, bias_grad.reshape(CZ)


def solution(mesh):
    fine = Mesh(mesh.devices.reshape(2, 4, 2, 2, 8), ("xh", "y", "core", "xl", "z"))
    in_specs = (P(None, ROW + COL, None), P(None, COL + ROW, None), P(), P(), P(ROW, COL, None))
    out_specs = (P(ROW, COL, None), P(None, ROW + COL, None), P(None, COL + ROW, None), P(), P())
    return jax.shard_map(
        per_device, mesh=fine, in_specs=in_specs, out_specs=out_specs, check_vma=False
    )
```

```python
import jax
import jax.numpy as jnp
from jax import lax
from jax.experimental import pallas as pl
from jax.experimental.pallas import tpu as pltpu
from jax.sharding import Mesh
from jax.sharding import PartitionSpec as P

S = 128
C = 32
CZ = 128
T = 32
PEERS = 16
F32 = jnp.float32
BF16 = jnp.bfloat16
ROW = ("xh", "y", "core")
COL = ("xl", "z")
PLANE = ("xh", "y", "xl")
OUTER_MIB, FACTOR_MIB, PAIR_MIB = 50, 52, 56
ORDER = (0, 4, 2, 6, 1, 5, 3, 7)


def params(mib):
    return pltpu.CompilerParams(vmem_limit_bytes=mib << 20)


def split(x):
    hi = x.astype(BF16)
    return hi, (x - hi.astype(F32)).astype(BF16)


def mm(a, b):
    return lax.dot_general(a, b, (((1,), (0,)), ((), ())), preferred_element_type=F32)


def mm_t(a, b):
    return lax.dot_general(a, b, (((1,), (1,)), ((), ())), preferred_element_type=F32)


def lanes(shape):
    return lax.broadcasted_iota(jnp.int32, shape, 1)


def swap_groups(a):
    lane = lanes(a[0].shape)
    low = lane < 64
    even = (lane & 32) == 0
    b = [None] * 4
    for g in (0, 1):
        turned = pltpu.roll(jnp.where(low, a[g + 2], a[g]), 64, 1)
        b[g] = jnp.where(low, a[g], turned)
        b[g + 2] = jnp.where(low, turned, a[g + 2])
    out = [None] * 4
    for g in (0, 2):
        out[g] = jnp.where(even, b[g], pltpu.roll(b[g + 1], 32, 1))
        out[g + 1] = jnp.where(even, pltpu.roll(b[g], 96, 1), b[g + 1])
    return out


def relayout(x, hi_ref, lo_ref, n):
    for q in range(8):
        for b in range(2):
            rows = [slice(32 * (4 * q + g), 32 * (4 * q + g) + 32) for g in range(4)]
            pieces = [x[r, 128 * b : 128 * b + 128] for r in rows]
            for r, piece in enumerate(swap_groups(pieces)):
                hi, lo = split(piece)
                to = pl.ds(pl.multiple_of((8 * n + 4 * b + r) * 32, 32), 32)
                hi_ref[to, 128 * q : 128 * q + 128] = hi
                lo_ref[to, 128 * q : 128 * q + 128] = lo


def by_second(w_ref, wide, low):
    for d in range(C):
        hi, lo = split(w_ref[pl.ds(d, C, stride=C), :])
        wide[32 * d : 32 * d + 32, 0:128] = hi
        wide[32 * d : 32 * d + 32, 128:256] = hi
        low[32 * d : 32 * d + 32, :] = lo


def where_index():
    return jnp.stack([lax.axis_index(a) for a in ROW + COL]).astype(jnp.int32)


def row_peer(at_ref, k, n, other, sign):
    xh, y, core = at_ref[0], at_ref[1], at_ref[2]
    y = lax.rem(y + (4 + sign * k), 4)
    xh = 1 - xh if n else xh
    core = 1 - core if other else core
    return xh * 8 + y * 2 + core


def outer_kernel(
    at_ref, gl_ref, r0, r1, r2, r3, o0, o1, o2, o3, cot_in,
    fhi_out, flo_out, l2_out, rt_out, keep_ref, send_ref,
    fhi, flo, l2, rt, rboth, wide, ct, wg, bias, cot, sems,
):
    fetched = pltpu.make_async_copy(cot_in, cot, sems.at[4])
    fetched.start()
    for q in range(4):
        rows = pl.ds(256 * q, 256)
        hi, lo = split(gl_ref[rows, :] * (1.0 / S))
        wide[rows, 0:128] = hi
        wide[rows, 128:256] = hi
        l2[rows, 0:128] = hi
        l2[rows, 128:256] = lo
    for other, refs in enumerate(((r0, r1, r2, r3), (o0, o1, o2, o3))):
        for k, ref in enumerate(refs):
            for n in range(2):
                p = row_peer(at_ref, k, n, other, -1)
                for t in range(2):
                    rt[pl.ds(2 * p + t, 32, stride=32), :] = ref[n, 32 * t : 32 * t + 32, :]
    copies = [
        pltpu.make_async_copy(src, dst, sems.at[n])
        for n, (src, dst) in enumerate(((l2, l2_out), (rt, rt_out), (fhi, fhi_out), (flo, flo_out)))
    ]
    copies[0].start()
    copies[1].start()

    for q in range(8):
        at = slice(128 * q, 128 * q + 128)
        hi, lo = split(rt[at, :])
        rboth[at, 0:128] = hi
        rboth[at, 128:256] = lo

    def step(n, carry):
        rows = pl.ds(pl.multiple_of(n * 256, 256), 256)
        x = mm_t(rboth[...], wide[rows, :]) + mm_t(rboth[:, 0:128], l2[rows, 128:256])
        relayout(x, fhi, flo, n)
        return carry

    lax.fori_loop(0, 4, step, 0)
    copies[2].start()
    copies[3].start()
    fetched.wait()
    for q in range(8):
        at = slice(128 * q, 128 * q + 128)
        part = cot[at, :].reshape(16, 8, CZ).sum(axis=0)
        bias[...] = part if q == 0 else bias[...] + part
        chi, clo = split(cot[at, :].T)
        ct[0:128, at] = chi
        ct[128:256, at] = clo

    def wgrad(n, carry):
        at = pl.multiple_of(n * 256, 256)
        both = mm(ct[...], fhi[:, pl.ds(at, 256)])
        out = both[:CZ] + both[CZ:] + mm(ct[0:128, :], flo[:, pl.ds(at, 256)])
        out = out.T
        for k in range(8):
            wg[pl.ds(n * 8 + k, C, stride=C), :] = out[32 * k : 32 * k + 32]
        return carry

    lax.fori_loop(0, 4, wgrad, 0, unroll=True)
    core = at_ref[2]
    for ref, half in ((keep_ref, core), (send_ref, 1 - core)):
        for k in range(16):
            ref[k, 0:32, :] = wg[pl.ds(pl.multiple_of(half * 512 + 32 * k, 32), 32), :]
            ref[k, 32:40, :] = bias[...]
    for copy in copies:
        copy.wait()


def fetch(sources, targets, sems):
    copies = [
        [
            pltpu.make_async_copy(src.at[256 * n : 256 * n + 256], dst.at[256 * n : 256 * n + 256], sems.at[n, m])
            for m, (src, dst) in enumerate(zip(sources, targets, strict=True))
        ]
        for n in range(4)
    ]
    for rows in copies:
        for copy in rows:
            copy.start()

    def arrived(n):
        for copy in copies[n]:
            copy.wait()

    return arrived


def pair_kernel(fhi_in, flo_in, w_in, bias_ref, out_ref, fhi, flo, w, w2, sems):
    fetched = pltpu.make_async_copy(w_in, w, sems.at[4, 0])
    fetched.start()
    arrived = fetch((fhi_in, flo_in), (fhi, flo), sems)
    fetched.wait()
    for d in range(C):
        hi, lo = split(w[pl.ds(d, C, stride=C), :])
        w2[32 * d : 32 * d + 32, 0:128] = hi
        w2[32 * d : 32 * d + 32, 128:256] = lo
    for n in range(2):
        arrived(2 * n)
        arrived(2 * n + 1)
        rows = slice(512 * n, 512 * n + 512)
        both = mm(fhi[rows, :], w2[...])
        out = both[:, :CZ] + both[:, CZ:] + mm(flo[rows, :], w2[:, 0:128])
        out_ref[rows, :] = out + bias_ref[...]


def factor_kernel(
    at_ref, w_in, cot_in, l2_in, rt_in, lkeep_ref, lsend_ref, keep_ref, send_ref,
    w, cot, wide, low, cboth, ghi, glo, l2, rt, r2, rp, lp, sems,
):
    copies = [
        pltpu.make_async_copy(src, dst, sems.at[n])
        for n, (src, dst) in enumerate(((w_in, w), (cot_in, cot), (l2_in, l2), (rt_in, rt)))
    ]
    for copy in copies:
        copy.start()
    copies[0].wait()
    by_second(w, wide, low)
    copies[1].wait()
    for q in range(8):
        at = slice(128 * q, 128 * q + 128)
        hi, lo = split(cot[at, :])
        cboth[at, 0:128] = hi
        cboth[at, 128:256] = lo

    def step(n, carry):
        rows = pl.ds(pl.multiple_of(n * 256, 256), 256)
        g = mm_t(cboth[...], wide[rows, :]) + mm_t(cboth[:, 0:128], low[rows, :])
        relayout(g, ghi, glo, n)
        return carry

    lax.fori_loop(0, 4, step, 0)
    copies[2].wait()
    copies[3].wait()
    for n in range(2):
        rows = slice(512 * n, 512 * n + 512)
        both = mm(ghi[rows, :], l2[...])
        rp[rows, :] = both[:, :S] + both[:, S:] + mm(glo[rows, :], l2[:, 0:128])
    for q in range(8):
        hi, lo = split(rt[128 * q : 128 * q + 128, :].T * (1.0 / S))
        r2[0:128, 128 * q : 128 * q + 128] = hi
        r2[128:256, 128 * q : 128 * q + 128] = lo
    for other, ref in enumerate((keep_ref, send_ref)):
        for k in range(4):
            for n in range(2):
                p = row_peer(at_ref, k, n, other, 1)
                for t in range(2):
                    ref[k, n, 32 * t : 32 * t + 32, :] = rp[pl.ds(2 * p + t, 32, stride=32), :]

    def left(n, carry):
        at = pl.multiple_of(n * 256, 256)
        both = mm(r2[...], ghi[:, pl.ds(at, 256)])
        out = both[:S] + both[S:] + mm(r2[0:128, :], glo[:, pl.ds(at, 256)])
        lp[pl.ds(at, 256), :] = out.T
        return carry

    lax.fori_loop(0, 4, left, 0, unroll=True)
    xl, z = at_ref[3], at_ref[4]
    for ref, x in ((lkeep_ref, xl), (lsend_ref, 1 - xl)):
        for n, k in enumerate(ORDER):
            p = x * 8 + lax.rem(z + k, 8)
            ref[n] = lp[pl.ds(pl.multiple_of(p * 64, 64), 64), :]


def copies_kernel(x_ref, y_ref, copies_ref, y_out):
    y_out[...] = y_ref[...]
    x = x_ref[...]
    for k in range(PEERS):
        copies_ref[k] = x


def parts_kernel(x_ref, y_ref, *outs):
    at = 0
    for out_ref in outs:
        n = out_ref.shape[0]
        out_ref[...] = x_ref[at : at + n] + y_ref[at : at + n]
        at += n


def add_kernel(x_ref, y_ref, out_ref):
    out_ref[...] = x_ref[...] + y_ref[...]


def sum_kernel(x_ref, out_ref):
    total = x_ref[0]
    for k in range(1, x_ref.shape[0]):
        total = total + x_ref[k]
    for k in range(out_ref.shape[0]):
        out_ref[k] = total


def total_kernel(x_ref, out_ref, bias_ref):
    total = x_ref[0]
    for k in range(1, x_ref.shape[0]):
        total = total + x_ref[k]
    total = total * (1.0 / 512)
    for k in range(out_ref.shape[0]):
        out_ref[k] = total[0:32]
    bias_ref[...] = total[32:40].sum(axis=0, keepdims=True)


def small(kernel, out_shape, name, *args):
    return pl.pallas_call(
        kernel,
        out_shape=out_shape,
        compiler_params=params(2),
        cost_estimate=cost(1 << 18, 3 << 20),
        name=name,
    )(*args)


def shapes(*entries):
    return [jax.ShapeDtypeStruct(s, t) for s, t in entries]


def cost(flops, moved):
    return pl.CostEstimate(flops=flops, bytes_accessed=moved, transcendentals=0)


BIG = 2 * 1024 * 1024 * 128


def exchange(x, axes):
    return lax.all_to_all(x, axes, split_axis=0, concat_axis=0, tiled=True)


def gather(x, axes, n):
    return exchange(jnp.broadcast_to(x, (n, *x.shape)), axes)


def other_core(x):
    return lax.ppermute(x, "core", [(0, 1), (1, 0)])


def across(x):
    return lax.ppermute(x, "xh", [(0, 1), (1, 0)])


def up(x, k):
    return lax.ppermute(x, "y", [(i, (i + k) % 4) for i in range(4)])


def along(x, k):
    return lax.ppermute(x, "z", [(i, (i + k) % 8) for i in range(8)])


def next_x(x):
    return lax.ppermute(x, "xl", [(0, 1), (1, 0)])


def in_hbm(x):
    return pltpu.with_memory_space_constraint(x, pltpu.HBM)


def after(event, *arrays):
    return lax.optimization_barrier((*arrays, event))[:-1]


VM = pl.BlockSpec(memory_space=pltpu.VMEM)
SM = pl.BlockSpec(memory_space=pltpu.SMEM)
HB = pl.BlockSpec(memory_space=pltpu.HBM)


def per_device(left, right, weight, bias, cotangent):
    at = where_index()
    cot = in_hbm(cotangent.reshape(T * T, CZ))
    weight = in_hbm(weight)
    left_own = left.transpose(1, 2, 0).reshape(64, S)
    right_own = right.transpose(1, 2, 0).reshape(64, S)
    left_copies, right_own = pl.pallas_call(
        copies_kernel,
        out_shape=[pltpu.VMEM((PEERS, 64, S), F32), pltpu.VMEM((64, S), F32)],
        compiler_params=params(2),
        name="copies",
    )(in_hbm(left_own), in_hbm(right_own))
    left_all = exchange(left_copies, COL)
    left_all = left_all.reshape(1024, S)
    pair_own = jnp.stack([right_own, across(right_own)])

    near = [pair_own] + [up(pair_own, k) for k in (1, 2, 3)]
    far = [other_core(x) for x in near]

    fhi, flo, l2, rt, keep, send = pl.pallas_call(
        outer_kernel,
        out_shape=[
            pltpu.HBM((1024, 1024), BF16),
            pltpu.HBM((1024, 1024), BF16),
            pltpu.HBM((1024, 256), BF16),
            pltpu.HBM((1024, S), F32),
            pltpu.VMEM((16, 40, CZ), F32),
            pltpu.VMEM((16, 40, CZ), F32),
        ],
        in_specs=[SM] + [VM] * 9 + [HB],
        out_specs=[HB] * 4 + [VM] * 2,
        scratch_shapes=[
            pltpu.VMEM((1024, 1024), BF16),
            pltpu.VMEM((1024, 1024), BF16),
            pltpu.VMEM((1024, 256), BF16),
            pltpu.VMEM((1024, S), F32),
            pltpu.VMEM((1024, 256), BF16),
            pltpu.VMEM((1024, 256), BF16),
            pltpu.VMEM((256, 1024), BF16),
            pltpu.VMEM((1024, CZ), F32),
            pltpu.VMEM((8, CZ), F32),
            pltpu.VMEM((1024, CZ), F32),
            pltpu.SemaphoreType.DMA((5,)),
        ],
        compiler_params=params(OUTER_MIB),
        cost_estimate=cost(6 * BIG, 8 << 20),
        name="outer_and_weight_grad",
    )(at, left_all, *near, *far, cot)

    chunks = small(add_kernel, pltpu.VMEM((16, 40, CZ), F32), "chip_sum", keep, other_core(send))
    chunks, l2 = lax.optimization_barrier((chunks, l2))
    lkeep, lsend, rkeep, rsend = pl.pallas_call(
        factor_kernel,
        out_shape=[pltpu.VMEM((8, 64, S), F32)] * 2 + [pltpu.VMEM((4, 2, 64, S), F32)] * 2,
        in_specs=[SM] + [HB] * 4,
        scratch_shapes=[
            pltpu.VMEM((1024, CZ), F32),
            pltpu.VMEM((1024, CZ), F32),
            pltpu.VMEM((1024, 256), BF16),
            pltpu.VMEM((1024, 128), BF16),
            pltpu.VMEM((1024, 256), BF16),
            pltpu.VMEM((1024, 1024), BF16),
            pltpu.VMEM((1024, 1024), BF16),
            pltpu.VMEM((1024, 256), BF16),
            pltpu.VMEM((1024, S), F32),
            pltpu.VMEM((256, 1024), BF16),
            pltpu.VMEM((1024, S), F32),
            pltpu.VMEM((1024, S), F32),
            pltpu.SemaphoreType.DMA((4,)),
        ],
        compiler_params=params(FACTOR_MIB),
        cost_estimate=cost(6 * BIG, 8 << 20),
        name="factor_grads",
    )(at, weight, cot, in_hbm(l2), in_hbm(rt))

    plane = exchange(chunks, PLANE)
    plane_sum = small(sum_kernel, pltpu.VMEM((8, 40, CZ), F32), "plane_sum", plane)
    lkeep, rkeep = after(plane_sum, lkeep, rkeep)
    (plane_sum,) = after(lsend, plane_sum)
    left_sum, sent = small(
        parts_kernel, [pltpu.VMEM((4, 64, S), F32)] * 2, "left_x", lkeep, next_x(lsend)
    )
    left_sum = left_sum + along(sent, 1)
    chip = rkeep + other_core(rsend)
    total, bias_grad = small(
        total_kernel,
        [pltpu.VMEM((16, 32, CZ), F32), jax.ShapeDtypeStruct((1, CZ), F32)],
        "total",
        exchange(plane_sum, ("z",)),
    )
    (fhi,) = after(sent, fhi)
    pair = pl.pallas_call(
        pair_kernel,
        out_shape=jax.ShapeDtypeStruct((1024, CZ), F32),
        in_specs=[HB] * 3 + [VM],
        scratch_shapes=[
            pltpu.VMEM((1024, 1024), BF16),
            pltpu.VMEM((1024, 1024), BF16),
            pltpu.VMEM((1024, CZ), F32),
            pltpu.VMEM((1024, 256), BF16),
            pltpu.SemaphoreType.DMA((5, 2)),
        ],
        compiler_params=params(PAIR_MIB),
        cost_estimate=cost(3 * BIG, 6 << 20),
        name="pair_out",
    )(in_hbm(fhi), in_hbm(flo), weight, bias.reshape(1, CZ))
    (ready,) = after(pair, total)
    half = exchange(ready, PLANE).reshape(512, CZ)
    half_other = other_core(half)
    core = lax.axis_index("core")
    first = jnp.where(core == 0, half, half_other)
    second = jnp.where(core == 0, half_other, half)
    weight_grad = jnp.concatenate([first, second])

    left_kept, right_kept = after(total, left_sum[:2], chip[0])
    line = right_kept + up(chip[1], 1) + up(chip[2], 2) + up(chip[3], 3)
    left_sum = left_kept + along(left_sum[2:], 2)
    last = left_sum
    left_sum = last[0] + along(last[1], 4)
    (line,) = after(last, line)
    right_sum = line[0] + across(line[1])
    left_grad = left_sum.reshape(2, C, S).transpose(2, 0, 1)
    right_grad = right_sum.reshape(2, C, S).transpose(2, 0, 1)
    return pair.reshape(T, T, CZ), left_grad, right_grad, weight_grad, bias_grad.reshape(CZ)


def solution(mesh):
    fine = Mesh(mesh.devices.reshape(2, 4, 2, 2, 8), ("xh", "y", "core", "xl", "z"))
    in_specs = (P(None, ROW + COL, None), P(None, COL + ROW, None), P(), P(), P(ROW, COL, None))
    out_specs = (P(ROW, COL, None), P(None, ROW + COL, None), P(None, COL + ROW, None), P(), P())
    return jax.shard_map(
        per_device, mesh=fine, in_specs=in_specs, out_specs=out_specs, check_vma=False
    )
```
